128 devices in a mesh: wide: 8 (over y, core), narrow: 16 (over z, x).
Axes of the slice: x: 4, y: 4, z: 4, core: 2. Of those that a mesh axis runs over, the one named last changes fastest.
Arguments:
- positions: float32 [3, 8, 16, 1, 128], P(None, 'wide', 'narrow'), may hold values from 0.08 to 0.92
- species: int32 [8, 16, 1, 128], P('wide', 'narrow'), may hold values 0 or 1
- neighbours: int32 [8, 16, 1, 128, 128], P('wide', 'narrow'), may hold values from 0 to 3455
- embed_one_w: float32 [2, 25], replicated, may hold values from -12 to 12
- embed_one_b: float32 [2, 25], replicated, may hold values from -6 to 6
- embed_two_w: float32 [25, 50], replicated, may hold values from -1.25 to 1.25
- embed_two_b: float32 [50], replicated, may hold values from -3 to 3
- embed_three_w: float32 [50, 100], replicated, may hold values from -0.875 to 0.875
- embed_three_b: float32 [100], replicated, may hold values from -3 to 3
- fit_one_w: float32 [1600, 240], replicated, may hold values from -0.15625 to 0.15625
- fit_one_b: float32 [240], replicated, may hold values from -6 to 6
- fit_two_w: float32 [240, 240], replicated, may hold values from -0.375 to 0.375
- fit_two_b: float32 [240], replicated, may hold values from -3 to 3
- fit_three_w: float32 [240, 240], replicated, may hold values from -0.375 to 0.375
- fit_three_b: float32 [240], replicated, may hold values from -3 to 3
- fit_out_w: float32 [240, 100], replicated, may hold values from -0.375 to 0.375
Outputs:
- dipole: float32 [3, 8, 16, 1, 128], P(None, 'wide', 'narrow')
- atom_field: float32 [4, 8, 16, 1, 128], P(None, 'wide', 'narrow')
- centroid_field: float32 [4, 8, 16, 1, 128], P(None, 'wide', 'narrow')
- energy: float32 [], replicated
The draws below stay inside these ranges and needn't reach their ends.
Inputs may be any that keep to these rules, and one draw needn't show every extreme that they name: `species`: 1 marks a hydrogen, 0 an oxygen. `neighbours`: entry c names slot c % 128 of the brick offset by (q // 9 - 1, q % 3 - 1, (q // 3) % 3 - 1) bricks along x, y, z from the atom's own, q = c // 128, periodically; an entry may name the atom itself.
All inputs are finite; a program needn't handle non-finite values. No bound on the sum of `species` on one device may be relied on, other than what follows from the above.
Results may differ from the reference program's by a relative error of at most 0.0003.
Values sent between devices are 32-bit elements; how exact they have to be, the bound alone decides.
A program may use at most 64 MiB of HBM per device.

```python
import math
import jax
import jax.numpy as jnp
from jax import lax

GRID_X = 256
GRID_Y = 256
GRID_Z = 256
BRICKS_Y = 1
BRICK_ATOMS = 128
NEIGHBOURS = 128
EMBED_ONE = 25
EMBED_TWO = 50
EMBED_THREE = 100
AXIS_COLUMNS = 16
FITTING = 240
N_WIDE = 8
N_NARROW = 16


def touch_ends(values, own_key, smallest, largest):
    longest = values.shape.index(max(values.shape))
    spots = []
    for shift in (0, 1):
        where = [jax.random.randint(jax.random.fold_in(own_key, axis), (), 0, length) for axis, length in enumerate(values.shape)]
        where[longest] = (where[longest] + shift) % values.shape[longest]
        spots.append(tuple(where))
    return values.at[spots[0]].set(smallest).at[spots[1]].set(largest)


def block_scale(stream_key, shape, pieces, low, high):
    def one(axis_at, shards_of):
        heights = jax.random.uniform(jax.random.fold_in(jax.random.fold_in(stream_key, 6), axis_at), (shards_of,), jnp.float32, low / len(pieces), high / len(pieces))
        return jnp.repeat(jnp.exp(heights), shape[axis_at] // shards_of).reshape((-1,) + (1,) * (len(shape) - axis_at - 1))

    level = one(*pieces[0])
    for cut in pieces[1:]:
        level = level * one(*cut)
    return level


def centred(rng, dims, scale, bound, held_as=jnp.bfloat16):
    return jnp.clip(scale * jax.random.normal(rng, dims, jnp.float32), -bound, bound).astype(held_as)


def setup_inputs(seed: int = 0) -> dict:
    arg_keys = jax.random.split(jax.random.key(seed), 17)
    positions = jnp.clip(0.08 + 0.84000002 * jax.random.uniform(arg_keys[0], (3, N_WIDE, N_NARROW, BRICKS_Y, BRICK_ATOMS), jnp.float32) ** block_scale(arg_keys[0], (3, N_WIDE, N_NARROW, BRICKS_Y, BRICK_ATOMS), ((1, 8), (2, 16)), -0.2, 0.2), 0.08, 0.92)
    species = touch_ends((jax.random.randint(arg_keys[1], (N_WIDE, N_NARROW, BRICKS_Y, BRICK_ATOMS), 0, 3) < 2).astype(jnp.int32), jax.random.fold_in(arg_keys[1], 1), 0, 1)
    neighbours = touch_ends(jax.random.randint(arg_keys[2], (N_WIDE, N_NARROW, BRICKS_Y, BRICK_ATOMS, NEIGHBOURS), 0, 27 * BRICK_ATOMS), jax.random.fold_in(arg_keys[2], 1), 0, (27 * BRICK_ATOMS) - 1).astype(jnp.int32)
    embed_one_w = centred(arg_keys[3], (2, EMBED_ONE), 2.0, 12.0, jnp.float32)
    embed_one_b = centred(arg_keys[4], (2, EMBED_ONE), 1.0, 6.0, jnp.float32)
    embed_two_w = centred(arg_keys[5], (EMBED_ONE, EMBED_TWO), EMBED_ONE ** -0.5, 1.25, jnp.float32)
    embed_two_b = centred(arg_keys[6], (EMBED_TWO,), 0.5, 3.0, jnp.float32)
    embed_three_w = centred(arg_keys[7], (EMBED_TWO, EMBED_THREE), EMBED_TWO ** -0.5, 0.875, jnp.float32)
    embed_three_b = centred(arg_keys[8], (EMBED_THREE,), 0.5, 3.0, jnp.float32)
    fit_one_w = centred(arg_keys[9], (AXIS_COLUMNS * EMBED_THREE, FITTING), (AXIS_COLUMNS * EMBED_THREE) ** -0.5, 0.15625, jnp.float32)
    fit_one_b = centred(arg_keys[10], (FITTING,), 1.0, 6.0, jnp.float32)
    fit_two_w = centred(arg_keys[11], (FITTING, FITTING), FITTING ** -0.5, 0.375, jnp.float32)
    fit_two_b = centred(arg_keys[12], (FITTING,), 0.5, 3.0, jnp.float32)
    fit_three_w = centred(arg_keys[13], (FITTING, FITTING), FITTING ** -0.5, 0.375, jnp.float32)
    fit_three_b = centred(arg_keys[14], (FITTING,), 0.5, 3.0, jnp.float32)
    fit_out_w = centred(arg_keys[15], (FITTING, EMBED_THREE), FITTING ** -0.5, 0.375, jnp.float32)
    return {"positions": positions, "species": species, "neighbours": neighbours, "embed_one_w": embed_one_w, "embed_one_b": embed_one_b, "embed_two_w": embed_two_w, "embed_two_b": embed_two_b, "embed_three_w": embed_three_w, "embed_three_b": embed_three_b, "fit_one_w": fit_one_w, "fit_one_b": fit_one_b, "fit_two_w": fit_two_w, "fit_two_b": fit_two_b, "fit_three_w": fit_three_w, "fit_three_b": fit_three_b, "fit_out_w": fit_out_w}


radius_scale = 24.0
wannier_reach = 0.5
ewald_beta = 0.9
coulomb = 0.25
atom_block = 64
largest_value = lax.Precision.HIGHEST


def spline(offset):
    square = offset * offset
    offset_cube = square * offset
    remain = 4.0 - offset
    piece_one = offset_cube / 6.0
    piece_two = (-3.0 * offset_cube + 12.0 * square - 12.0 * offset + 4.0) / 6.0
    piece_three = (3.0 * offset_cube - 24.0 * square + 60.0 * offset - 44.0) / 6.0
    piece_four = remain * remain * remain / 6.0
    result_value = jnp.where(offset < 1.0, piece_one, jnp.where(offset < 2.0, piece_two, jnp.where(offset < 3.0, piece_three, piece_four)))
    inside = (offset >= 0.0) & (offset < 4.0)
    return jnp.where(inside, result_value, jnp.zeros_like(offset))


def slope(offset):
    square = offset * offset
    remain = 4.0 - offset
    piece_one = square / 2.0
    piece_two = (-9.0 * square + 24.0 * offset - 12.0) / 6.0
    piece_three = (9.0 * square - 48.0 * offset + 60.0) / 6.0
    piece_four = -remain * remain / 2.0
    result_value = jnp.where(offset < 1.0, piece_one, jnp.where(offset < 2.0, piece_two, jnp.where(offset < 3.0, piece_three, piece_four)))
    inside = (offset >= 0.0) & (offset < 4.0)
    return jnp.where(inside, result_value, jnp.zeros_like(offset))


def environment(relative, hydrogen, one_w, one_b, second_weight, second_bias, third_weight, third_bias):
    scaled = relative / radius_scale
    square = jnp.sum(scaled * scaled, axis=0)
    smooth = 1.0 / (1.0 + square)
    radial = jnp.concatenate([smooth[None], smooth[None] * scaled], axis=0)
    is_hydrogen = hydrogen[None] > 0.5
    weight = jnp.where(is_hydrogen, one_w[1][:, None, None], one_w[0][:, None, None])
    offset_b = jnp.where(is_hydrogen, one_b[1][:, None, None], one_b[0][:, None, None])
    first_layer = jnp.tanh(weight * smooth[None] + offset_b)
    second_layer = jnp.tanh(jnp.einsum('tky,ti->iky', first_layer, second_weight, precision=largest_value) + second_bias[:, None, None]) + jnp.concatenate([first_layer, first_layer], axis=0)
    third_layer = jnp.tanh(jnp.einsum('tky,ti->iky', second_layer, third_weight, precision=largest_value) + third_bias[:, None, None]) + jnp.concatenate([second_layer, second_layer], axis=0)
    return jnp.einsum('pbn,dbn->pdb', radial, third_layer, precision=largest_value) / relative.shape[2]


def fitting(matrix, one_w, one_b, second_weight, second_bias, third_weight, third_bias, out_w):
    descriptor = jnp.einsum('pda,pea->dea', matrix, matrix[:, :AXIS_COLUMNS], precision=largest_value)
    descriptor = descriptor.reshape(-1, matrix.shape[2])
    hidden = jnp.tanh(jnp.einsum('fh,fa->ha', one_w, descriptor, precision=largest_value) + one_b[:, None])
    hidden = hidden + jnp.tanh(jnp.einsum('gh,ga->ha', second_weight, hidden, precision=largest_value) + second_bias[:, None])
    hidden = hidden + jnp.tanh(jnp.einsum('gh,ga->ha', third_weight, hidden, precision=largest_value) + third_bias[:, None])
    coeffs = jnp.einsum('hk,ha->ka', out_w, hidden, precision=largest_value)
    return jnp.einsum('ka,cka->ca', coeffs, matrix[1:], precision=largest_value)


def folded(mode_index, length):
    wrapped = mode_index % length
    return jnp.where(2 * wrapped >= length, wrapped - length, wrapped)


def modulus(mode_index, length):
    phase_angle = (mode_index % length).astype(jnp.float32) * (2.0 * math.pi / length)
    divisor = (4.0 + 2.0 * jnp.cos(phase_angle)) / 6.0
    return 1.0 / (divisor * divisor)


def influence(index_x, index_y, index_z):
    fold_x = folded(index_x, GRID_X)
    fold_y = folded(index_y, GRID_Y)
    fold_z = folded(index_z, GRID_Z)
    freq_x = fold_x.astype(jnp.float32) / GRID_X
    freq_y = fold_y.astype(jnp.float32) / GRID_Y
    freq_z = fold_z.astype(jnp.float32) / GRID_Z
    square = freq_x * freq_x + freq_y * freq_y + freq_z * freq_z
    is_zero = (fold_x == 0) & (fold_y == 0) & (fold_z == 0)
    safe_square = jnp.where(is_zero, 1.0, square)
    result_value = jnp.exp(-(math.pi * math.pi) * square / (ewald_beta * ewald_beta)) / safe_square
    result_value = result_value * modulus(index_x, GRID_X) * modulus(index_y, GRID_Y) * modulus(index_z, GRID_Z)
    return jnp.where(is_zero, 0.0, result_value) * (coulomb / (math.pi * GRID_X * GRID_Y * GRID_Z))


def stencil(local, anchor, length):
    lower_cell = jnp.floor(local)
    counter = jnp.arange(4, dtype=jnp.int32)
    offsets = (local - lower_cell)[:, None] + counter.astype(local.dtype)[None, :]
    cell_index = (anchor[:, None] + lower_cell.astype(jnp.int32)[:, None] - counter[None, :]) % length
    return cell_index, spline(offsets), slope(offsets)


def reference(positions, species, neighbours, embed_one_w, embed_one_b, embed_two_w, embed_two_b, embed_three_w, embed_three_b, fit_one_w, fit_one_b, fit_two_w, fit_two_b, fit_three_w, fit_three_b, fit_out_w):
    cells_x = GRID_X // N_WIDE
    cells_z = GRID_Z // N_NARROW
    brick_y = GRID_Y // BRICKS_Y
    device_atoms = BRICKS_Y * BRICK_ATOMS
    atom_total = N_WIDE * N_NARROW * device_atoms
    pair_shape = (N_WIDE, N_NARROW, BRICKS_Y, BRICK_ATOMS, NEIGHBOURS)
    wide_at = lax.broadcasted_iota(jnp.int32, pair_shape, 0)
    narrow_at = lax.broadcasted_iota(jnp.int32, pair_shape, 1)
    brick_at = lax.broadcasted_iota(jnp.int32, pair_shape, 2)
    slot_index = neighbours % BRICK_ATOMS
    offset = neighbours // BRICK_ATOMS
    step_x = offset // 9
    step_z = (offset // 3) % 3
    step_y = offset % 3
    source = (((wide_at + step_x - 1) % N_WIDE * N_NARROW + (narrow_at + step_z - 1) % N_NARROW) * BRICKS_Y + (brick_at + step_y - 1) % BRICKS_Y) * BRICK_ATOMS + slot_index
    source = source.reshape(atom_total, NEIGHBOURS)
    flat_positions = positions.reshape(3, atom_total)
    hydrogen = species.reshape(atom_total).astype(jnp.float32)
    nearby = jnp.take(flat_positions, source, axis=1)
    near_kind = jnp.take(hydrogen, source)
    extent = jnp.array([cells_x, brick_y, cells_z], jnp.float32)[:, None, None]
    steps_all = (jnp.stack([step_x, step_y, step_z]) - 1).reshape(3, atom_total, NEIGHBOURS)
    relative = steps_all.astype(jnp.float32) * extent + (nearby - flat_positions[:, :, None]) * extent

    block_size = min(atom_block, device_atoms)
    block_count = atom_total // block_size
    rel_blocks = relative.reshape(3, block_count, block_size, NEIGHBOURS).transpose(1, 0, 2, 3)
    kind_blocks = near_kind.reshape(block_count, block_size, NEIGHBOURS)

    def one_block(operands):
        matrix = environment(operands[0], operands[1], embed_one_w, embed_one_b, embed_two_w, embed_two_b, embed_three_w, embed_three_b)
        return fitting(matrix, fit_one_w, fit_one_b, fit_two_w, fit_two_b, fit_three_w, fit_three_b, fit_out_w)

    dipole = lax.map(one_block, (rel_blocks, kind_blocks))
    dipole = dipole.transpose(1, 0, 2).reshape(3, atom_total)
    oxygen = 1.0 - hydrogen

    atom_shape = (N_WIDE, N_NARROW, BRICKS_Y, BRICK_ATOMS)
    wide_index = lax.broadcasted_iota(jnp.int32, atom_shape, 0).reshape(atom_total)
    narrow_index = lax.broadcasted_iota(jnp.int32, atom_shape, 1).reshape(atom_total)
    home_y = lax.broadcasted_iota(jnp.int32, atom_shape, 2).reshape(atom_total).astype(jnp.float32)
    atom_x = flat_positions[0] * cells_x
    atom_y = home_y * brick_y + flat_positions[1] * brick_y
    atom_z = flat_positions[2] * cells_z
    displace = wannier_reach * jnp.tanh(dipole)
    site_x = jnp.concatenate([atom_x, atom_x + displace[0]])
    site_y = jnp.concatenate([atom_y, atom_y + displace[1]])
    site_z = jnp.concatenate([atom_z, atom_z + displace[2]])
    charge = jnp.concatenate([6.0 * oxygen + hydrogen, -8.0 * oxygen])
    anchor_x = jnp.concatenate([wide_index, wide_index]) * cells_x
    anchor_z = jnp.concatenate([narrow_index, narrow_index]) * cells_z
    anchor_y = jnp.zeros_like(anchor_x)
    cell_x, weight_x, slope_x = stencil(site_x, anchor_x, GRID_X)
    cell_y, weight_y, slope_y = stencil(site_y, anchor_y, GRID_Y)
    cell_z, weight_z, slope_z = stencil(site_z, anchor_z, GRID_Z)
    place_x = cell_x[:, :, None, None]
    place_y = cell_y[:, None, :, None]
    place_z = cell_z[:, None, None, :]
    spread_values = charge[:, None, None, None] * weight_x[:, :, None, None] * weight_y[:, None, :, None] * weight_z[:, None, None, :]
    charge_grid = jnp.zeros((GRID_X, GRID_Y, GRID_Z), jnp.float32).at[place_x, place_y, place_z].add(spread_values)

    spectrum = jnp.fft.fftn(charge_grid)
    index_x = jnp.arange(GRID_X, dtype=jnp.int32)[:, None, None]
    index_y = jnp.arange(GRID_Y, dtype=jnp.int32)[None, :, None]
    index_z = jnp.arange(GRID_Z, dtype=jnp.int32)[None, None, :]
    green_table = influence(index_x, index_y, index_z)
    real_part = jnp.real(spectrum)
    imag_part = jnp.imag(spectrum)
    energy = 0.5 * jnp.sum(green_table * (real_part * real_part + imag_part * imag_part)) / atom_total
    potential_grid = jnp.real(jnp.fft.ifftn(green_table * spectrum)) * (GRID_X * GRID_Y * GRID_Z)

    local_values = potential_grid[place_x, place_y, place_z]
    potential = jnp.sum(local_values * weight_x[:, :, None, None] * weight_y[:, None, :, None] * weight_z[:, None, None, :], axis=(1, 2, 3))
    field_x = -jnp.sum(local_values * slope_x[:, :, None, None] * weight_y[:, None, :, None] * weight_z[:, None, None, :], axis=(1, 2, 3))
    field_y = -jnp.sum(local_values * weight_x[:, :, None, None] * slope_y[:, None, :, None] * weight_z[:, None, None, :], axis=(1, 2, 3))
    field_z = -jnp.sum(local_values * weight_x[:, :, None, None] * weight_y[:, None, :, None] * slope_z[:, None, None, :], axis=(1, 2, 3))
    fields = jnp.stack([potential, field_x, field_y, field_z])
    atom_field = fields[:, :atom_total].reshape(4, N_WIDE, N_NARROW, BRICKS_Y, BRICK_ATOMS)
    centroid_field = (fields[:, atom_total:] * oxygen[None]).reshape(4, N_WIDE, N_NARROW, BRICKS_Y, BRICK_ATOMS)
    dipole_out = (dipole * oxygen[None]).reshape(3, N_WIDE, N_NARROW, BRICKS_Y, BRICK_ATOMS)
    return (dipole_out, atom_field, centroid_field, energy)
```

```python
import functools
import math

import jax
import jax.numpy as jnp
import numpy as np
from jax import lax
from jax.experimental import pallas as pl
from jax.experimental.pallas import tpu as pltpu
from jax.sharding import PartitionSpec as P

NW, NN = 8, 16
ND = NW * NN
CX, CY, CZ = 32, 256, 16
TX, TZ = 40, 19
TILE = 768
FOLD = 640
MODES = 512
ATOMS = 128
F32 = jnp.float32
BF16 = jnp.bfloat16
MESH = pl.DeviceIdType.MESH
HIGHEST = lax.Precision.HIGHEST
NT = (((1,), (1,)), ((), ()))
NNN = (((1,), (0,)), ((), ()))


def split(x):
    high = x.astype(BF16)
    return high, (x - high.astype(F32)).astype(BF16)


def mm(a, b, dims=NNN):
    return lax.dot_general(a, b, dims, preferred_element_type=F32)


def mm3(a, b, dims=NNN):
    return mm(a[0], b[0], dims) + mm(a[0], b[1], dims) + mm(a[1], b[0], dims)


def exact(a, b, dims=NNN):
    return lax.dot_general(a, b, dims, precision=HIGHEST, preferred_element_type=F32)


def iota(shape, dim):
    return lax.broadcasted_iota(jnp.int32, shape, dim)


def spline(offset):
    square = offset * offset
    cube = square * offset
    remain = 4.0 - offset
    one = cube * (1.0 / 6.0)
    two = (-3.0 * cube + 12.0 * square - 12.0 * offset + 4.0) * (1.0 / 6.0)
    three = (3.0 * cube - 24.0 * square + 60.0 * offset - 44.0) * (1.0 / 6.0)
    four = remain * remain * remain * (1.0 / 6.0)
    value = jnp.where(
        offset < 1.0, one, jnp.where(offset < 2.0, two, jnp.where(offset < 3.0, three, four))
    )
    return jnp.where((offset >= 0.0) & (offset < 4.0), value, 0.0)


def slope(offset):
    square = offset * offset
    remain = 4.0 - offset
    one = square * 0.5
    two = (-9.0 * square + 24.0 * offset - 12.0) * (1.0 / 6.0)
    three = (9.0 * square - 48.0 * offset + 60.0) * (1.0 / 6.0)
    four = -0.5 * remain * remain
    value = jnp.where(
        offset < 1.0, one, jnp.where(offset < 2.0, two, jnp.where(offset < 3.0, three, four))
    )
    return jnp.where((offset >= 0.0) & (offset < 4.0), value, 0.0)


def halo_kernel(own_ref, ghost_ref, send_sem, recv_sem):
    wide = lax.axis_index("wide")
    narrow = lax.axis_index("narrow")
    steps = [(sx, sz) for sx in range(3) for sz in range(3) if (sx, sz) != (1, 1)]
    barrier = pltpu.get_barrier_semaphore()

    def device(sx, sz):
        return (lax.rem(wide + (NW + 1 - sx), NW), lax.rem(narrow + (NN + 1 - sz), NN))

    for sx, sz in steps:
        pl.semaphore_signal(barrier, inc=1, device_id=device(sx, sz), device_id_type=MESH)
    pl.semaphore_wait(barrier, len(steps))
    copies = []
    for at, (sx, sz) in enumerate(steps):
        copy = pltpu.make_async_remote_copy(
            src_ref=own_ref,
            dst_ref=ghost_ref.at[sx * 3 + sz],
            send_sem=send_sem.at[at],
            recv_sem=recv_sem.at[at],
            device_id=device(sx, sz),
            device_id_type=MESH,
        )
        copy.start()
        copies.append(copy)
    ghost_ref[4] = own_ref[...]
    for copy in copies:
        copy.wait()


def halo(own):
    return pl.pallas_call(
        halo_kernel,
        out_shape=jax.ShapeDtypeStruct((9, 8, ATOMS), F32),
        in_specs=[pl.BlockSpec(memory_space=pltpu.VMEM)],
        out_specs=pl.BlockSpec(memory_space=pltpu.VMEM),
        scratch_shapes=[pltpu.SemaphoreType.DMA((8,)), pltpu.SemaphoreType.DMA((8,))],
        compiler_params=pltpu.CompilerParams(collective_id=0, has_side_effects=True),
        name="halo",
    )(own)


def spread_rows(rows, count):
    r = iota((rows, count), 0)
    c = iota((rows, count), 1)
    i = r & 31
    return jnp.where((i < 25) & (c == (r >> 5) * 25 + i), 1.0, 0.0).astype(F32)


def net_kernel(
    ghost_ref,
    near_ref,
    e1w_ref,
    e1b_ref,
    e2w_ref,
    e2b_ref,
    e3w_ref,
    e3b_ref,
    f1w_ref,
    f1b_ref,
    f2w_ref,
    f2b_ref,
    f3w_ref,
    f3b_ref,
    fow_ref,
    dip_ref,
    table_ref,
    own_ref,
    mat_ref,
    left_ref,
    right_ref,
):
    extent = (float(CX), float(CY), float(CZ))
    for k in range(9):
        shift = (float(k // 3 - 1), 0.0, float(k % 3 - 1))
        for c in range(3):
            table_ref[k * 4 + c] = jnp.broadcast_to(ghost_ref[k, c : c + 1, :] + shift[c], (8, ATOMS))
        table_ref[k * 4 + 3] = jnp.broadcast_to(ghost_ref[k, 3:4, :], (8, ATOMS))
    for c in range(3):
        own_ref[c] = jnp.broadcast_to(ghost_ref[4, c : c + 1, :], (ATOMS, ATOMS)).T

    pick1 = spread_rows(32, 25)
    pick2 = spread_rows(64, 50)
    pick3 = spread_rows(128, 100)

    def column(pick, row):
        return exact(pick, jnp.broadcast_to(row, (ATOMS, row.shape[1])), NT)

    w_oxygen = column(pick1, e1w_ref[0:1, :])
    w_hydrogen = column(pick1, e1w_ref[1:2, :])
    b_oxygen = column(pick1, e1b_ref[0:1, :])
    b_hydrogen = column(pick1, e1b_ref[1:2, :])
    bias2 = column(pick2, e2b_ref[...])
    bias3 = column(pick3, e3b_ref[...])
    w2 = exact(pick2, exact(pick1, e2w_ref[...]), NT)
    w3 = exact(pick3, exact(pick2, e3w_ref[...]), NT)
    w2_high, w2_low = split(w2)
    w3_high, w3_low = split(w3)
    w2_all = jnp.concatenate([w2_high, w2_high, w2_low], axis=1)
    w3_all = jnp.concatenate([w3_high, w3_high, w3_low], axis=1)
    bias2 = jnp.concatenate([bias2] * 8, axis=1)
    bias3 = jnp.concatenate([bias3] * 8, axis=1)
    sublane = iota((8, ATOMS), 0)

    def group(g, carry):
        rows = pl.ds(pl.multiple_of(g * 8, 8), 8)
        code = near_ref[rows, :]
        slot = code & 127
        offset = code >> 7
        brick = (offset * 11) >> 5
        step_y = (offset - 3 * brick - 1).astype(F32)
        parts = [jnp.zeros((8, ATOMS), F32)] * 4
        for k in range(9):
            here = brick == k
            for c in range(4):
                found = jnp.take_along_axis(table_ref[k * 4 + c], slot, axis=1)
                parts[c] = jnp.where(here, found, parts[c])
        parts[1] = parts[1] + step_y
        scaled = [(parts[c] - own_ref[c, rows, :]) * (extent[c] / 24.0) for c in range(3)]
        square = scaled[0] * scaled[0] + scaled[1] * scaled[1] + scaled[2] * scaled[2]
        smooth = 1.0 / (1.0 + square)
        kind = parts[3]
        pieces = []
        for b in range(8):
            s = jnp.broadcast_to(smooth[b : b + 1, :], (32, ATOMS))
            h = jnp.broadcast_to(kind[b : b + 1, :], (32, ATOMS)) > 0.5
            pieces.append(
                jnp.where(h, w_hydrogen, w_oxygen) * s + jnp.where(h, b_hydrogen, b_oxygen)
            )
        one = jnp.tanh(jnp.concatenate(pieces, axis=1))
        high, low = split(one)
        two = jnp.tanh(mm(w2_all, jnp.concatenate([high, low, high], axis=0)) + bias2)
        two = two + jnp.concatenate([one, one], axis=0)
        high, low = split(two)
        three = jnp.tanh(mm(w3_all, jnp.concatenate([high, low, high], axis=0)) + bias3)
        three = three + jnp.concatenate([two, two], axis=0)
        high, low = split(three)
        scale = smooth * (1.0 / 128.0)
        radial = [scale] + [scale * scaled[c] for c in range(3)]
        blocks = []
        for b in range(8):
            mine = sublane == b
            blocks.append(jnp.concatenate([jnp.where(mine, r, 0.0) for r in radial], axis=0))
        radial = jnp.concatenate(blocks, axis=1)
        r_high, r_low = split(radial)
        found = mm(r_high, high, NT) + mm(r_high, low, NT) + mm(r_low, high, NT)
        for p in range(4):
            mat_ref[p, rows, :] = found[p * 8 : (p + 1) * 8]
        return carry

    lax.fori_loop(0, ATOMS // 8, group, 0)

    matrix = [exact(mat_ref[p], pick3) for p in range(4)]
    left_ref[...] = f1w_ref[:, :128]
    right_ref[...] = jnp.concatenate([f1w_ref[:, 128:], jnp.zeros((1600, 16), F32)], axis=1)
    hidden = jnp.zeros((ATOMS, 256), F32)
    for e in range(16):
        entry = matrix[0] * matrix[0][:, e : e + 1]
        for p in range(1, 4):
            entry = entry + matrix[p] * matrix[p][:, e : e + 1]
        weight = jnp.concatenate(
            [left_ref[pl.ds(e, 100, stride=16), :], right_ref[pl.ds(e, 100, stride=16), :]], axis=1
        )
        hidden = hidden + mm3(split(entry), split(weight))
    hidden = hidden[:, :240]
    hidden = jnp.tanh(hidden + f1b_ref[...])
    hidden = hidden + jnp.tanh(mm3(split(hidden), split(f2w_ref[...])) + f2b_ref[...])
    hidden = hidden + jnp.tanh(mm3(split(hidden), split(f3w_ref[...])) + f3b_ref[...])
    coeffs = mm3(split(hidden), split(fow_ref[...]))
    lane = iota((ATOMS, ATOMS), 1)
    result = jnp.zeros((ATOMS, ATOMS), F32)
    for c in range(3):
        total = jnp.sum(coeffs * matrix[1 + c], axis=1, keepdims=True)
        result = jnp.where(lane == c, total, result)
    dip_ref[...] = result.T[:8]


def net(ghosts, neighbours, weights):
    vmem = pl.BlockSpec(memory_space=pltpu.VMEM)
    return pl.pallas_call(
        net_kernel,
        out_shape=jax.ShapeDtypeStruct((8, ATOMS), F32),
        in_specs=[vmem] * (2 + len(weights)),
        out_specs=vmem,
        scratch_shapes=[
            pltpu.VMEM((36, 8, ATOMS), F32),
            pltpu.VMEM((3, ATOMS, ATOMS), F32),
            pltpu.VMEM((4, ATOMS, ATOMS), F32),
            pltpu.VMEM((1600, ATOMS), F32),
            pltpu.VMEM((1600, ATOMS), F32),
        ],
        compiler_params=pltpu.CompilerParams(vmem_limit_bytes=32 << 20),
        name="net",
    )(ghosts, neighbours, *weights)


def np_split(x):
    x = np.asarray(x, np.float32)
    high = x.astype(jnp.bfloat16)
    low = (x - high.astype(np.float32)).astype(jnp.bfloat16)
    return np.stack([high, low])


@functools.lru_cache(None)
def tables():
    m = np.arange(128)[:, None]
    y = np.arange(CY)[None, :]
    angle = 2 * np.pi * (m * y % CY) / CY
    lower = -np.sin(angle)
    lower[0] = 1 - 2 * (y[0] % 2)
    dft_y = np_split(np.concatenate([np.cos(angle), lower]))
    j, k = np.divmod(np.arange(ND), NN)
    phi = 2 * np.pi * ((2 * j[:, None] * j[None] + k[:, None] * k[None]) % 16) / 16
    cos, sin = np.cos(phi), np.sin(phi)
    dft_b = np_split(np.block([[cos, sin], [-sin, cos]]))
    z, x = np.divmod(np.arange(TILE), TX)
    turn = 2 * np.pi * ((j[:, None] * (x - 3)[None] + k[:, None] * (z - 3)[None]) % 256) / 256
    twiddle = np.stack([np.cos(turn), np.sin(turn)]).astype(np.float32)
    v, u = np.divmod(np.arange(MODES), 32)
    ax = 2 * np.pi * ((np.arange(TX)[:, None] - 3) * u[None] % 32) / 32
    az = 2 * np.pi * ((np.arange(16)[:, None] - 3) * v[None] % 16) / 16
    fac_x = np.stack([np.cos(ax), np.sin(ax)]).astype(np.float32)
    fac_z = np.stack([np.cos(az), np.sin(az)]).astype(np.float32)

    def fold(i, n):
        return np.where(2 * i >= n, i - n, i) / n

    def modulus(i, n):
        return 36.0 / (4 + 2 * np.cos(2 * np.pi * i / n)) ** 2

    def decay(f):
        return np.exp(-np.pi**2 * f * f / 0.81)

    mx = j[:, None] + 8 * u[None]
    mz = k[:, None] + 16 * v[None]
    fx, fz = fold(mx, 256), fold(mz, 256)
    scale = 0.25 / (np.pi * 256.0**3)
    plane = scale * decay(fx) * decay(fz) * modulus(mx, 256) * modulus(mz, 256)
    green = np.stack([plane, fx * fx + fz * fz]).astype(np.float32)
    my = np.arange(129)
    fy = fold(my, 256)
    column = np.stack([decay(fy) * modulus(my, 256), fy * fy]).astype(np.float32)
    return dft_y, dft_b, twiddle, fac_x, fac_z, green, column


def long_kernel(
    own_ref,
    dip_ref,
    dft_y_ref,
    dft_b_ref,
    twiddle_ref,
    fac_x_ref,
    fac_z_ref,
    green_ref,
    column_ref,
    dipole_ref,
    atom_ref,
    centroid_ref,
    energy_ref,
    mix_ref,
    wave_ref,
    tab_ref,
    out_one,
    in_one,
    out_two,
    in_two,
    send_sem,
    recv_sem,
):
    wide = lax.axis_index("wide")
    narrow = lax.axis_index("narrow")
    me = wide * NN + narrow
    barrier = pltpu.get_barrier_semaphore()

    def peer(d):
        at = lax.rem(me + d, ND)
        return at, (at // NN, lax.rem(at, NN))

    def greet(d, carry):
        pl.semaphore_signal(barrier, inc=1, device_id=peer(d)[1], device_id_type=MESH)
        return carry

    lax.fori_loop(1, ND, greet, 0)

    kind = own_ref[3:4, :]
    oxygen = 1.0 - kind
    dip = dip_ref[...]
    dipole_ref[...] = dip * oxygen
    shift = 0.5 * jnp.tanh(dip)

    def sites(c, extent):
        atom = own_ref[c : c + 1, :] * float(extent)
        return jnp.concatenate([atom, atom + shift[c : c + 1, :]], axis=1)

    charge = jnp.concatenate([6.0 * oxygen + kind, -8.0 * oxygen], axis=1)
    off_x = sites(0, CX) - (iota((TX, 256), 0).astype(F32) - 3.0)
    off_z = sites(2, CZ) - (iota((24, 256), 0).astype(F32) - 3.0)
    off_y = sites(1, CY) - iota((CY, 256), 0).astype(F32)
    off_y = jnp.where(off_y < 0.0, off_y + float(CY), off_y)
    wx, sx = spline(off_x), slope(off_x)
    wz, sz = spline(off_z), slope(off_z)
    wave = mm3(
        (dft_y_ref[0], dft_y_ref[1]),
        split(jnp.concatenate([spline(off_y), slope(off_y)], axis=1)),
    )
    wave_ref[...] = wave
    rest = jnp.zeros((TILE - TX * TZ, 256), F32)
    for at, (left, right) in enumerate(((wz, wx), (wz, sx), (sz, wx))):
        full = jnp.concatenate([left[z : z + 1, :] * right for z in range(TZ)] + [rest], axis=0)
        high, low = split(full)
        mix_ref[0, :, at * 256 : (at + 1) * 256] = high
        mix_ref[1, :, at * 256 : (at + 1) * 256] = low
    spread = mm3(
        split(wave[:, :256] * charge), (mix_ref[0, :, :256], mix_ref[1, :, :256]), NT
    )
    for part in range(2):
        for t in range(6):
            out_one[:, part * 6 + t, :] = spread[part * 128 : (part + 1) * 128, t * 128 : (t + 1) * 128]

    pl.semaphore_wait(barrier, ND - 1)

    def exchange(out_ref, in_ref, s):
        def one(d, carry):
            at, device = peer(d)
            pltpu.make_async_remote_copy(
                src_ref=out_ref.at[at],
                dst_ref=in_ref.at[me],
                send_sem=send_sem.at[s],
                recv_sem=recv_sem.at[s],
                device_id=device,
                device_id_type=MESH,
            ).start()
            return carry

        lax.fori_loop(1, ND, one, 0)
        in_ref[me] = out_ref[me]

    def settle(out_ref, in_ref, s):
        whole = pltpu.make_async_remote_copy(
            src_ref=out_ref.at[pl.ds(0, ND - 1)],
            dst_ref=in_ref.at[pl.ds(0, ND - 1)],
            send_sem=send_sem.at[s],
            recv_sem=recv_sem.at[s],
            device_id=peer(1)[1],
            device_id_type=MESH,
        )
        whole.wait_send()
        whole.wait_recv()

    exchange(out_one, in_one, 0)

    def build(z, carry):
        cz = fac_z_ref[0, pl.ds(z, 1), :]
        zz = fac_z_ref[1, pl.ds(z, 1), :]
        cx, xx = fac_x_ref[0], fac_x_ref[1]
        rows = pl.ds(pl.multiple_of(z * TX, 8), TX)
        tab_ref[0, rows, :] = cx * cz - xx * zz
        tab_ref[1, rows, :] = xx * cz + cx * zz
        return carry

    lax.fori_loop(0, 16, build, 0)
    cos_e = split(tab_ref[0])
    sin_e = split(tab_ref[1])

    settle(out_one, in_one, 0)

    def gathered(in_ref):
        return jnp.concatenate(
            [
                jnp.concatenate([in_ref[:, part * 6 + t, :] for t in range(6)], axis=1)
                for part in range(2)
            ],
            axis=0,
        )

    tiles = gathered(in_one)
    bricks = mm3((dft_b_ref[0], dft_b_ref[1]), split(tiles))
    real, imag = bricks[:128], bricks[128:]
    cos_t, sin_t = twiddle_ref[0], twiddle_ref[1]
    turned = jnp.concatenate(
        [real * cos_t + imag * sin_t, imag * cos_t - real * sin_t], axis=0
    )
    turned = jnp.concatenate(
        [turned[:, :128] + turned[:, FOLD:], turned[:, 128:FOLD]], axis=1
    )
    turned = split(turned)
    by_cos = mm3(turned, cos_e)
    by_sin = mm3(turned, sin_e)
    real = by_cos[:128] + by_sin[128:]
    imag = by_cos[128:] - by_sin[:128]

    def influence(at, weight):
        total = green_ref[1] + column_ref[1, at]
        inverse = jnp.where(total == 0.0, 0.0, 1.0 / jnp.where(total == 0.0, 1.0, total))
        return green_ref[0] * (inverse * (column_ref[0, at] * weight))

    first = me == 0
    weight = jnp.where(first, 1.0, 2.0)
    green_a = influence(me, weight)
    green_b = influence(jnp.where(first, 128, me), weight)
    modes = split(
        jnp.concatenate(
            [green_a * real, green_a * imag, green_b * real, green_b * imag], axis=0
        )
    )
    by_cos = mm3(modes, cos_e, NT)
    by_sin = mm3(modes, sin_e, NT)

    def widen(x):
        return jnp.concatenate([x, x[:, :128]], axis=1)

    def back(at):
        real = widen(by_cos[at : at + 128] - by_sin[at + 128 : at + 256])
        imag = widen(by_sin[at : at + 128] + by_cos[at + 128 : at + 256])
        return real * cos_t - imag * sin_t, imag * cos_t + real * sin_t

    real_a, imag_a = back(0)
    real_b, imag_b = back(256)
    field_r = mm3(
        (dft_b_ref[0, :128], dft_b_ref[1, :128]),
        split(jnp.concatenate([real_a, -imag_a], axis=0)),
    )
    field_i = mm3(
        (dft_b_ref[0, 128:], dft_b_ref[1, 128:]),
        split(jnp.concatenate([-real_b, imag_b], axis=0)),
    )
    partial = jnp.sum(tiles[:128] * field_r + tiles[128:] * field_i, keepdims=True)
    partial = partial * (0.5 / (ND * ATOMS))
    lane = iota((ND, 128), 1)
    for t in range(6):
        piece = field_r[:, t * 128 : (t + 1) * 128]
        if t == 5:
            piece = jnp.where(lane == 127, partial, piece)
        out_two[:, t, :] = piece
        out_two[:, 6 + t, :] = field_i[:, t * 128 : (t + 1) * 128]

    exchange(out_two, in_two, 1)
    settle(out_two, in_two, 1)

    planes = gathered(in_two)
    inner = mm3(split(planes), (mix_ref[0], mix_ref[1]))
    wave = wave_ref[:, :256]
    wave_slope = wave_ref[:, 256:]
    rows = [
        jnp.sum(wave * inner[:, :256], axis=0, keepdims=True),
        -jnp.sum(wave * inner[:, 256:512], axis=0, keepdims=True),
        -jnp.sum(wave_slope * inner[:, :256], axis=0, keepdims=True),
        -jnp.sum(wave * inner[:, 512:], axis=0, keepdims=True),
    ]
    for c in range(4):
        atom_ref[c : c + 1, :] = rows[c][:, :128]
        centroid_ref[c : c + 1, :] = rows[c][:, 128:] * oxygen
    energy_ref[...] = jnp.broadcast_to(
        jnp.sum(planes[:128, TILE - 1 : TILE], axis=0, keepdims=True), (8, 128)
    )


def long_range(own, dip):
    vmem = pl.BlockSpec(memory_space=pltpu.VMEM)
    smem = pl.BlockSpec(memory_space=pltpu.SMEM)
    consts = [jnp.asarray(t) for t in tables()]
    return pl.pallas_call(
        long_kernel,
        out_shape=(
            jax.ShapeDtypeStruct((8, ATOMS), F32),
            jax.ShapeDtypeStruct((4, ATOMS), F32),
            jax.ShapeDtypeStruct((4, ATOMS), F32),
            jax.ShapeDtypeStruct((8, ATOMS), F32),
        ),
        in_specs=[vmem] * 8 + [smem],
        out_specs=(vmem,) * 4,
        scratch_shapes=[
            pltpu.VMEM((2, TILE, TILE), BF16),
            pltpu.VMEM((CY, 512), F32),
            pltpu.VMEM((2, FOLD, MODES), F32),
            pltpu.VMEM((ND, 12, 128), F32),
            pltpu.VMEM((ND, 12, 128), F32),
            pltpu.VMEM((ND, 12, 128), F32),
            pltpu.VMEM((ND, 12, 128), F32),
            pltpu.SemaphoreType.DMA((2,)),
            pltpu.SemaphoreType.DMA((2,)),
        ],
        compiler_params=pltpu.CompilerParams(
            collective_id=1, has_side_effects=True, vmem_limit_bytes=50 << 20
        ),
        name="long_range",
    )(own, dip, *consts)


def local(positions, species, neighbours, *weights):
    own = jnp.concatenate(
        [
            positions.reshape(3, ATOMS),
            species.reshape(1, ATOMS).astype(F32),
            jnp.zeros((4, ATOMS), F32),
        ],
        axis=0,
    )
    ghosts = halo(own)
    weights = [w.reshape(1, -1) if w.ndim == 1 else w for w in weights]
    dip = net(ghosts, neighbours.reshape(ATOMS, ATOMS), weights)
    dipole, atom, centroid, energy = long_range(own, dip)
    return (
        dipole[:3].reshape(3, 1, 1, 1, ATOMS),
        atom.reshape(4, 1, 1, 1, ATOMS),
        centroid.reshape(4, 1, 1, 1, ATOMS),
        energy[0, 0],
    )


def solution(mesh):
    return jax.shard_map(
        local,
        mesh=mesh,
        in_specs=(
            P(None, "wide", "narrow", None, None),
            P("wide", "narrow", None, None),
            P("wide", "narrow", None, None, None),
        )
        + (P(),) * 13,
        out_specs=(
            P(None, "wide", "narrow", None, None),
            P(None, "wide", "narrow", None, None),
            P(None, "wide", "narrow", None, None),
            P(),
        ),
        check_vma=False,
    )
```

```python
import functools
import math

import jax
import jax.numpy as jnp
import numpy as np
from jax import lax
from jax.experimental import pallas as pl
from jax.experimental.pallas import tpu as pltpu
from jax.sharding import PartitionSpec as P

NW, NN = 8, 16
ND = NW * NN
CX, CY, CZ = 32, 256, 16
TX, TZ = 40, 19
TILE = 768
FOLD = 640
MODES = 512
ATOMS = 128
F32 = jnp.float32
BF16 = jnp.bfloat16
MESH = pl.DeviceIdType.MESH
HIGHEST = lax.Precision.HIGHEST
NT = (((1,), (1,)), ((), ()))
NNN = (((1,), (0,)), ((), ()))


def split(x):
    high = x.astype(BF16)
    return high, (x - high.astype(F32)).astype(BF16)


def mm(a, b, dims=NNN):
    return lax.dot_general(a, b, dims, preferred_element_type=F32)


def mm3(a, b, dims=NNN):
    return mm(a[0], b[0], dims) + mm(a[0], b[1], dims) + mm(a[1], b[0], dims)


def exact(a, b, dims=NNN):
    return lax.dot_general(a, b, dims, precision=HIGHEST, preferred_element_type=F32)


def iota(shape, dim):
    return lax.broadcasted_iota(jnp.int32, shape, dim)


def spline(offset):
    square = offset * offset
    cube = square * offset
    remain = 4.0 - offset
    one = cube * (1.0 / 6.0)
    two = (-3.0 * cube + 12.0 * square - 12.0 * offset + 4.0) * (1.0 / 6.0)
    three = (3.0 * cube - 24.0 * square + 60.0 * offset - 44.0) * (1.0 / 6.0)
    four = remain * remain * remain * (1.0 / 6.0)
    value = jnp.where(
        offset < 1.0, one, jnp.where(offset < 2.0, two, jnp.where(offset < 3.0, three, four))
    )
    return jnp.where((offset >= 0.0) & (offset < 4.0), value, 0.0)


def slope(offset):
    square = offset * offset
    remain = 4.0 - offset
    one = square * 0.5
    two = (-9.0 * square + 24.0 * offset - 12.0) * (1.0 / 6.0)
    three = (9.0 * square - 48.0 * offset + 60.0) * (1.0 / 6.0)
    four = -0.5 * remain * remain
    value = jnp.where(
        offset < 1.0, one, jnp.where(offset < 2.0, two, jnp.where(offset < 3.0, three, four))
    )
    return jnp.where((offset >= 0.0) & (offset < 4.0), value, 0.0)


def halo_kernel(positions_ref, species_ref, ghost_ref, own_ref, send_sem, recv_sem):
    wide = lax.axis_index("wide")
    narrow = lax.axis_index("narrow")
    steps = [(sx, sz) for sx in range(3) for sz in range(3) if (sx, sz) != (1, 1)]
    barrier = pltpu.get_barrier_semaphore()

    def device(sx, sz):
        return (lax.rem(wide + (NW + 1 - sx), NW), lax.rem(narrow + (NN + 1 - sz), NN))

    own_ref[...] = jnp.concatenate(
        [positions_ref[c, 0, 0] for c in range(3)]
        + [species_ref[0, 0].astype(F32), jnp.zeros((4, ATOMS), F32)],
        axis=0,
    )
    ghost_ref[4] = own_ref[...]
    for sx, sz in steps:
        pl.semaphore_signal(barrier, inc=1, device_id=device(sx, sz), device_id_type=MESH)
    pl.semaphore_wait(barrier, len(steps))
    copies = []
    for at, (sx, sz) in enumerate(steps):
        copy = pltpu.make_async_remote_copy(
            src_ref=own_ref,
            dst_ref=ghost_ref.at[sx * 3 + sz],
            send_sem=send_sem.at[at],
            recv_sem=recv_sem.at[at],
            device_id=device(sx, sz),
            device_id_type=MESH,
        )
        copy.start()
        copies.append(copy)
    for copy in copies:
        copy.wait()


def halo(positions, species):
    vmem = pl.BlockSpec(memory_space=pltpu.VMEM)
    return pl.pallas_call(
        halo_kernel,
        out_shape=jax.ShapeDtypeStruct((9, 8, ATOMS), F32),
        in_specs=[vmem, vmem],
        out_specs=vmem,
        scratch_shapes=[
            pltpu.VMEM((8, ATOMS), F32),
            pltpu.SemaphoreType.DMA((8,)),
            pltpu.SemaphoreType.DMA((8,)),
        ],
        compiler_params=pltpu.CompilerParams(collective_id=0, has_side_effects=True),
        name="halo",
    )(positions, species)


def spread_rows(rows, count):
    r = iota((rows, count), 0)
    c = iota((rows, count), 1)
    i = r & 31
    return jnp.where((i < 25) & (c == (r >> 5) * 25 + i), 1.0, 0.0).astype(F32)


def network(
    ghost_ref,
    near_ref,
    e1w_ref,
    e1b_ref,
    e2w_ref,
    e2b_ref,
    e3w_ref,
    e3b_ref,
    f1b_ref,
    f2b_ref,
    f3b_ref,
    f1w_ref,
    f2w_ref,
    f3w_ref,
    fow_ref,
    table_ref,
    own_ref,
    mat_ref,
    arrived,
):
    extent = (float(CX), float(CY), float(CZ))
    for k in range(9):
        shift = (float(k // 3 - 1), 0.0, float(k % 3 - 1))
        for c in range(3):
            table_ref[k * 4 + c] = jnp.broadcast_to(ghost_ref[k, c : c + 1, :] + shift[c], (8, ATOMS))
        table_ref[k * 4 + 3] = jnp.broadcast_to(ghost_ref[k, 3:4, :], (8, ATOMS))
    for c in range(3):
        own_ref[c] = jnp.broadcast_to(ghost_ref[4, c : c + 1, :], (ATOMS, ATOMS)).T

    pick1 = spread_rows(32, 25)
    pick2 = spread_rows(64, 50)
    pick3 = spread_rows(128, 100)

    def column(pick, row):
        return exact(pick, jnp.broadcast_to(row, (ATOMS, row.shape[1])), NT)

    w_oxygen = column(pick1, e1w_ref[0:1, :])
    w_hydrogen = column(pick1, e1w_ref[1:2, :])
    b_oxygen = column(pick1, e1b_ref[0:1, :])
    b_hydrogen = column(pick1, e1b_ref[1:2, :])
    bias2 = column(pick2, e2b_ref[...])
    bias3 = column(pick3, e3b_ref[...])
    w2 = exact(pick2, exact(pick1, e2w_ref[...]), NT)
    w3 = exact(pick3, exact(pick2, e3w_ref[...]), NT)
    w2_high, w2_low = split(w2)
    w3_high, w3_low = split(w3)
    w2_all = jnp.concatenate([w2_high, w2_high, w2_low], axis=1)
    w3_all = jnp.concatenate([w3_high, w3_high, w3_low], axis=1)
    bias2 = jnp.concatenate([bias2] * 8, axis=1)
    bias3 = jnp.concatenate([bias3] * 8, axis=1)
    sublane = iota((8, ATOMS), 0)

    def group(g, carry):
        rows = pl.ds(pl.multiple_of(g * 8, 8), 8)
        code = near_ref[rows, :]
        slot = code & 127
        offset = code >> 7
        brick = (offset * 11) >> 5
        step_y = (offset - 3 * brick - 1).astype(F32)
        parts = [jnp.zeros((8, ATOMS), F32)] * 4
        for k in range(9):
            here = brick == k
            for c in range(4):
                found = jnp.take_along_axis(table_ref[k * 4 + c], slot, axis=1)
                parts[c] = jnp.where(here, found, parts[c])
        parts[1] = parts[1] + step_y
        scaled = [(parts[c] - own_ref[c, rows, :]) * (extent[c] / 24.0) for c in range(3)]
        square = scaled[0] * scaled[0] + scaled[1] * scaled[1] + scaled[2] * scaled[2]
        smooth = 1.0 / (1.0 + square)
        kind = parts[3]
        pieces = []
        for b in range(8):
            s = jnp.broadcast_to(smooth[b : b + 1, :], (32, ATOMS))
            h = jnp.broadcast_to(kind[b : b + 1, :], (32, ATOMS)) > 0.5
            pieces.append(
                jnp.where(h, w_hydrogen, w_oxygen) * s + jnp.where(h, b_hydrogen, b_oxygen)
            )
        one = jnp.tanh(jnp.concatenate(pieces, axis=1))
        high, low = split(one)
        two = jnp.tanh(mm(w2_all, jnp.concatenate([high, low, high], axis=0)) + bias2)
        two = two + jnp.concatenate([one, one], axis=0)
        high, low = split(two)
        three = jnp.tanh(mm(w3_all, jnp.concatenate([high, low, high], axis=0)) + bias3)
        three = three + jnp.concatenate([two, two], axis=0)
        high, low = split(three)
        scale = smooth * (1.0 / 128.0)
        radial = [scale] + [scale * scaled[c] for c in range(3)]
        blocks = []
        for b in range(8):
            mine = sublane == b
            blocks.append(jnp.concatenate([jnp.where(mine, r, 0.0) for r in radial], axis=0))
        radial = jnp.concatenate(blocks, axis=1)
        r_high, r_low = split(radial)
        found = mm(r_high, high, NT) + mm(r_high, low, NT) + mm(r_low, high, NT)
        for p in range(4):
            mat_ref[p, rows, :] = found[p * 8 : (p + 1) * 8]
        return carry

    lax.fori_loop(0, ATOMS // 8, group, 0, unroll=4)

    row = iota((ATOMS, ATOMS), 0)
    lane = iota((ATOMS, ATOMS), 1)
    inner = row & 31
    kept = jnp.where(inner < 25, (row >> 5) * 25 + inner, -1)
    pick = [jnp.where(kept == (lane >> 4) + 8 * t, 1.0, 0.0).astype(BF16) for t in range(13)]
    pick.append(jnp.where(row == (lane & 15), 1.0, 0.0).astype(BF16))
    pick = jnp.concatenate(pick, axis=1)
    matrix = [mat_ref[p] for p in range(4)]
    entries = None
    for p in range(4):
        high, low = split(matrix[p])
        wide = mm(high, pick) + mm(low, pick)
        tiled = wide[:, 1664:]
        term = jnp.concatenate([wide[:, t * 128 : (t + 1) * 128] * tiled for t in range(13)], axis=1)
        entries = term if entries is None else entries + term
    arrived()
    hidden = mm3(split(entries[:, :1600]), split(f1w_ref[...]), NT)
    hidden = jnp.tanh(hidden + f1b_ref[...])
    hidden = hidden + jnp.tanh(mm3(split(hidden), split(f2w_ref[...])) + f2b_ref[...])
    hidden = hidden + jnp.tanh(mm3(split(hidden), split(f3w_ref[...])) + f3b_ref[...])
    coeffs = mm3(split(hidden), split(exact(pick3, fow_ref[...])), NT)
    result = jnp.zeros((ATOMS, ATOMS), F32)
    for c in range(3):
        total = jnp.sum(coeffs * matrix[1 + c], axis=1, keepdims=True)
        result = jnp.where(lane == c, total, result)
    return result.T[:8]


def np_split(x):
    x = np.asarray(x, np.float32)
    high = x.astype(jnp.bfloat16)
    low = (x - high.astype(np.float32)).astype(jnp.bfloat16)
    return np.stack([high, low])


@functools.lru_cache(None)
def tables():
    m = np.arange(128)[:, None]
    y = np.arange(CY)[None, :]
    angle = 2 * np.pi * (m * y % CY) / CY
    lower = -np.sin(angle)
    lower[0] = 1 - 2 * (y[0] % 2)
    dft_y = np_split(np.concatenate([np.cos(angle), lower]))
    j, k = np.divmod(np.arange(ND), NN)
    phi = 2 * np.pi * ((2 * j[:, None] * j[None] + k[:, None] * k[None]) % 16) / 16
    cos, sin = np.cos(phi), np.sin(phi)
    dft_b = np_split(np.block([[cos, sin], [-sin, cos]]))
    z, x = np.divmod(np.arange(TILE), TX)
    turn = 2 * np.pi * ((j[:, None] * (x - 3)[None] + k[:, None] * (z - 3)[None]) % 256) / 256
    twiddle = np.stack([np.cos(turn), np.sin(turn)]).astype(np.float32)
    v, u = np.divmod(np.arange(MODES), 32)
    ax = 2 * np.pi * ((np.arange(TX)[:, None] - 3) * u[None] % 32) / 32
    az = 2 * np.pi * ((np.arange(16)[:, None] - 3) * v[None] % 16) / 16
    fac_x = np.stack([np.cos(ax), np.sin(ax)]).astype(np.float32)
    fac_z = np.stack([np.cos(az), np.sin(az)]).astype(np.float32)

    def fold(i, n):
        return np.where(2 * i >= n, i - n, i) / n

    def modulus(i, n):
        return 36.0 / (4 + 2 * np.cos(2 * np.pi * i / n)) ** 2

    def decay(f):
        return np.exp(-np.pi**2 * f * f / 0.81)

    mx = j[:, None] + 8 * u[None]
    mz = k[:, None] + 16 * v[None]
    fx, fz = fold(mx, 256), fold(mz, 256)
    scale = 0.25 / (np.pi * 256.0**3)
    plane = scale * decay(fx) * decay(fz) * modulus(mx, 256) * modulus(mz, 256)
    green = np.stack([plane, fx * fx + fz * fz]).astype(np.float32)
    my = np.arange(129)
    fy = fold(my, 256)
    column = np.stack([decay(fy) * modulus(my, 256), fy * fy]).astype(np.float32)
    return dft_y, dft_b, twiddle, fac_x, fac_z, green, column


EARLY = (
    ((9, 8, ATOMS), F32),
    ((ATOMS, ATOMS), jnp.int32),
    ((2, 25), F32),
    ((2, 25), F32),
    ((25, 50), F32),
    ((1, 50), F32),
    ((50, 100), F32),
    ((1, 100), F32),
    ((1, 240), F32),
    ((1, 240), F32),
    ((1, 240), F32),
)
LATE = (
    ((240, 1600), F32),
    ((240, 240), F32),
    ((240, 240), F32),
    ((100, 240), F32),
    ((2, 256, CY), BF16),
    ((2, 256, 256), BF16),
    ((2, ND, TILE), F32),
    ((2, TX, MODES), F32),
    ((2, 16, MODES), F32),
    ((2, ND, MODES), F32),
)


def main_kernel(*refs):
    count = len(EARLY) + len(LATE)
    column_ref = refs[0]
    far = refs[1 : 1 + count]
    result_ref = refs[1 + count]
    near = refs[2 + count : 2 + 2 * count]
    (
        ghost_ref,
        near_ref,
        e1w_ref,
        e1b_ref,
        e2w_ref,
        e2b_ref,
        e3w_ref,
        e3b_ref,
        f1b_ref,
        f2b_ref,
        f3b_ref,
    ) = near[: len(EARLY)]
    (
        table_ref,
        home_ref,
        mat_ref,
        mix_ref,
        wave_ref,
        tab_ref,
        out_one,
        in_one,
        out_two,
        in_two,
        late_sem,
        send_sem,
        recv_sem,
    ) = refs[2 + 2 * count :]
    f1w_ref, f2w_ref, f3w_ref, fow_ref = near[len(EARLY) : len(EARLY) + 4]
    dft_y_ref, dft_b_ref, twiddle_ref, fac_x_ref, fac_z_ref, green_ref = near[len(EARLY) + 4 :]
    fetch = [pltpu.make_async_copy(far[i], near[i], late_sem.at[i]) for i in range(count)]
    for copy in fetch:
        copy.start()
    wide = lax.axis_index("wide")
    narrow = lax.axis_index("narrow")
    me = wide * NN + narrow
    barrier = pltpu.get_barrier_semaphore()

    def peer(d):
        at = lax.rem(me + d, ND)
        return at, (at // NN, lax.rem(at, NN))

    def greet(d, carry):
        pl.semaphore_signal(barrier, inc=1, device_id=peer(d)[1], device_id_type=MESH)
        return carry

    lax.fori_loop(1, ND, greet, 0)

    def arrived():
        for copy in fetch[len(EARLY) :]:
            copy.wait()

    for copy in fetch[: len(EARLY)]:
        copy.wait()
    dip = network(
        ghost_ref,
        near_ref,
        e1w_ref,
        e1b_ref,
        e2w_ref,
        e2b_ref,
        e3w_ref,
        e3b_ref,
        f1b_ref,
        f2b_ref,
        f3b_ref,
        f1w_ref,
        f2w_ref,
        f3w_ref,
        fow_ref,
        table_ref,
        home_ref,
        mat_ref,
        arrived,
    )

    kind = ghost_ref[4, 3:4, :]
    oxygen = 1.0 - kind
    result_ref[0:8, :] = dip * oxygen
    shift = 0.5 * jnp.tanh(dip)

    def sites(c, extent):
        atom = ghost_ref[4, c : c + 1, :] * float(extent)
        return jnp.concatenate([atom, atom + shift[c : c + 1, :]], axis=1)

    charge = jnp.concatenate([6.0 * oxygen + kind, -8.0 * oxygen], axis=1)
    off_x = sites(0, CX) - (iota((TX, 256), 0).astype(F32) - 3.0)
    off_z = sites(2, CZ) - (iota((24, 256), 0).astype(F32) - 3.0)
    off_y = sites(1, CY) - iota((CY, 256), 0).astype(F32)
    off_y = jnp.where(off_y < 0.0, off_y + float(CY), off_y)
    wx, sx = spline(off_x), slope(off_x)
    wz, sz = spline(off_z), slope(off_z)
    wave = mm3(
        (dft_y_ref[0], dft_y_ref[1]),
        split(jnp.concatenate([spline(off_y), slope(off_y)], axis=1)),
    )
    wave_ref[...] = wave
    rest = jnp.zeros((TILE - TX * TZ, 256), F32)
    for at, (left, right) in enumerate(((wz, wx), (wz, sx), (sz, wx))):
        full = jnp.concatenate([left[z : z + 1, :] * right for z in range(TZ)] + [rest], axis=0)
        high, low = split(full)
        mix_ref[0, :, at * 256 : (at + 1) * 256] = high
        mix_ref[1, :, at * 256 : (at + 1) * 256] = low
    spread = mm3(
        split(wave[:, :256] * charge), (mix_ref[0, :, :256], mix_ref[1, :, :256]), NT
    )
    for part in range(2):
        for t in range(6):
            out_one[:, part * 6 + t, :] = spread[part * 128 : (part + 1) * 128, t * 128 : (t + 1) * 128]

    pl.semaphore_wait(barrier, ND - 1)

    def exchange(out_ref, in_ref, s):
        def one(d, carry):
            at, device = peer(d)
            pltpu.make_async_remote_copy(
                src_ref=out_ref.at[at],
                dst_ref=in_ref.at[me],
                send_sem=send_sem.at[s],
                recv_sem=recv_sem.at[s],
                device_id=device,
                device_id_type=MESH,
            ).start()
            return carry

        lax.fori_loop(1, ND, one, 0)
        in_ref[me] = out_ref[me]

    def settle(out_ref, in_ref, s):
        whole = pltpu.make_async_remote_copy(
            src_ref=out_ref.at[pl.ds(0, ND - 1)],
            dst_ref=in_ref.at[pl.ds(0, ND - 1)],
            send_sem=send_sem.at[s],
            recv_sem=recv_sem.at[s],
            device_id=peer(1)[1],
            device_id_type=MESH,
        )
        whole.wait_send()
        whole.wait_recv()

    exchange(out_one, in_one, 0)

    def build(z, carry):
        cz = fac_z_ref[0, pl.ds(z, 1), :]
        zz = fac_z_ref[1, pl.ds(z, 1), :]
        cx, xx = fac_x_ref[0], fac_x_ref[1]
        rows = pl.ds(pl.multiple_of(z * TX, 8), TX)
        tab_ref[0, rows, :] = cx * cz - xx * zz
        tab_ref[1, rows, :] = xx * cz + cx * zz
        return carry

    lax.fori_loop(0, 16, build, 0)
    cos_e = split(tab_ref[0])
    sin_e = split(tab_ref[1])

    settle(out_one, in_one, 0)

    def gathered(in_ref):
        return jnp.concatenate(
            [
                jnp.concatenate([in_ref[:, part * 6 + t, :] for t in range(6)], axis=1)
                for part in range(2)
            ],
            axis=0,
        )

    tiles = gathered(in_one)
    bricks = mm3((dft_b_ref[0], dft_b_ref[1]), split(tiles))
    real, imag = bricks[:128], bricks[128:]
    cos_t, sin_t = twiddle_ref[0], twiddle_ref[1]
    turned = jnp.concatenate(
        [real * cos_t + imag * sin_t, imag * cos_t - real * sin_t], axis=0
    )
    turned = jnp.concatenate(
        [turned[:, :128] + turned[:, FOLD:], turned[:, 128:FOLD]], axis=1
    )
    turned = split(turned)
    by_cos = mm3(turned, cos_e)
    by_sin = mm3(turned, sin_e)
    real = by_cos[:128] + by_sin[128:]
    imag = by_cos[128:] - by_sin[:128]

    def influence(at, weight):
        total = green_ref[1] + column_ref[1, at]
        inverse = jnp.where(total == 0.0, 0.0, 1.0 / jnp.where(total == 0.0, 1.0, total))
        return green_ref[0] * (inverse * (column_ref[0, at] * weight))

    first = me == 0
    weight = jnp.where(first, 1.0, 2.0)
    green_a = influence(me, weight)
    green_b = influence(jnp.where(first, 128, me), weight)
    modes = split(
        jnp.concatenate(
            [green_a * real, green_a * imag, green_b * real, green_b * imag], axis=0
        )
    )
    by_cos = mm3(modes, cos_e, NT)
    by_sin = mm3(modes, sin_e, NT)

    def widen(x):
        return jnp.concatenate([x, x[:, :128]], axis=1)

    def back(at):
        real = widen(by_cos[at : at + 128] - by_sin[at + 128 : at + 256])
        imag = widen(by_sin[at : at + 128] + by_cos[at + 128 : at + 256])
        return real * cos_t - imag * sin_t, imag * cos_t + real * sin_t

    real_a, imag_a = back(0)
    real_b, imag_b = back(256)
    field_r = mm3(
        (dft_b_ref[0, :128], dft_b_ref[1, :128]),
        split(jnp.concatenate([real_a, -imag_a], axis=0)),
    )
    field_i = mm3(
        (dft_b_ref[0, 128:], dft_b_ref[1, 128:]),
        split(jnp.concatenate([-real_b, imag_b], axis=0)),
    )
    partial = jnp.sum(tiles[:128] * field_r + tiles[128:] * field_i, keepdims=True)
    partial = partial * (0.5 / (ND * ATOMS))
    lane = iota((ND, 128), 1)
    for t in range(6):
        piece = field_r[:, t * 128 : (t + 1) * 128]
        if t == 5:
            piece = jnp.where(lane == 127, partial, piece)
        out_two[:, t, :] = piece
        out_two[:, 6 + t, :] = field_i[:, t * 128 : (t + 1) * 128]

    exchange(out_two, in_two, 1)
    settle(out_two, in_two, 1)

    planes = gathered(in_two)
    inner = mm3(split(planes), (mix_ref[0], mix_ref[1]))
    wave = wave_ref[:, :256]
    wave_slope = wave_ref[:, 256:]
    rows = [
        jnp.sum(wave * inner[:, :256], axis=0, keepdims=True),
        -jnp.sum(wave * inner[:, 256:512], axis=0, keepdims=True),
        -jnp.sum(wave_slope * inner[:, :256], axis=0, keepdims=True),
        -jnp.sum(wave * inner[:, 512:], axis=0, keepdims=True),
    ]
    total = jnp.sum(planes[:128, TILE - 1 : TILE], axis=0, keepdims=True)
    atom = [r[:, :128] for r in rows]
    centroid = [r[:, 128:] * oxygen for r in rows]
    result_ref[8:24, :] = jnp.concatenate(
        atom + centroid + [jnp.broadcast_to(total, (8, ATOMS))], axis=0
    )


def deal_kernel(result_ref, dipole_ref, atom_ref, centroid_ref, energy_ref):
    for c in range(3):
        dipole_ref[c, 0, 0] = result_ref[c : c + 1, :]
    for c in range(4):
        atom_ref[c, 0, 0] = result_ref[8 + c : 9 + c, :]
        centroid_ref[c, 0, 0] = result_ref[12 + c : 13 + c, :]
    energy_ref[...] = result_ref[16:17, 0:1]


def local(
    positions,
    species,
    neighbours,
    e1w,
    e1b,
    e2w,
    e2b,
    e3w,
    e3b,
    f1w,
    f1b,
    f2w,
    f2b,
    f3w,
    f3b,
    fow,
):
    ghosts = halo(positions, species)
    *late, column = [jnp.asarray(t) for t in tables()]
    vmem = pl.BlockSpec(memory_space=pltpu.VMEM)
    anywhere = pl.BlockSpec(memory_space=pl.ANY)
    row = lambda x: x.reshape(1, -1)
    result = pl.pallas_call(
        main_kernel,
        out_shape=jax.ShapeDtypeStruct((24, ATOMS), F32),
        in_specs=[pl.BlockSpec(memory_space=pltpu.SMEM)] + [anywhere] * (len(EARLY) + len(LATE)),
        out_specs=vmem,
        scratch_shapes=[pltpu.VMEM(shape, dtype) for shape, dtype in EARLY + LATE]
        + [
            pltpu.VMEM((36, 8, ATOMS), F32),
            pltpu.VMEM((3, ATOMS, ATOMS), F32),
            pltpu.VMEM((4, ATOMS, ATOMS), F32),
            pltpu.VMEM((2, TILE, TILE), BF16),
            pltpu.VMEM((CY, 512), F32),
            pltpu.VMEM((2, FOLD, MODES), F32),
            pltpu.VMEM((ND, 12, 128), F32),
            pltpu.VMEM((ND, 12, 128), F32),
            pltpu.VMEM((ND, 12, 128), F32),
            pltpu.VMEM((ND, 12, 128), F32),
            pltpu.SemaphoreType.DMA((len(EARLY) + len(LATE),)),
            pltpu.SemaphoreType.DMA((2,)),
            pltpu.SemaphoreType.DMA((2,)),
        ],
        compiler_params=pltpu.CompilerParams(
            collective_id=1, has_side_effects=True, vmem_limit_bytes=58 << 20
        ),
        name="main",
    )(
        column,
        ghosts,
        neighbours.reshape(ATOMS, ATOMS),
        e1w,
        e1b,
        e2w,
        row(e2b),
        e3w,
        row(e3b),
        row(f1b),
        row(f2b),
        row(f3b),
        f1w.T,
        f2w,
        f3w,
        fow.T,
        *late,
    )
    dipole, atom, centroid, energy = pl.pallas_call(
        deal_kernel,
        out_shape=(
            jax.ShapeDtypeStruct((3, 1, 1, 1, ATOMS), F32),
            jax.ShapeDtypeStruct((4, 1, 1, 1, ATOMS), F32),
            jax.ShapeDtypeStruct((4, 1, 1, 1, ATOMS), F32),
            jax.ShapeDtypeStruct((1, 1), F32),
        ),
        in_specs=[vmem],
        out_specs=(vmem,) * 4,
        name="deal",
    )(result)
    return dipole, atom, centroid, energy.reshape(())


def solution(mesh):
    return jax.shard_map(
        local,
        mesh=mesh,
        in_specs=(
            P(None, "wide", "narrow", None, None),
            P("wide", "narrow", None, None),
            P("wide", "narrow", None, None, None),
        )
        + (P(),) * 13,
        out_specs=(
            P(None, "wide", "narrow", None, None),
            P(None, "wide", "narrow", None, None),
            P(None, "wide", "narrow", None, None),
            P(),
        ),
        check_vma=False,
    )
```

```python
import functools
import math

import jax
import jax.numpy as jnp
import numpy as np
from jax import lax
from jax.experimental import pallas as pl
from jax.experimental.pallas import tpu as pltpu
from jax.sharding import PartitionSpec as P

NW, NN = 8, 16
ND = NW * NN
CX, CY, CZ = 32, 256, 16
TX, TZ = 32, 19
TILE = 640
FOLD = 512
ROWS = 10
MODES = 512
ATOMS = 128
F32 = jnp.float32
BF16 = jnp.bfloat16
MESH = pl.DeviceIdType.MESH
HIGHEST = lax.Precision.HIGHEST
NT = (((1,), (1,)), ((), ()))
NNN = (((1,), (0,)), ((), ()))


def split(x):
    high = x.astype(BF16)
    return high, (x - high.astype(F32)).astype(BF16)


def mm(a, b, dims=NNN):
    return lax.dot_general(a, b, dims, preferred_element_type=F32)


def mm3(a, b, dims=NNN):
    return mm(a[0], b[0], dims) + mm(a[0], b[1], dims) + mm(a[1], b[0], dims)


def exact(a, b, dims=NNN):
    return lax.dot_general(a, b, dims, precision=HIGHEST, preferred_element_type=F32)


def iota(shape, dim):
    return lax.broadcasted_iota(jnp.int32, shape, dim)


def spline(offset):
    square = offset * offset
    cube = square * offset
    remain = 4.0 - offset
    one = cube * (1.0 / 6.0)
    two = (-3.0 * cube + 12.0 * square - 12.0 * offset + 4.0) * (1.0 / 6.0)
    three = (3.0 * cube - 24.0 * square + 60.0 * offset - 44.0) * (1.0 / 6.0)
    four = remain * remain * remain * (1.0 / 6.0)
    value = jnp.where(
        offset < 1.0, one, jnp.where(offset < 2.0, two, jnp.where(offset < 3.0, three, four))
    )
    return jnp.where((offset >= 0.0) & (offset < 4.0), value, 0.0)


def slope(offset):
    square = offset * offset
    remain = 4.0 - offset
    one = square * 0.5
    two = (-9.0 * square + 24.0 * offset - 12.0) * (1.0 / 6.0)
    three = (9.0 * square - 48.0 * offset + 60.0) * (1.0 / 6.0)
    four = -0.5 * remain * remain
    value = jnp.where(
        offset < 1.0, one, jnp.where(offset < 2.0, two, jnp.where(offset < 3.0, three, four))
    )
    return jnp.where((offset >= 0.0) & (offset < 4.0), value, 0.0)


def halo_kernel(positions_ref, species_ref, ghost_ref, own_ref, send_sem, recv_sem):
    wide = lax.axis_index("wide")
    narrow = lax.axis_index("narrow")
    steps = [(sx, sz) for sx in range(3) for sz in range(3) if (sx, sz) != (1, 1)]
    barrier = pltpu.get_barrier_semaphore()

    def device(sx, sz):
        return (lax.rem(wide + (NW + 1 - sx), NW), lax.rem(narrow + (NN + 1 - sz), NN))

    own_ref[...] = jnp.concatenate(
        [positions_ref[c, 0, 0] for c in range(3)]
        + [species_ref[0, 0].astype(F32), jnp.zeros((4, ATOMS), F32)],
        axis=0,
    )
    ghost_ref[4] = own_ref[...]
    for sx, sz in steps:
        pl.semaphore_signal(barrier, inc=1, device_id=device(sx, sz), device_id_type=MESH)
    pl.semaphore_wait(barrier, len(steps))
    copies = []
    for at, (sx, sz) in enumerate(steps):
        copy = pltpu.make_async_remote_copy(
            src_ref=own_ref,
            dst_ref=ghost_ref.at[sx * 3 + sz],
            send_sem=send_sem.at[at],
            recv_sem=recv_sem.at[at],
            device_id=device(sx, sz),
            device_id_type=MESH,
        )
        copy.start()
        copies.append(copy)
    for copy in copies:
        copy.wait()


def halo(positions, species):
    vmem = pl.BlockSpec(memory_space=pltpu.VMEM)
    return pl.pallas_call(
        halo_kernel,
        out_shape=jax.ShapeDtypeStruct((9, 8, ATOMS), F32),
        in_specs=[vmem, vmem],
        out_specs=vmem,
        scratch_shapes=[
            pltpu.VMEM((8, ATOMS), F32),
            pltpu.SemaphoreType.DMA((8,)),
            pltpu.SemaphoreType.DMA((8,)),
        ],
        compiler_params=pltpu.CompilerParams(collective_id=0, has_side_effects=True),
        name="halo",
    )(positions, species)


def spread_rows(rows, count):
    r = iota((rows, count), 0)
    c = iota((rows, count), 1)
    i = r & 31
    return jnp.where((i < 25) & (c == (r >> 5) * 25 + i), 1.0, 0.0).astype(F32)


def network(
    ghost_ref,
    near_ref,
    e1w_ref,
    e1b_ref,
    e2w_ref,
    e2b_ref,
    e3w_ref,
    e3b_ref,
    f1b_ref,
    f2b_ref,
    f3b_ref,
    f1w_ref,
    f2w_ref,
    f3w_ref,
    fow_ref,
    table_ref,
    own_ref,
    mat_ref,
    arrived,
):
    extent = (float(CX), float(CY), float(CZ))
    for k in range(9):
        shift = (float(k // 3 - 1), 0.0, float(k % 3 - 1))
        for c in range(3):
            table_ref[k * 4 + c] = jnp.broadcast_to(ghost_ref[k, c : c + 1, :] + shift[c], (8, ATOMS))
        table_ref[k * 4 + 3] = jnp.broadcast_to(ghost_ref[k, 3:4, :], (8, ATOMS))
    for c in range(3):
        own_ref[c] = jnp.broadcast_to(ghost_ref[4, c : c + 1, :], (ATOMS, ATOMS)).T

    pick1 = spread_rows(32, 25)
    pick2 = spread_rows(64, 50)
    pick3 = spread_rows(128, 100)

    def column(pick, row):
        return exact(pick, jnp.broadcast_to(row, (ATOMS, row.shape[1])), NT)

    w_oxygen = column(pick1, e1w_ref[0:1, :])
    w_hydrogen = column(pick1, e1w_ref[1:2, :])
    b_oxygen = column(pick1, e1b_ref[0:1, :])
    b_hydrogen = column(pick1, e1b_ref[1:2, :])
    bias2 = column(pick2, e2b_ref[...])
    bias3 = column(pick3, e3b_ref[...])
    w2 = exact(pick2, exact(pick1, e2w_ref[...]), NT)
    w3 = exact(pick3, exact(pick2, e3w_ref[...]), NT)
    w2_high, w2_low = split(w2)
    w3_high, w3_low = split(w3)
    w2_all = jnp.concatenate([w2_high, w2_high, w2_low], axis=1)
    w3_all = jnp.concatenate([w3_high, w3_high, w3_low], axis=1)
    bias2 = jnp.concatenate([bias2] * 8, axis=1)
    bias3 = jnp.concatenate([bias3] * 8, axis=1)
    sublane = iota((8, ATOMS), 0)

    def group(g, carry):
        rows = pl.ds(pl.multiple_of(g * 8, 8), 8)
        code = near_ref[rows, :]
        slot = code & 127
        offset = code >> 7
        brick = (offset * 11) >> 5
        step_y = (offset - 3 * brick - 1).astype(F32)
        parts = [jnp.zeros((8, ATOMS), F32)] * 4
        for k in range(9):
            here = brick == k
            for c in range(4):
                found = jnp.take_along_axis(table_ref[k * 4 + c], slot, axis=1)
                parts[c] = jnp.where(here, found, parts[c])
        parts[1] = parts[1] + step_y
        scaled = [(parts[c] - own_ref[c, rows, :]) * (extent[c] / 24.0) for c in range(3)]
        square = scaled[0] * scaled[0] + scaled[1] * scaled[1] + scaled[2] * scaled[2]
        smooth = 1.0 / (1.0 + square)
        kind = parts[3]
        pieces = []
        for b in range(8):
            s = jnp.broadcast_to(smooth[b : b + 1, :], (32, ATOMS))
            h = jnp.broadcast_to(kind[b : b + 1, :], (32, ATOMS)) > 0.5
            pieces.append(
                jnp.where(h, w_hydrogen, w_oxygen) * s + jnp.where(h, b_hydrogen, b_oxygen)
            )
        one = jnp.tanh(jnp.concatenate(pieces, axis=1))
        high, low = split(one)
        two = jnp.tanh(mm(w2_all, jnp.concatenate([high, low, high], axis=0)) + bias2)
        two = two + jnp.concatenate([one, one], axis=0)
        high, low = split(two)
        three = jnp.tanh(mm(w3_all, jnp.concatenate([high, low, high], axis=0)) + bias3)
        three = three + jnp.concatenate([two, two], axis=0)
        high, low = split(three)
        scale = smooth * (1.0 / 128.0)
        radial = [scale] + [scale * scaled[c] for c in range(3)]
        blocks = []
        for b in range(8):
            mine = sublane == b
            blocks.append(jnp.concatenate([jnp.where(mine, r, 0.0) for r in radial], axis=0))
        radial = jnp.concatenate(blocks, axis=1)
        r_high, r_low = split(radial)
        found = mm(r_high, high, NT) + mm(r_high, low, NT) + mm(r_low, high, NT)
        for p in range(4):
            mat_ref[p, rows, :] = found[p * 8 : (p + 1) * 8]
        return carry

    lax.fori_loop(0, ATOMS // 8, group, 0, unroll=4)

    row = iota((ATOMS, ATOMS), 0)
    lane = iota((ATOMS, ATOMS), 1)
    inner = row & 31
    kept = jnp.where(inner < 25, (row >> 5) * 25 + inner, -1)
    pick = [jnp.where(kept == (lane >> 4) + 8 * t, 1.0, 0.0).astype(BF16) for t in range(13)]
    pick.append(jnp.where(row == (lane & 15), 1.0, 0.0).astype(BF16))
    pick = jnp.concatenate(pick, axis=1)
    matrix = [mat_ref[p] for p in range(4)]
    entries = None
    for p in range(4):
        high, low = split(matrix[p])
        wide = mm(high, pick) + mm(low, pick)
        tiled = wide[:, 1664:]
        term = jnp.concatenate([wide[:, t * 128 : (t + 1) * 128] * tiled for t in range(13)], axis=1)
        entries = term if entries is None else entries + term
    arrived()
    hidden = mm3(split(entries[:, :1600]), split(f1w_ref[...]), NT)
    hidden = jnp.tanh(hidden + f1b_ref[...])
    hidden = hidden + jnp.tanh(mm3(split(hidden), split(f2w_ref[...])) + f2b_ref[...])
    hidden = hidden + jnp.tanh(mm3(split(hidden), split(f3w_ref[...])) + f3b_ref[...])
    coeffs = mm3(split(hidden), split(exact(pick3, fow_ref[...])), NT)
    result = jnp.zeros((ATOMS, ATOMS), F32)
    for c in range(3):
        total = jnp.sum(coeffs * matrix[1 + c], axis=1, keepdims=True)
        result = jnp.where(lane == c, total, result)
    return result.T[:8]


def np_split(x):
    x = np.asarray(x, np.float32)
    high = x.astype(jnp.bfloat16)
    low = (x - high.astype(np.float32)).astype(jnp.bfloat16)
    return np.stack([high, low])


@functools.lru_cache(None)
def tables():
    m = np.arange(128)[:, None]
    y = np.arange(CY)[None, :]
    angle = 2 * np.pi * (m * y % CY) / CY
    lower = -np.sin(angle)
    lower[0] = 1 - 2 * (y[0] % 2)
    dft_y = np_split(np.concatenate([np.cos(angle), lower]))
    j, k = np.divmod(np.arange(ND), NN)
    phi = 2 * np.pi * ((2 * j[:, None] * j[None] + k[:, None] * k[None]) % 16) / 16
    cos, sin = np.cos(phi), np.sin(phi)
    dft_b = np_split(np.block([[cos, sin], [-sin, cos]]))
    z, x = np.divmod(np.arange(TILE), TX)
    turn = 2 * np.pi * ((j[:, None] * (x - 1)[None] + k[:, None] * (z - 3)[None]) % 256) / 256
    twiddle = np.stack([np.cos(turn), np.sin(turn)]).astype(np.float32)
    v, u = np.divmod(np.arange(MODES), 32)
    ax = 2 * np.pi * ((np.arange(TX)[:, None] - 1) * u[None] % 32) / 32
    az = 2 * np.pi * ((np.arange(16)[:, None] - 3) * v[None] % 16) / 16
    fac_x = np.stack([np.cos(ax), np.sin(ax)]).astype(np.float32)
    fac_z = np.stack([np.cos(az), np.sin(az)]).astype(np.float32)

    def fold(i, n):
        return np.where(2 * i >= n, i - n, i) / n

    def modulus(i, n):
        return 36.0 / (4 + 2 * np.cos(2 * np.pi * i / n)) ** 2

    def decay(f):
        return np.exp(-np.pi**2 * f * f / 0.81)

    mx = j[:, None] + 8 * u[None]
    mz = k[:, None] + 16 * v[None]
    fx, fz = fold(mx, 256), fold(mz, 256)
    scale = 0.25 / (np.pi * 256.0**3)
    plane = scale * decay(fx) * decay(fz) * modulus(mx, 256) * modulus(mz, 256)
    green = np.stack([plane, fx * fx + fz * fz]).astype(np.float32)
    my = np.arange(129)
    fy = fold(my, 256)
    column = np.stack([decay(fy) * modulus(my, 256), fy * fy]).astype(np.float32)
    return dft_y, dft_b, twiddle, fac_x, fac_z, green, column


EARLY = (
    ((9, 8, ATOMS), F32),
    ((ATOMS, ATOMS), jnp.int32),
    ((2, 25), F32),
    ((2, 25), F32),
    ((25, 50), F32),
    ((1, 50), F32),
    ((50, 100), F32),
    ((1, 100), F32),
    ((1, 240), F32),
    ((1, 240), F32),
    ((1, 240), F32),
)
LATE = (
    ((240, 1600), F32),
    ((240, 240), F32),
    ((240, 240), F32),
    ((100, 240), F32),
    ((2, 256, CY), BF16),
    ((2, 256, 256), BF16),
    ((2, ND, TILE), F32),
    ((2, TX, MODES), F32),
    ((2, 16, MODES), F32),
    ((2, ND, MODES), F32),
)


def main_kernel(*refs):
    count = len(EARLY) + len(LATE)
    column_ref = refs[0]
    far = refs[1 : 1 + count]
    result_ref = refs[1 + count]
    near = refs[2 + count : 2 + 2 * count]
    (
        ghost_ref,
        near_ref,
        e1w_ref,
        e1b_ref,
        e2w_ref,
        e2b_ref,
        e3w_ref,
        e3b_ref,
        f1b_ref,
        f2b_ref,
        f3b_ref,
    ) = near[: len(EARLY)]
    (
        table_ref,
        home_ref,
        mat_ref,
        mix_ref,
        wave_ref,
        tab_ref,
        out_one,
        in_one,
        out_two,
        in_two,
        late_sem,
        send_sem,
        recv_sem,
    ) = refs[2 + 2 * count :]
    f1w_ref, f2w_ref, f3w_ref, fow_ref = near[len(EARLY) : len(EARLY) + 4]
    dft_y_ref, dft_b_ref, twiddle_ref, fac_x_ref, fac_z_ref, green_ref = near[len(EARLY) + 4 :]
    fetch = [pltpu.make_async_copy(far[i], near[i], late_sem.at[i]) for i in range(count)]
    for copy in fetch:
        copy.start()
    wide = lax.axis_index("wide")
    narrow = lax.axis_index("narrow")
    me = wide * NN + narrow
    barrier = pltpu.get_barrier_semaphore()

    def peer(d):
        at = lax.rem(me + d, ND)
        return at, (at // NN, lax.rem(at, NN))

    def greet(d, carry):
        pl.semaphore_signal(barrier, inc=1, device_id=peer(d)[1], device_id_type=MESH)
        return carry

    lax.fori_loop(1, ND, greet, 0)

    def arrived():
        for copy in fetch[len(EARLY) :]:
            copy.wait()

    for copy in fetch[: len(EARLY)]:
        copy.wait()
    dip = network(
        ghost_ref,
        near_ref,
        e1w_ref,
        e1b_ref,
        e2w_ref,
        e2b_ref,
        e3w_ref,
        e3b_ref,
        f1b_ref,
        f2b_ref,
        f3b_ref,
        f1w_ref,
        f2w_ref,
        f3w_ref,
        fow_ref,
        table_ref,
        home_ref,
        mat_ref,
        arrived,
    )

    kind = ghost_ref[4, 3:4, :]
    oxygen = 1.0 - kind
    result_ref[0:8, :] = dip * oxygen
    shift = 0.5 * jnp.tanh(dip)

    def sites(c, extent):
        atom = ghost_ref[4, c : c + 1, :] * float(extent)
        return jnp.concatenate([atom, atom + shift[c : c + 1, :]], axis=1)

    charge = jnp.concatenate([6.0 * oxygen + kind, -8.0 * oxygen], axis=1)
    off_x = sites(0, CX) - (iota((TX, 256), 0).astype(F32) - 1.0)
    off_z = sites(2, CZ) - (iota((24, 256), 0).astype(F32) - 3.0)
    off_y = sites(1, CY) - iota((CY, 256), 0).astype(F32)
    off_y = jnp.where(off_y < 0.0, off_y + float(CY), off_y)
    wx, sx = spline(off_x), slope(off_x)
    wz, sz = spline(off_z), slope(off_z)
    wave = mm3(
        (dft_y_ref[0], dft_y_ref[1]),
        split(jnp.concatenate([spline(off_y), slope(off_y)], axis=1)),
    )
    wave_ref[...] = wave
    rest = jnp.zeros((TILE - TX * TZ, 256), F32)
    for at, (left, right) in enumerate(((wz, wx), (wz, sx), (sz, wx))):
        full = jnp.concatenate([left[z : z + 1, :] * right for z in range(TZ)] + [rest], axis=0)
        high, low = split(full)
        mix_ref[0, :, at * 256 : (at + 1) * 256] = high
        mix_ref[1, :, at * 256 : (at + 1) * 256] = low
    spread = mm3(
        split(wave[:, :256] * charge), (mix_ref[0, :, :256], mix_ref[1, :, :256]), NT
    )
    for part in range(2):
        for t in range(5):
            out_one[:, part * 5 + t, :] = spread[part * 128 : (part + 1) * 128, t * 128 : (t + 1) * 128]

    pl.semaphore_wait(barrier, ND - 1)

    def exchange(out_ref, in_ref, s):
        def one(d, carry):
            at, device = peer(d)
            pltpu.make_async_remote_copy(
                src_ref=out_ref.at[at],
                dst_ref=in_ref.at[me],
                send_sem=send_sem.at[s],
                recv_sem=recv_sem.at[s],
                device_id=device,
                device_id_type=MESH,
            ).start()
            return carry

        lax.fori_loop(1, ND, one, 0)
        in_ref[me] = out_ref[me]

    def settle(out_ref, in_ref, s):
        whole = pltpu.make_async_remote_copy(
            src_ref=out_ref.at[pl.ds(0, ND - 1)],
            dst_ref=in_ref.at[pl.ds(0, ND - 1)],
            send_sem=send_sem.at[s],
            recv_sem=recv_sem.at[s],
            device_id=peer(1)[1],
            device_id_type=MESH,
        )
        whole.wait_send()
        whole.wait_recv()

    exchange(out_one, in_one, 0)

    def build(z, carry):
        cz = fac_z_ref[0, pl.ds(z, 1), :]
        zz = fac_z_ref[1, pl.ds(z, 1), :]
        cx, xx = fac_x_ref[0], fac_x_ref[1]
        rows = pl.ds(pl.multiple_of(z * TX, 8), TX)
        tab_ref[0, rows, :] = cx * cz - xx * zz
        tab_ref[1, rows, :] = xx * cz + cx * zz
        return carry

    lax.fori_loop(0, 16, build, 0)
    cos_e = split(tab_ref[0])
    sin_e = split(tab_ref[1])

    settle(out_one, in_one, 0)

    def gathered(in_ref):
        return jnp.concatenate(
            [
                jnp.concatenate([in_ref[:, part * 5 + t, :] for t in range(5)], axis=1)
                for part in range(2)
            ],
            axis=0,
        )

    tiles = gathered(in_one)
    bricks = mm3((dft_b_ref[0], dft_b_ref[1]), split(tiles))
    real, imag = bricks[:128], bricks[128:]
    cos_t, sin_t = twiddle_ref[0], twiddle_ref[1]
    turned = jnp.concatenate(
        [real * cos_t + imag * sin_t, imag * cos_t - real * sin_t], axis=0
    )
    turned = jnp.concatenate(
        [turned[:, :128] + turned[:, FOLD:], turned[:, 128:FOLD]], axis=1
    )
    turned = split(turned)
    by_cos = mm3(turned, cos_e)
    by_sin = mm3(turned, sin_e)
    real = by_cos[:128] + by_sin[128:]
    imag = by_cos[128:] - by_sin[:128]

    def influence(at, weight):
        total = green_ref[1] + column_ref[1, at]
        inverse = jnp.where(total == 0.0, 0.0, 1.0 / jnp.where(total == 0.0, 1.0, total))
        return green_ref[0] * (inverse * (column_ref[0, at] * weight))

    first = me == 0
    weight = jnp.where(first, 1.0, 2.0)
    green_a = influence(me, weight)
    green_b = influence(jnp.where(first, 128, me), weight)
    modes = split(
        jnp.concatenate(
            [green_a * real, green_a * imag, green_b * real, green_b * imag], axis=0
        )
    )
    by_cos = mm3(modes, cos_e, NT)
    by_sin = mm3(modes, sin_e, NT)

    def widen(x):
        return jnp.concatenate([x, x[:, :128]], axis=1)

    def back(at):
        real = widen(by_cos[at : at + 128] - by_sin[at + 128 : at + 256])
        imag = widen(by_sin[at : at + 128] + by_cos[at + 128 : at + 256])
        return real * cos_t - imag * sin_t, imag * cos_t + real * sin_t

    real_a, imag_a = back(0)
    real_b, imag_b = back(256)
    field_r = mm3(
        (dft_b_ref[0, :128], dft_b_ref[1, :128]),
        split(jnp.concatenate([real_a, -imag_a], axis=0)),
    )
    field_i = mm3(
        (dft_b_ref[0, 128:], dft_b_ref[1, 128:]),
        split(jnp.concatenate([-real_b, imag_b], axis=0)),
    )
    partial = jnp.sum(tiles[:128] * field_r + tiles[128:] * field_i, keepdims=True)
    partial = partial * (0.5 / (ND * ATOMS))
    lane = iota((ND, 128), 1)
    for t in range(5):
        piece = field_r[:, t * 128 : (t + 1) * 128]
        if t == 4:
            piece = jnp.where(lane == 127, partial, piece)
        out_two[:, t, :] = piece
        out_two[:, 5 + t, :] = field_i[:, t * 128 : (t + 1) * 128]

    def place(c, i):
        step = c * 2 + i // NN
        w = lax.rem(wide + step, NW)
        n = lax.rem(narrow + lax.rem(i, NN), NN)
        return w * NN + n, (w, n)

    for c in range(4):

        def one(i, carry):
            at, device = place(c, i)
            pltpu.make_async_remote_copy(
                src_ref=out_two.at[at],
                dst_ref=in_two.at[me],
                send_sem=send_sem.at[1],
                recv_sem=recv_sem.at[1 + c],
                device_id=device,
                device_id_type=MESH,
            ).start()
            return carry

        lax.fori_loop(1 if c == 0 else 0, 32, one, 0)
    in_two[me] = out_two[me]
    mix = (mix_ref[0], mix_ref[1])
    rows = [jnp.zeros((1, 256), F32)] * 4
    total = jnp.zeros((1, 1), F32)
    for c in range(4):
        size = 31 if c == 0 else 32
        pltpu.make_async_remote_copy(
            src_ref=out_two.at[pl.ds(0, size)],
            dst_ref=in_two.at[pl.ds(0, size)],
            send_sem=send_sem.at[1],
            recv_sem=recv_sem.at[1 + c],
            device_id=peer(1)[1],
            device_id_type=MESH,
        ).wait_recv()
        spans = [lax.rem(wide + (NW - 2 * c - i), NW) * NN for i in range(2)]
        spans = [pl.ds(pl.multiple_of(at, NN), NN) for at in spans]
        lower = [pl.ds(pl.multiple_of(at.start + ND, NN), NN) for at in spans]
        planes = jnp.concatenate(
            [
                jnp.concatenate([in_two[at, part * 5 + t, :] for t in range(5)], axis=1)
                for part in range(2)
                for at in spans
            ],
            axis=0,
        )
        inner = mm3(split(planes), mix)
        wave = jnp.concatenate([wave_ref[at, :] for at in spans + lower], axis=0)
        wave, wave_slope = wave[:, :256], wave[:, 256:]
        parts = [
            wave * inner[:, :256],
            -wave * inner[:, 256:512],
            -wave_slope * inner[:, :256],
            -wave * inner[:, 512:],
        ]
        rows = [r + jnp.sum(p, axis=0, keepdims=True) for r, p in zip(rows, parts)]
        total = total + jnp.sum(planes[:32, TILE - 1 : TILE], axis=0, keepdims=True)
    pltpu.make_async_remote_copy(
        src_ref=out_two.at[pl.ds(0, ND - 1)],
        dst_ref=in_two.at[pl.ds(0, ND - 1)],
        send_sem=send_sem.at[1],
        recv_sem=recv_sem.at[1],
        device_id=peer(1)[1],
        device_id_type=MESH,
    ).wait_send()
    atom = [r[:, :128] for r in rows]
    centroid = [r[:, 128:] * oxygen for r in rows]
    result_ref[8:24, :] = jnp.concatenate(
        atom + centroid + [jnp.broadcast_to(total, (8, ATOMS))], axis=0
    )


def deal_kernel(result_ref, dipole_ref, atom_ref, centroid_ref, energy_ref):
    for c in range(3):
        dipole_ref[c, 0, 0] = result_ref[c : c + 1, :]
    for c in range(4):
        atom_ref[c, 0, 0] = result_ref[8 + c : 9 + c, :]
        centroid_ref[c, 0, 0] = result_ref[12 + c : 13 + c, :]
    energy_ref[...] = result_ref[16:17, 0:1]


def local(
    positions,
    species,
    neighbours,
    e1w,
    e1b,
    e2w,
    e2b,
    e3w,
    e3b,
    f1w,
    f1b,
    f2w,
    f2b,
    f3w,
    f3b,
    fow,
):
    ghosts = halo(positions, species)
    *late, column = [jnp.asarray(t) for t in tables()]
    vmem = pl.BlockSpec(memory_space=pltpu.VMEM)
    anywhere = pl.BlockSpec(memory_space=pl.ANY)
    row = lambda x: x.reshape(1, -1)
    result = pl.pallas_call(
        main_kernel,
        out_shape=jax.ShapeDtypeStruct((24, ATOMS), F32),
        in_specs=[pl.BlockSpec(memory_space=pltpu.SMEM)] + [anywhere] * (len(EARLY) + len(LATE)),
        out_specs=vmem,
        scratch_shapes=[pltpu.VMEM(shape, dtype) for shape, dtype in EARLY + LATE]
        + [
            pltpu.VMEM((36, 8, ATOMS), F32),
            pltpu.VMEM((3, ATOMS, ATOMS), F32),
            pltpu.VMEM((4, ATOMS, ATOMS), F32),
            pltpu.VMEM((2, TILE, 768), BF16),
            pltpu.VMEM((CY, 512), F32),
            pltpu.VMEM((2, FOLD, MODES), F32),
            pltpu.VMEM((ND, ROWS, 128), F32),
            pltpu.VMEM((ND, ROWS, 128), F32),
            pltpu.VMEM((ND, ROWS, 128), F32),
            pltpu.VMEM((ND, ROWS, 128), F32),
            pltpu.SemaphoreType.DMA((len(EARLY) + len(LATE),)),
            pltpu.SemaphoreType.DMA((2,)),
            pltpu.SemaphoreType.DMA((5,)),
        ],
        compiler_params=pltpu.CompilerParams(
            collective_id=1, has_side_effects=True, vmem_limit_bytes=58 << 20
        ),
        name="main",
    )(
        column,
        ghosts,
        neighbours.reshape(ATOMS, ATOMS),
        e1w,
        e1b,
        e2w,
        row(e2b),
        e3w,
        row(e3b),
        row(f1b),
        row(f2b),
        row(f3b),
        f1w.T,
        f2w,
        f3w,
        fow.T,
        *late,
    )
    dipole, atom, centroid, energy = pl.pallas_call(
        deal_kernel,
        out_shape=(
            jax.ShapeDtypeStruct((3, 1, 1, 1, ATOMS), F32),
            jax.ShapeDtypeStruct((4, 1, 1, 1, ATOMS), F32),
            jax.ShapeDtypeStruct((4, 1, 1, 1, ATOMS), F32),
            jax.ShapeDtypeStruct((1, 1), F32),
        ),
        in_specs=[vmem],
        out_specs=(vmem,) * 4,
        name="deal",
    )(result)
    return dipole, atom, centroid, energy.reshape(())


def solution(mesh):
    return jax.shard_map(
        local,
        mesh=mesh,
        in_specs=(
            P(None, "wide", "narrow", None, None),
            P("wide", "narrow", None, None),
            P("wide", "narrow", None, None, None),
        )
        + (P(),) * 13,
        out_specs=(
            P(None, "wide", "narrow", None, None),
            P(None, "wide", "narrow", None, None),
            P(None, "wide", "narrow", None, None),
            P(),
        ),
        check_vma=False,
    )
```

```python
import functools
import math

import jax
import jax.numpy as jnp
import numpy as np
from jax import lax
from jax.experimental import pallas as pl
from jax.experimental.pallas import tpu as pltpu
from jax.sharding import PartitionSpec as P

NW, NN = 8, 16
ND = NW * NN
CX, CY, CZ = 32, 256, 16
TX, TZ = 32, 19
TILE = 640
FOLD = 512
ROWS = 10
WIDTH = 8
MODES = 512
ATOMS = 128
F32 = jnp.float32
BF16 = jnp.bfloat16
MESH = pl.DeviceIdType.MESH
HIGHEST = lax.Precision.HIGHEST
NT = (((1,), (1,)), ((), ()))
NNN = (((1,), (0,)), ((), ()))


def split(x):
    high = x.astype(BF16)
    return high, (x - high.astype(F32)).astype(BF16)


def mm(a, b, dims=NNN):
    return lax.dot_general(a, b, dims, preferred_element_type=F32)


def mm3(a, b, dims=NNN):
    return mm(a[0], b[0], dims) + mm(a[0], b[1], dims) + mm(a[1], b[0], dims)


def exact(a, b, dims=NNN):
    return lax.dot_general(a, b, dims, precision=HIGHEST, preferred_element_type=F32)


def iota(shape, dim):
    return lax.broadcasted_iota(jnp.int32, shape, dim)


def spline(offset):
    from_middle = offset - 2.0
    away = jnp.abs(from_middle)
    outer = jnp.maximum(2.0 - away, 0.0)
    inner = jnp.maximum(1.0 - away, 0.0)
    outer_square, inner_square = outer * outer, inner * inner
    value = (outer_square * outer - 4.0 * (inner_square * inner)) * (1.0 / 6.0)
    fall = 0.5 * outer_square - 2.0 * inner_square
    return value, jnp.where(from_middle > 0.0, -fall, fall)


def halo_kernel(positions_ref, species_ref, ghost_ref, own_ref, send_sem, recv_sem):
    wide = lax.axis_index("wide")
    narrow = lax.axis_index("narrow")
    steps = [(sx, sz) for sx in range(3) for sz in range(3) if (sx, sz) != (1, 1)]
    barrier = pltpu.get_barrier_semaphore()

    def device(sx, sz):
        return (lax.rem(wide + (NW + 1 - sx), NW), lax.rem(narrow + (NN + 1 - sz), NN))

    own_ref[...] = jnp.concatenate(
        [positions_ref[c, 0, 0] for c in range(3)]
        + [species_ref[0, 0].astype(F32), jnp.zeros((4, ATOMS), F32)],
        axis=0,
    )
    ghost_ref[4] = own_ref[...]
    for sx, sz in steps:
        pl.semaphore_signal(barrier, inc=1, device_id=device(sx, sz), device_id_type=MESH)
    pl.semaphore_wait(barrier, len(steps))
    copies = []
    for at, (sx, sz) in enumerate(steps):
        copy = pltpu.make_async_remote_copy(
            src_ref=own_ref,
            dst_ref=ghost_ref.at[sx * 3 + sz],
            send_sem=send_sem.at[at],
            recv_sem=recv_sem.at[at],
            device_id=device(sx, sz),
            device_id_type=MESH,
        )
        copy.start()
        copies.append(copy)
    for copy in copies:
        copy.wait()


def halo(positions, species):
    vmem = pl.BlockSpec(memory_space=pltpu.VMEM)
    return pl.pallas_call(
        halo_kernel,
        out_shape=jax.ShapeDtypeStruct((9, 8, ATOMS), F32),
        in_specs=[vmem, vmem],
        out_specs=vmem,
        scratch_shapes=[
            pltpu.VMEM((8, ATOMS), F32),
            pltpu.SemaphoreType.DMA((8,)),
            pltpu.SemaphoreType.DMA((8,)),
        ],
        compiler_params=pltpu.CompilerParams(collective_id=0, has_side_effects=True),
        name="halo",
    )(positions, species)


def spread_rows(rows, count):
    r = iota((rows, count), 0)
    c = iota((rows, count), 1)
    i = r & 31
    return jnp.where((i < 25) & (c == (r >> 5) * 25 + i), 1.0, 0.0).astype(F32)


def network(
    ghost_ref,
    near_ref,
    e1w_ref,
    e1b_ref,
    e2w_ref,
    e2b_ref,
    e3w_ref,
    e3b_ref,
    f1b_ref,
    f2b_ref,
    f3b_ref,
    f1w_ref,
    f2w_ref,
    f3w_ref,
    fow_ref,
    table_ref,
    own_ref,
    mat_ref,
    arrived,
):
    extent = (float(CX), float(CY), float(CZ))
    for k in range(9):
        shift = (float(k // 3 - 1), 0.0, float(k % 3 - 1))
        for c in range(3):
            table_ref[k * 4 + c] = jnp.broadcast_to(ghost_ref[k, c : c + 1, :] + shift[c], (8, ATOMS))
        table_ref[k * 4 + 3] = jnp.broadcast_to(ghost_ref[k, 3:4, :], (8, ATOMS))
    for c in range(3):
        own_ref[c] = jnp.broadcast_to(ghost_ref[4, c : c + 1, :], (ATOMS, ATOMS)).T

    pick1 = spread_rows(32, 25)
    pick2 = spread_rows(64, 50)
    pick3 = spread_rows(128, 100)

    def column(pick, row):
        return exact(pick, jnp.broadcast_to(row, (ATOMS, row.shape[1])), NT)

    w_oxygen = column(pick1, e1w_ref[0:1, :])
    w_hydrogen = column(pick1, e1w_ref[1:2, :])
    b_oxygen = column(pick1, e1b_ref[0:1, :])
    b_hydrogen = column(pick1, e1b_ref[1:2, :])
    bias2 = column(pick2, e2b_ref[...])
    bias3 = column(pick3, e3b_ref[...])
    w2 = exact(pick2, exact(pick1, e2w_ref[...]), NT)
    w3 = exact(pick3, exact(pick2, e3w_ref[...]), NT)
    last = iota((32, ATOMS), 0) == 31
    b_oxygen = jnp.where(last, 20.0, b_oxygen)
    b_hydrogen = jnp.where(last, 20.0, b_hydrogen)
    w2 = jnp.where(iota((64, 32), 1) == 31, bias2[:, :32], w2)
    w3 = jnp.where(iota((128, 64), 1) == 31, bias3[:, :64], w3)
    w2_high, w2_low = split(w2)
    w3_high, w3_low = split(w3)
    w2_all = jnp.concatenate([w2_high, w2_high, w2_low], axis=1)
    w3_all = jnp.concatenate([w3_high, w3_high, w3_low], axis=1)
    sublane = iota((8, ATOMS), 0)

    def group(g, carry):
        rows = pl.ds(pl.multiple_of(g * 8, 8), 8)
        code = near_ref[rows, :]
        slot = code & 127
        offset = code >> 7
        brick = (offset * 11) >> 5
        step_y = (offset - 3 * brick - 1).astype(F32)
        parts = [jnp.zeros((8, ATOMS), F32)] * 4
        for k in range(9):
            here = brick == k
            for c in range(4):
                found = jnp.take_along_axis(table_ref[k * 4 + c], slot, axis=1)
                parts[c] = jnp.where(here, found, parts[c])
        parts[1] = parts[1] + step_y
        scaled = [(parts[c] - own_ref[c, rows, :]) * (extent[c] / 24.0) for c in range(3)]
        square = scaled[0] * scaled[0] + scaled[1] * scaled[1] + scaled[2] * scaled[2]
        smooth = 1.0 / (1.0 + square)
        kind = parts[3]
        scale = smooth * (1.0 / 128.0)
        radial = [scale] + [scale * scaled[c] for c in range(3)]
        found = jnp.zeros((32, ATOMS), F32)
        for pair in range(8 // WIDTH):
            pieces, blocks = [], []
            for b in range(WIDTH * pair, WIDTH * pair + WIDTH):
                s = jnp.broadcast_to(smooth[b : b + 1, :], (32, ATOMS))
                h = jnp.broadcast_to(kind[b : b + 1, :], (32, ATOMS)) > 0.5
                pieces.append(
                    jnp.where(h, w_hydrogen, w_oxygen) * s + jnp.where(h, b_hydrogen, b_oxygen)
                )
                blocks.append(
                    jnp.concatenate([jnp.where(sublane == b, r, 0.0) for r in radial], axis=0)
                )
            one = jnp.tanh(jnp.concatenate(pieces, axis=1))
            high, low = split(one)
            two = jnp.tanh(mm(w2_all, jnp.concatenate([high, low, high], axis=0)))
            two = two + jnp.concatenate([one, one], axis=0)
            high, low = split(two)
            three = jnp.tanh(mm(w3_all, jnp.concatenate([high, low, high], axis=0)))
            three = three + jnp.concatenate([two, two], axis=0)
            high, low = split(three)
            r_high, r_low = split(jnp.concatenate(blocks, axis=1))
            both = mm(jnp.concatenate([r_high, r_low], axis=0), high, NT)
            found = found + (both[:32] + both[32:]) + mm(r_high, low, NT)
        for p in range(4):
            mat_ref[p, rows, :] = found[p * 8 : (p + 1) * 8]
        return carry

    lax.fori_loop(0, ATOMS // 8, group, 0, unroll=4)

    lane = iota((ATOMS, ATOMS), 1)
    entries = None
    matrix = [mat_ref[p] for p in range(4)]
    for p in range(4):
        tiled = jnp.take_along_axis(matrix[p], lane & 15, axis=1)
        term = []
        for t in range(13):
            d = jnp.minimum((lane >> 4) + 8 * t, 99)
            block = (d * 41) >> 10
            term.append(jnp.take_along_axis(matrix[p], d + 7 * block, axis=1) * tiled)
        term = jnp.concatenate(term, axis=1)
        entries = term if entries is None else entries + term
    arrived()
    hidden = mm3(split(entries[:, :1600]), split(f1w_ref[...]), NT)
    hidden = jnp.tanh(hidden + f1b_ref[...])
    hidden = hidden + jnp.tanh(mm3(split(hidden), split(f2w_ref[...])) + f2b_ref[...])
    hidden = hidden + jnp.tanh(mm3(split(hidden), split(f3w_ref[...])) + f3b_ref[...])
    coeffs = mm3(split(hidden), split(exact(pick3, fow_ref[...])), NT)
    result = jnp.zeros((ATOMS, ATOMS), F32)
    for c in range(3):
        total = jnp.sum(coeffs * matrix[1 + c], axis=1, keepdims=True)
        result = jnp.where(lane == c, total, result)
    return result.T[:8]


def np_split(x):
    x = np.asarray(x, np.float32)
    high = x.astype(jnp.bfloat16)
    low = (x - high.astype(np.float32)).astype(jnp.bfloat16)
    return np.stack([high, low])


@functools.lru_cache(None)
def tables():
    m = np.arange(128)[:, None]
    y = np.arange(CY)[None, :]
    angle = 2 * np.pi * (m * y % CY) / CY
    lower = -np.sin(angle)
    lower[0] = 1 - 2 * (y[0] % 2)
    dft_y = np_split(np.concatenate([np.cos(angle), lower]))
    j, k = np.divmod(np.arange(ND), NN)
    phi = 2 * np.pi * ((2 * j[:, None] * j[None] + k[:, None] * k[None]) % 16) / 16
    cos, sin = np.cos(phi), np.sin(phi)
    dft_b = np_split(np.block([[cos, sin], [-sin, cos]]))
    z, x = np.divmod(np.arange(TILE), TX)
    turn = 2 * np.pi * ((j[:, None] * (x - 1)[None] + k[:, None] * (z - 3)[None]) % 256) / 256
    twiddle = np.stack([np.cos(turn), np.sin(turn)]).astype(np.float32)
    v, u = np.divmod(np.arange(MODES), 32)
    ax = 2 * np.pi * ((np.arange(TX)[:, None] - 1) * u[None] % 32) / 32
    az = 2 * np.pi * ((np.arange(16)[:, None] - 3) * v[None] % 16) / 16
    fac_x = np.stack([np.cos(ax), np.sin(ax)]).astype(np.float32)
    fac_z = np.stack([np.cos(az), np.sin(az)]).astype(np.float32)

    def fold(i, n):
        return np.where(2 * i >= n, i - n, i) / n

    def modulus(i, n):
        return 36.0 / (4 + 2 * np.cos(2 * np.pi * i / n)) ** 2

    def decay(f):
        return np.exp(-np.pi**2 * f * f / 0.81)

    mx = j[:, None] + 8 * u[None]
    mz = k[:, None] + 16 * v[None]
    fx, fz = fold(mx, 256), fold(mz, 256)
    scale = 0.25 / (np.pi * 256.0**3)
    plane = scale * decay(fx) * decay(fz) * modulus(mx, 256) * modulus(mz, 256)
    green = np.stack([plane, fx * fx + fz * fz]).astype(np.float32)
    my = np.arange(129)
    fy = fold(my, 256)
    column = np.stack([decay(fy) * modulus(my, 256), fy * fy]).astype(np.float32)
    return dft_y, dft_b, twiddle, fac_x, fac_z, green, column


EARLY = (
    ((9, 8, ATOMS), F32),
    ((ATOMS, ATOMS), jnp.int32),
    ((2, 25), F32),
    ((2, 25), F32),
    ((25, 50), F32),
    ((1, 50), F32),
    ((50, 100), F32),
    ((1, 100), F32),
    ((1, 240), F32),
    ((1, 240), F32),
    ((1, 240), F32),
)
LATE = (
    ((240, 1600), F32),
    ((240, 240), F32),
    ((240, 240), F32),
    ((100, 240), F32),
    ((2, 256, CY), BF16),
    ((2, 256, 256), BF16),
    ((2, ND, TILE), F32),
    ((2, TX, MODES), F32),
    ((2, 16, MODES), F32),
    ((2, ND, MODES), F32),
)


def main_kernel(*refs):
    count = len(EARLY) + len(LATE)
    column_ref = refs[0]
    far = refs[1 : 1 + count]
    result_ref = refs[1 + count]
    near = refs[2 + count : 2 + 2 * count]
    (
        ghost_ref,
        near_ref,
        e1w_ref,
        e1b_ref,
        e2w_ref,
        e2b_ref,
        e3w_ref,
        e3b_ref,
        f1b_ref,
        f2b_ref,
        f3b_ref,
    ) = near[: len(EARLY)]
    (
        table_ref,
        home_ref,
        mat_ref,
        mix_ref,
        wave_ref,
        tab_ref,
        out_one,
        in_one,
        out_two,
        in_two,
        late_sem,
        send_sem,
        recv_sem,
    ) = refs[2 + 2 * count :]
    f1w_ref, f2w_ref, f3w_ref, fow_ref = near[len(EARLY) : len(EARLY) + 4]
    dft_y_ref, dft_b_ref, twiddle_ref, fac_x_ref, fac_z_ref, green_ref = near[len(EARLY) + 4 :]
    fetch = [pltpu.make_async_copy(far[i], near[i], late_sem.at[i]) for i in range(count)]
    for copy in fetch:
        copy.start()
    wide = lax.axis_index("wide")
    narrow = lax.axis_index("narrow")
    me = wide * NN + narrow
    barrier = pltpu.get_barrier_semaphore()

    def peer(d):
        at = lax.rem(me + d, ND)
        return at, (at // NN, lax.rem(at, NN))

    def greet(d, carry):
        pl.semaphore_signal(barrier, inc=1, device_id=peer(d)[1], device_id_type=MESH)
        return carry

    lax.fori_loop(1, ND, greet, 0)

    def arrived():
        for copy in fetch[len(EARLY) :]:
            copy.wait()

    for copy in fetch[: len(EARLY)]:
        copy.wait()
    dip = network(
        ghost_ref,
        near_ref,
        e1w_ref,
        e1b_ref,
        e2w_ref,
        e2b_ref,
        e3w_ref,
        e3b_ref,
        f1b_ref,
        f2b_ref,
        f3b_ref,
        f1w_ref,
        f2w_ref,
        f3w_ref,
        fow_ref,
        table_ref,
        home_ref,
        mat_ref,
        arrived,
    )

    kind = ghost_ref[4, 3:4, :]
    oxygen = 1.0 - kind
    result_ref[0:8, :] = dip * oxygen
    shift = 0.5 * jnp.tanh(dip)

    def sites(c, extent):
        atom = ghost_ref[4, c : c + 1, :] * float(extent)
        return jnp.concatenate([atom, atom + shift[c : c + 1, :]], axis=1)

    charge = jnp.concatenate([6.0 * oxygen + kind, -8.0 * oxygen], axis=1)
    off_x = sites(0, CX) - (iota((TX, 256), 0).astype(F32) - 1.0)
    off_z = sites(2, CZ) - (iota((24, 256), 0).astype(F32) - 3.0)
    off_y = sites(1, CY) - iota((CY, 256), 0).astype(F32)
    wx, sx = spline(off_x)
    wz, sz = spline(off_z)
    wave = mm3(
        (dft_y_ref[0], dft_y_ref[1]),
        split(jnp.concatenate(spline(off_y), axis=1)),
    )
    wave_ref[...] = wave
    rest = jnp.zeros((TILE - TX * TZ, 256), F32)
    for at, (left, right) in enumerate(((wz, wx), (wz, sx), (sz, wx))):
        full = jnp.concatenate([left[z : z + 1, :] * right for z in range(TZ)] + [rest], axis=0)
        high, low = split(full)
        mix_ref[0, :, at * 256 : (at + 1) * 256] = high
        mix_ref[1, :, at * 256 : (at + 1) * 256] = low
    spread = mm3(
        split(wave[:, :256] * charge), (mix_ref[0, :, :256], mix_ref[1, :, :256]), NT
    )
    for part in range(2):
        for t in range(5):
            out_one[:, part * 5 + t, :] = spread[part * 128 : (part + 1) * 128, t * 128 : (t + 1) * 128]

    pl.semaphore_wait(barrier, ND - 1)

    def exchange(out_ref, in_ref, s):
        def one(d, carry):
            at, device = peer(d)
            pltpu.make_async_remote_copy(
                src_ref=out_ref.at[at],
                dst_ref=in_ref.at[me],
                send_sem=send_sem.at[s],
                recv_sem=recv_sem.at[s],
                device_id=device,
                device_id_type=MESH,
            ).start()
            return carry

        lax.fori_loop(1, ND, one, 0)
        in_ref[me] = out_ref[me]

    def settle(out_ref, in_ref, s):
        whole = pltpu.make_async_remote_copy(
            src_ref=out_ref.at[pl.ds(0, ND - 1)],
            dst_ref=in_ref.at[pl.ds(0, ND - 1)],
            send_sem=send_sem.at[s],
            recv_sem=recv_sem.at[s],
            device_id=peer(1)[1],
            device_id_type=MESH,
        )
        whole.wait_send()
        whole.wait_recv()

    exchange(out_one, in_one, 0)

    def build(z, carry):
        cz = fac_z_ref[0, pl.ds(z, 1), :]
        zz = fac_z_ref[1, pl.ds(z, 1), :]
        cx, xx = fac_x_ref[0], fac_x_ref[1]
        rows = pl.ds(pl.multiple_of(z * TX, 8), TX)
        tab_ref[0, rows, :] = cx * cz - xx * zz
        tab_ref[1, rows, :] = xx * cz + cx * zz
        return carry

    lax.fori_loop(0, 16, build, 0)
    cos_e = split(tab_ref[0])
    sin_e = split(tab_ref[1])

    settle(out_one, in_one, 0)

    def gathered(in_ref):
        return jnp.concatenate(
            [
                jnp.concatenate([in_ref[:, part * 5 + t, :] for t in range(5)], axis=1)
                for part in range(2)
            ],
            axis=0,
        )

    tiles = gathered(in_one)
    bricks = mm3((dft_b_ref[0], dft_b_ref[1]), split(tiles))
    real, imag = bricks[:128], bricks[128:]
    cos_t, sin_t = twiddle_ref[0], twiddle_ref[1]
    turned = jnp.concatenate(
        [real * cos_t + imag * sin_t, imag * cos_t - real * sin_t], axis=0
    )
    turned = jnp.concatenate(
        [turned[:, :128] + turned[:, FOLD:], turned[:, 128:FOLD]], axis=1
    )
    turned = split(turned)
    by_cos = mm3(turned, cos_e)
    by_sin = mm3(turned, sin_e)
    real = by_cos[:128] + by_sin[128:]
    imag = by_cos[128:] - by_sin[:128]

    def influence(at, weight):
        total = green_ref[1] + column_ref[1, at]
        inverse = jnp.where(total == 0.0, 0.0, 1.0 / jnp.where(total == 0.0, 1.0, total))
        return green_ref[0] * (inverse * (column_ref[0, at] * weight))

    first = me == 0
    weight = jnp.where(first, 1.0, 2.0)
    green_a = influence(me, weight)
    green_b = influence(jnp.where(first, 128, me), weight)
    modes = split(
        jnp.concatenate(
            [green_a * real, green_a * imag, green_b * real, green_b * imag], axis=0
        )
    )
    by_cos = mm3(modes, cos_e, NT)
    by_sin = mm3(modes, sin_e, NT)

    def widen(x):
        return jnp.concatenate([x, x[:, :128]], axis=1)

    def back(at):
        real = widen(by_cos[at : at + 128] - by_sin[at + 128 : at + 256])
        imag = widen(by_sin[at : at + 128] + by_cos[at + 128 : at + 256])
        return real * cos_t - imag * sin_t, imag * cos_t + real * sin_t

    real_a, imag_a = back(0)
    real_b, imag_b = back(256)
    field_r = mm3(
        (dft_b_ref[0, :128], dft_b_ref[1, :128]),
        split(jnp.concatenate([real_a, -imag_a], axis=0)),
    )
    field_i = mm3(
        (dft_b_ref[0, 128:], dft_b_ref[1, 128:]),
        split(jnp.concatenate([-real_b, imag_b], axis=0)),
    )
    partial = jnp.sum(tiles[:128] * field_r + tiles[128:] * field_i, keepdims=True)
    partial = partial * (0.5 / (ND * ATOMS))
    lane = iota((ND, 128), 1)
    for t in range(5):
        piece = field_r[:, t * 128 : (t + 1) * 128]
        if t == 4:
            piece = jnp.where(lane == 127, partial, piece)
        out_two[:, t, :] = piece
        out_two[:, 5 + t, :] = field_i[:, t * 128 : (t + 1) * 128]

    def place(c, i):
        step = c * 2 + i // NN
        w = lax.rem(wide + step, NW)
        n = lax.rem(narrow + lax.rem(i, NN), NN)
        return w * NN + n, (w, n)

    for c in range(4):

        def one(i, carry):
            at, device = place(c, i)
            pltpu.make_async_remote_copy(
                src_ref=out_two.at[at],
                dst_ref=in_two.at[me],
                send_sem=send_sem.at[1],
                recv_sem=recv_sem.at[1 + c],
                device_id=device,
                device_id_type=MESH,
            ).start()
            return carry

        lax.fori_loop(1 if c == 0 else 0, 32, one, 0)
    in_two[me] = out_two[me]
    mix = (mix_ref[0], mix_ref[1])
    rows = [jnp.zeros((1, 256), F32)] * 4
    total = jnp.zeros((1, 1), F32)
    for c in range(4):
        size = 31 if c == 0 else 32
        pltpu.make_async_remote_copy(
            src_ref=out_two.at[pl.ds(0, size)],
            dst_ref=in_two.at[pl.ds(0, size)],
            send_sem=send_sem.at[1],
            recv_sem=recv_sem.at[1 + c],
            device_id=peer(1)[1],
            device_id_type=MESH,
        ).wait_recv()
        spans = [lax.rem(wide + (NW - 2 * c - i), NW) * NN for i in range(2)]
        spans = [pl.ds(pl.multiple_of(at, NN), NN) for at in spans]
        lower = [pl.ds(pl.multiple_of(at.start + ND, NN), NN) for at in spans]
        planes = jnp.concatenate(
            [
                jnp.concatenate([in_two[at, part * 5 + t, :] for t in range(5)], axis=1)
                for part in range(2)
                for at in spans
            ],
            axis=0,
        )
        inner = mm3(split(planes), mix)
        wave = jnp.concatenate([wave_ref[at, :] for at in spans + lower], axis=0)
        wave, wave_slope = wave[:, :256], wave[:, 256:]
        parts = [
            wave * inner[:, :256],
            -wave * inner[:, 256:512],
            -wave_slope * inner[:, :256],
            -wave * inner[:, 512:],
        ]
        rows = [r + jnp.sum(p, axis=0, keepdims=True) for r, p in zip(rows, parts)]
        total = total + jnp.sum(planes[:32, TILE - 1 : TILE], axis=0, keepdims=True)
    pltpu.make_async_remote_copy(
        src_ref=out_two.at[pl.ds(0, ND - 1)],
        dst_ref=in_two.at[pl.ds(0, ND - 1)],
        send_sem=send_sem.at[1],
        recv_sem=recv_sem.at[1],
        device_id=peer(1)[1],
        device_id_type=MESH,
    ).wait_send()
    atom = [r[:, :128] for r in rows]
    centroid = [r[:, 128:] * oxygen for r in rows]
    result_ref[8:24, :] = jnp.concatenate(
        atom + centroid + [jnp.broadcast_to(total, (8, ATOMS))], axis=0
    )


def deal_kernel(result_ref, dipole_ref, atom_ref, centroid_ref, energy_ref):
    for c in range(3):
        dipole_ref[c, 0, 0] = result_ref[c : c + 1, :]
    for c in range(4):
        atom_ref[c, 0, 0] = result_ref[8 + c : 9 + c, :]
        centroid_ref[c, 0, 0] = result_ref[12 + c : 13 + c, :]
    energy_ref[...] = result_ref[16:17, 0:1]


def local(
    positions,
    species,
    neighbours,
    e1w,
    e1b,
    e2w,
    e2b,
    e3w,
    e3b,
    f1w,
    f1b,
    f2w,
    f2b,
    f3w,
    f3b,
    fow,
):
    ghosts = halo(positions, species)
    *late, column = [jnp.asarray(t) for t in tables()]
    vmem = pl.BlockSpec(memory_space=pltpu.VMEM)
    anywhere = pl.BlockSpec(memory_space=pl.ANY)
    row = lambda x: x.reshape(1, -1)
    result = pl.pallas_call(
        main_kernel,
        out_shape=jax.ShapeDtypeStruct((24, ATOMS), F32),
        in_specs=[pl.BlockSpec(memory_space=pltpu.SMEM)] + [anywhere] * (len(EARLY) + len(LATE)),
        out_specs=vmem,
        scratch_shapes=[pltpu.VMEM(shape, dtype) for shape, dtype in EARLY + LATE]
        + [
            pltpu.VMEM((36, 8, ATOMS), F32),
            pltpu.VMEM((3, ATOMS, ATOMS), F32),
            pltpu.VMEM((4, ATOMS, ATOMS), F32),
            pltpu.VMEM((2, TILE, 768), BF16),
            pltpu.VMEM((CY, 512), F32),
            pltpu.VMEM((2, FOLD, MODES), F32),
            pltpu.VMEM((ND, ROWS, 128), F32),
            pltpu.VMEM((ND, ROWS, 128), F32),
            pltpu.VMEM((ND, ROWS, 128), F32),
            pltpu.VMEM((ND, ROWS, 128), F32),
            pltpu.SemaphoreType.DMA((len(EARLY) + len(LATE),)),
            pltpu.SemaphoreType.DMA((2,)),
            pltpu.SemaphoreType.DMA((5,)),
        ],
        compiler_params=pltpu.CompilerParams(
            collective_id=1, has_side_effects=True, vmem_limit_bytes=58 << 20
        ),
        name="main",
    )(
        column,
        ghosts,
        neighbours.reshape(ATOMS, ATOMS),
        e1w,
        e1b,
        e2w,
        row(e2b),
        e3w,
        row(e3b),
        row(f1b),
        row(f2b),
        row(f3b),
        f1w.T,
        f2w,
        f3w,
        fow.T,
        *late,
    )
    dipole, atom, centroid, energy = pl.pallas_call(
        deal_kernel,
        out_shape=(
            jax.ShapeDtypeStruct((3, 1, 1, 1, ATOMS), F32),
            jax.ShapeDtypeStruct((4, 1, 1, 1, ATOMS), F32),
            jax.ShapeDtypeStruct((4, 1, 1, 1, ATOMS), F32),
            jax.ShapeDtypeStruct((1, 1), F32),
        ),
        in_specs=[vmem],
        out_specs=(vmem,) * 4,
        name="deal",
    )(result)
    return dipole, atom, centroid, energy.reshape(())


def solution(mesh):
    return jax.shard_map(
        local,
        mesh=mesh,
        in_specs=(
            P(None, "wide", "narrow", None, None),
            P("wide", "narrow", None, None),
            P("wide", "narrow", None, None, None),
        )
        + (P(),) * 13,
        out_specs=(
            P(None, "wide", "narrow", None, None),
            P(None, "wide", "narrow", None, None),
            P(None, "wide", "narrow", None, None),
            P(),
        ),
        check_vma=False,
    )
```

```python
import functools
import math

import jax
import jax.numpy as jnp
import numpy as np
from jax import lax
from jax.experimental import pallas as pl
from jax.experimental.pallas import tpu as pltpu
from jax.sharding import PartitionSpec as P

NW, NN = 8, 16
ND = NW * NN
CX, CY, CZ = 32, 256, 16
TX, TZ = 32, 19
TILE = 640
FOLD = 512
ROWS = 10
SIDE = 4
UNROLL = 2
MODES = 512
ATOMS = 128
F32 = jnp.float32
BF16 = jnp.bfloat16
MESH = pl.DeviceIdType.MESH
HIGHEST = lax.Precision.HIGHEST
NT = (((1,), (1,)), ((), ()))
NNN = (((1,), (0,)), ((), ()))


def split(x):
    high = x.astype(BF16)
    return high, (x - high.astype(F32)).astype(BF16)


def mm(a, b, dims=NNN):
    return lax.dot_general(a, b, dims, preferred_element_type=F32)


def mm3(a, b, dims=NNN):
    return mm(a[0], b[0], dims) + mm(a[0], b[1], dims) + mm(a[1], b[0], dims)


def exact(a, b, dims=NNN):
    return lax.dot_general(a, b, dims, precision=HIGHEST, preferred_element_type=F32)


def iota(shape, dim):
    return lax.broadcasted_iota(jnp.int32, shape, dim)


def spline(offset):
    from_middle = offset - 2.0
    away = jnp.abs(from_middle)
    outer = jnp.maximum(2.0 - away, 0.0)
    inner = jnp.maximum(1.0 - away, 0.0)
    outer_square, inner_square = outer * outer, inner * inner
    value = (outer_square * outer - 4.0 * (inner_square * inner)) * (1.0 / 6.0)
    fall = 0.5 * outer_square - 2.0 * inner_square
    return value, jnp.where(from_middle > 0.0, -fall, fall)


def halo_kernel(positions_ref, species_ref, ghost_ref, own_ref, send_sem, recv_sem):
    wide = lax.axis_index("wide")
    narrow = lax.axis_index("narrow")
    steps = [(sx, sz) for sx in range(3) for sz in range(3) if (sx, sz) != (1, 1)]
    barrier = pltpu.get_barrier_semaphore()

    def device(sx, sz):
        return (lax.rem(wide + (NW + 1 - sx), NW), lax.rem(narrow + (NN + 1 - sz), NN))

    own_ref[...] = jnp.concatenate(
        [positions_ref[c, 0, 0] for c in range(3)]
        + [species_ref[0, 0].astype(F32), jnp.zeros((4, ATOMS), F32)],
        axis=0,
    )
    ghost_ref[4] = own_ref[...]
    for sx, sz in steps:
        pl.semaphore_signal(barrier, inc=1, device_id=device(sx, sz), device_id_type=MESH)
    pl.semaphore_wait(barrier, len(steps))
    copies = []
    for at, (sx, sz) in enumerate(steps):
        copy = pltpu.make_async_remote_copy(
            src_ref=own_ref,
            dst_ref=ghost_ref.at[sx * 3 + sz],
            send_sem=send_sem.at[at],
            recv_sem=recv_sem.at[at],
            device_id=device(sx, sz),
            device_id_type=MESH,
        )
        copy.start()
        copies.append(copy)
    for copy in copies:
        copy.wait()


def halo(positions, species):
    vmem = pl.BlockSpec(memory_space=pltpu.VMEM)
    return pl.pallas_call(
        halo_kernel,
        out_shape=jax.ShapeDtypeStruct((9, 8, ATOMS), F32),
        in_specs=[vmem, vmem],
        out_specs=vmem,
        scratch_shapes=[
            pltpu.VMEM((8, ATOMS), F32),
            pltpu.SemaphoreType.DMA((8,)),
            pltpu.SemaphoreType.DMA((8,)),
        ],
        compiler_params=pltpu.CompilerParams(collective_id=0, has_side_effects=True),
        name="halo",
    )(positions, species)


def spread_rows(rows, count):
    r = iota((rows, count), 0)
    c = iota((rows, count), 1)
    i = r & 31
    return jnp.where((i < 25) & (c == (r >> 5) * 25 + i), 1.0, 0.0).astype(F32)


def network(
    ghost_ref,
    near_ref,
    e1w_ref,
    e1b_ref,
    e2w_ref,
    e2b_ref,
    e3w_ref,
    e3b_ref,
    f1b_ref,
    f2b_ref,
    f3b_ref,
    f1w_ref,
    f2w_ref,
    f3w_ref,
    fow_ref,
    table_ref,
    own_ref,
    mat_ref,
    arrived,
):
    extent = (float(CX), float(CY), float(CZ))
    for k in range(9):
        shift = (float(k // 3 - 1), 0.0, float(k % 3 - 1))
        for c in range(3):
            table_ref[k * 4 + c] = jnp.broadcast_to(ghost_ref[k, c : c + 1, :] + shift[c], (8, ATOMS))
        table_ref[k * 4 + 3] = jnp.broadcast_to(ghost_ref[k, 3:4, :], (8, ATOMS))
    for c in range(3):
        own_ref[c] = jnp.broadcast_to(ghost_ref[4, c : c + 1, :], (ATOMS, ATOMS)).T

    pick1 = spread_rows(32, 25)
    pick2 = spread_rows(64, 50)
    pick3 = spread_rows(128, 100)

    def column(pick, row):
        return exact(pick, jnp.broadcast_to(row, (ATOMS, row.shape[1])), NT)

    w_oxygen = column(pick1, e1w_ref[0:1, :])
    w_hydrogen = column(pick1, e1w_ref[1:2, :])
    b_oxygen = column(pick1, e1b_ref[0:1, :])
    b_hydrogen = column(pick1, e1b_ref[1:2, :])
    bias2 = column(pick2, e2b_ref[...])
    bias3 = column(pick3, e3b_ref[...])
    w2 = exact(pick2, exact(pick1, e2w_ref[...]), NT)
    w3 = exact(pick3, exact(pick2, e3w_ref[...]), NT)
    last = iota((32, ATOMS), 0) == 31
    b_oxygen = jnp.where(last, 20.0, b_oxygen)
    b_hydrogen = jnp.where(last, 20.0, b_hydrogen)
    w2 = jnp.where(iota((64, 32), 1) == 31, bias2[:, :32], w2)
    w3 = jnp.where(iota((128, 64), 1) == 31, bias3[:, :64], w3)
    w2_high, w2_low = split(w2)
    w3_high, w3_low = split(w3)
    w2_all = jnp.concatenate([w2_high, w2_high, w2_low], axis=1)
    w3_all = jnp.concatenate([w3_high, w3_high, w3_low], axis=1)
    sublane = iota((8, ATOMS), 0)

    def geometry(g):
        rows = pl.ds(pl.multiple_of(g * 8, 8), 8)
        code = near_ref[rows, :]
        slot = code & 127
        offset = code >> 7
        brick = (offset * 11) >> 5
        step_y = (offset - 3 * brick - 1).astype(F32)
        parts = [jnp.zeros((8, ATOMS), F32)] * 4
        for k in range(9):
            here = brick == k
            for c in range(4):
                found = jnp.take_along_axis(table_ref[k * 4 + c], slot, axis=1)
                parts[c] = jnp.where(here, found, parts[c])
        parts[1] = parts[1] + step_y
        scaled = [(parts[c] - own_ref[c, rows, :]) * (extent[c] / 24.0) for c in range(3)]
        square = scaled[0] * scaled[0] + scaled[1] * scaled[1] + scaled[2] * scaled[2]
        smooth = 1.0 / (1.0 + square)
        scale = smooth * (1.0 / 128.0)
        return rows, smooth, parts[3], [scale] + [scale * scaled[c] for c in range(3)]

    def group(g, carry):
        sets = [geometry(g * SIDE + i) for i in range(SIDE)]
        pieces = []
        for _, smooth, kind, _ in sets:
            for b in range(8):
                s = jnp.broadcast_to(smooth[b : b + 1, :], (32, ATOMS))
                h = jnp.broadcast_to(kind[b : b + 1, :], (32, ATOMS)) > 0.5
                pieces.append(
                    jnp.where(h, w_hydrogen, w_oxygen) * s + jnp.where(h, b_hydrogen, b_oxygen)
                )
        one = jnp.tanh(jnp.concatenate(pieces, axis=1))
        high, low = split(one)
        two = jnp.tanh(mm(w2_all, jnp.concatenate([high, low, high], axis=0)))
        two = two + jnp.concatenate([one, one], axis=0)
        high, low = split(two)
        three = jnp.tanh(mm(w3_all, jnp.concatenate([high, low, high], axis=0)))
        three = three + jnp.concatenate([two, two], axis=0)
        high, low = split(three)
        for i, (rows, _, _, radial) in enumerate(sets):
            blocks = [
                jnp.concatenate([jnp.where(sublane == b, r, 0.0) for r in radial], axis=0)
                for b in range(8)
            ]
            r_high, r_low = split(jnp.concatenate(blocks, axis=1))
            mine = high[:, i * 1024 : (i + 1) * 1024]
            both = mm(jnp.concatenate([r_high, r_low], axis=0), mine, NT)
            found = (both[:32] + both[32:]) + mm(r_high, low[:, i * 1024 : (i + 1) * 1024], NT)
            for p in range(4):
                mat_ref[p, rows, :] = found[p * 8 : (p + 1) * 8]
        return carry

    lax.fori_loop(0, ATOMS // 8 // SIDE, group, 0, unroll=UNROLL)

    lane = iota((ATOMS, ATOMS), 1)
    entries = None
    matrix = [mat_ref[p] for p in range(4)]
    for p in range(4):
        tiled = jnp.take_along_axis(matrix[p], lane & 15, axis=1)
        term = []
        for t in range(13):
            d = jnp.minimum((lane >> 4) + 8 * t, 99)
            block = (d * 41) >> 10
            term.append(jnp.take_along_axis(matrix[p], d + 7 * block, axis=1) * tiled)
        term = jnp.concatenate(term, axis=1)
        entries = term if entries is None else entries + term
    arrived()
    hidden = mm3(split(entries[:, :1600]), split(f1w_ref[...]), NT)
    hidden = jnp.tanh(hidden + f1b_ref[...])
    hidden = hidden + jnp.tanh(mm3(split(hidden), split(f2w_ref[...])) + f2b_ref[...])
    hidden = hidden + jnp.tanh(mm3(split(hidden), split(f3w_ref[...])) + f3b_ref[...])
    coeffs = mm3(split(hidden), split(exact(pick3, fow_ref[...])), NT)
    result = jnp.zeros((ATOMS, ATOMS), F32)
    for c in range(3):
        total = jnp.sum(coeffs * matrix[1 + c], axis=1, keepdims=True)
        result = jnp.where(lane == c, total, result)
    return result.T[:8]


def np_split(x):
    x = np.asarray(x, np.float32)
    high = x.astype(jnp.bfloat16)
    low = (x - high.astype(np.float32)).astype(jnp.bfloat16)
    return np.stack([high, low])


@functools.lru_cache(None)
def tables():
    m = np.arange(128)[:, None]
    y = np.arange(CY)[None, :]
    angle = 2 * np.pi * (m * y % CY) / CY
    lower = -np.sin(angle)
    lower[0] = 1 - 2 * (y[0] % 2)
    dft_y = np_split(np.concatenate([np.cos(angle), lower]))
    j, k = np.divmod(np.arange(ND), NN)
    phi = 2 * np.pi * ((2 * j[:, None] * j[None] + k[:, None] * k[None]) % 16) / 16
    cos, sin = np.cos(phi), np.sin(phi)
    dft_b = np_split(np.block([[cos, sin], [-sin, cos]]))
    z, x = np.divmod(np.arange(TILE), TX)
    turn = 2 * np.pi * ((j[:, None] * (x - 1)[None] + k[:, None] * (z - 3)[None]) % 256) / 256
    twiddle = np.stack([np.cos(turn), np.sin(turn)]).astype(np.float32)
    v, u = np.divmod(np.arange(MODES), 32)
    ax = 2 * np.pi * ((np.arange(TX)[:, None] - 1) * u[None] % 32) / 32
    az = 2 * np.pi * ((np.arange(16)[:, None] - 3) * v[None] % 16) / 16
    fac_x = np.stack([np.cos(ax), np.sin(ax)]).astype(np.float32)
    fac_z = np.stack([np.cos(az), np.sin(az)]).astype(np.float32)

    def fold(i, n):
        return np.where(2 * i >= n, i - n, i) / n

    def modulus(i, n):
        return 36.0 / (4 + 2 * np.cos(2 * np.pi * i / n)) ** 2

    def decay(f):
        return np.exp(-np.pi**2 * f * f / 0.81)

    mx = j[:, None] + 8 * u[None]
    mz = k[:, None] + 16 * v[None]
    fx, fz = fold(mx, 256), fold(mz, 256)
    scale = 0.25 / (np.pi * 256.0**3)
    plane = scale * decay(fx) * decay(fz) * modulus(mx, 256) * modulus(mz, 256)
    green = np.stack([plane, fx * fx + fz * fz]).astype(np.float32)
    my = np.arange(129)
    fy = fold(my, 256)
    column = np.stack([decay(fy) * modulus(my, 256), fy * fy]).astype(np.float32)
    return dft_y, dft_b, twiddle, fac_x, fac_z, green, column


EARLY = (
    ((9, 8, ATOMS), F32),
    ((ATOMS, ATOMS), jnp.int32),
    ((2, 25), F32),
    ((2, 25), F32),
    ((25, 50), F32),
    ((1, 50), F32),
    ((50, 100), F32),
    ((1, 100), F32),
    ((1, 240), F32),
    ((1, 240), F32),
    ((1, 240), F32),
)
LATE = (
    ((240, 1600), F32),
    ((240, 240), F32),
    ((240, 240), F32),
    ((100, 240), F32),
    ((2, 256, CY), BF16),
    ((2, 256, 256), BF16),
    ((2, ND, TILE), F32),
    ((2, TX, MODES), F32),
    ((2, 16, MODES), F32),
    ((2, ND, MODES), F32),
)


def main_kernel(*refs):
    count = len(EARLY) + len(LATE)
    column_ref = refs[0]
    far = refs[1 : 1 + count]
    result_ref = refs[1 + count]
    near = refs[2 + count : 2 + 2 * count]
    (
        ghost_ref,
        near_ref,
        e1w_ref,
        e1b_ref,
        e2w_ref,
        e2b_ref,
        e3w_ref,
        e3b_ref,
        f1b_ref,
        f2b_ref,
        f3b_ref,
    ) = near[: len(EARLY)]
    (
        table_ref,
        home_ref,
        mat_ref,
        mix_ref,
        wave_ref,
        tab_ref,
        out_one,
        in_one,
        out_two,
        in_two,
        late_sem,
        send_sem,
        recv_sem,
    ) = refs[2 + 2 * count :]
    f1w_ref, f2w_ref, f3w_ref, fow_ref = near[len(EARLY) : len(EARLY) + 4]
    dft_y_ref, dft_b_ref, twiddle_ref, fac_x_ref, fac_z_ref, green_ref = near[len(EARLY) + 4 :]
    fetch = [pltpu.make_async_copy(far[i], near[i], late_sem.at[i]) for i in range(count)]
    for copy in fetch:
        copy.start()
    wide = lax.axis_index("wide")
    narrow = lax.axis_index("narrow")
    me = wide * NN + narrow
    barrier = pltpu.get_barrier_semaphore()

    def peer(d):
        at = lax.rem(me + d, ND)
        return at, (at // NN, lax.rem(at, NN))

    def greet(d, carry):
        pl.semaphore_signal(barrier, inc=1, device_id=peer(d)[1], device_id_type=MESH)
        return carry

    lax.fori_loop(1, ND, greet, 0)

    def arrived():
        for copy in fetch[len(EARLY) :]:
            copy.wait()

    for copy in fetch[: len(EARLY)]:
        copy.wait()
    dip = network(
        ghost_ref,
        near_ref,
        e1w_ref,
        e1b_ref,
        e2w_ref,
        e2b_ref,
        e3w_ref,
        e3b_ref,
        f1b_ref,
        f2b_ref,
        f3b_ref,
        f1w_ref,
        f2w_ref,
        f3w_ref,
        fow_ref,
        table_ref,
        home_ref,
        mat_ref,
        arrived,
    )

    kind = ghost_ref[4, 3:4, :]
    oxygen = 1.0 - kind
    result_ref[0:8, :] = dip * oxygen
    shift = 0.5 * jnp.tanh(dip)

    def sites(c, extent):
        atom = ghost_ref[4, c : c + 1, :] * float(extent)
        return jnp.concatenate([atom, atom + shift[c : c + 1, :]], axis=1)

    charge = jnp.concatenate([6.0 * oxygen + kind, -8.0 * oxygen], axis=1)
    off_x = sites(0, CX) - (iota((TX, 256), 0).astype(F32) - 1.0)
    off_z = sites(2, CZ) - (iota((24, 256), 0).astype(F32) - 3.0)
    off_y = sites(1, CY) - iota((CY, 256), 0).astype(F32)
    wx, sx = spline(off_x)
    wz, sz = spline(off_z)
    wy, sy = spline(off_y)
    dft_y = (dft_y_ref[0], dft_y_ref[1])
    wave = mm3(dft_y, split(wy))
    wave_ref[:, :256] = wave
    wave_ref[:, 256:] = sy
    rest = jnp.zeros((TILE - TX * TZ, 256), F32)

    def blend(at, left, right):
        full = jnp.concatenate([left[z : z + 1, :] * right for z in range(TZ)] + [rest], axis=0)
        high, low = split(full)
        mix_ref[0, :, at * 256 : (at + 1) * 256] = high
        mix_ref[1, :, at * 256 : (at + 1) * 256] = low
        return high, low

    spread = mm3(split(wave * charge), blend(0, wz, wx), NT)
    for part in range(2):
        for t in range(5):
            out_one[:, part * 5 + t, :] = spread[part * 128 : (part + 1) * 128, t * 128 : (t + 1) * 128]

    pl.semaphore_wait(barrier, ND - 1)

    def exchange(out_ref, in_ref, s):
        def one(d, carry):
            at, device = peer(d)
            pltpu.make_async_remote_copy(
                src_ref=out_ref.at[at],
                dst_ref=in_ref.at[me],
                send_sem=send_sem.at[s],
                recv_sem=recv_sem.at[s],
                device_id=device,
                device_id_type=MESH,
            ).start()
            return carry

        lax.fori_loop(1, ND, one, 0)
        in_ref[me] = out_ref[me]

    def settle(out_ref, in_ref, s):
        whole = pltpu.make_async_remote_copy(
            src_ref=out_ref.at[pl.ds(0, ND - 1)],
            dst_ref=in_ref.at[pl.ds(0, ND - 1)],
            send_sem=send_sem.at[s],
            recv_sem=recv_sem.at[s],
            device_id=peer(1)[1],
            device_id_type=MESH,
        )
        whole.wait_send()
        whole.wait_recv()

    exchange(out_one, in_one, 0)

    blend(1, wz, sx)
    blend(2, sz, wx)
    wave_ref[:, 256:] = mm3(dft_y, split(wave_ref[:, 256:]))

    def build(z, carry):
        cz = fac_z_ref[0, pl.ds(z, 1), :]
        zz = fac_z_ref[1, pl.ds(z, 1), :]
        cx, xx = fac_x_ref[0], fac_x_ref[1]
        rows = pl.ds(pl.multiple_of(z * TX, 8), TX)
        tab_ref[0, rows, :] = cx * cz - xx * zz
        tab_ref[1, rows, :] = xx * cz + cx * zz
        return carry

    lax.fori_loop(0, 16, build, 0)
    cos_e = split(tab_ref[0])
    sin_e = split(tab_ref[1])

    def influence(at, weight):
        total = green_ref[1] + column_ref[1, at]
        inverse = jnp.where(total == 0.0, 0.0, 1.0 / jnp.where(total == 0.0, 1.0, total))
        return green_ref[0] * (inverse * (column_ref[0, at] * weight))

    first = me == 0
    weight = jnp.where(first, 1.0, 2.0)
    green_a = influence(me, weight)
    green_b = influence(jnp.where(first, 128, me), weight)
    settle(out_one, in_one, 0)

    def gathered(in_ref):
        return jnp.concatenate(
            [
                jnp.concatenate([in_ref[:, part * 5 + t, :] for t in range(5)], axis=1)
                for part in range(2)
            ],
            axis=0,
        )

    tiles = gathered(in_one)
    bricks = mm3((dft_b_ref[0], dft_b_ref[1]), split(tiles))
    real, imag = bricks[:128], bricks[128:]
    cos_t, sin_t = twiddle_ref[0], twiddle_ref[1]
    turned = jnp.concatenate(
        [real * cos_t + imag * sin_t, imag * cos_t - real * sin_t], axis=0
    )
    turned = jnp.concatenate(
        [turned[:, :128] + turned[:, FOLD:], turned[:, 128:FOLD]], axis=1
    )
    turned = split(turned)
    by_cos = mm3(turned, cos_e)
    by_sin = mm3(turned, sin_e)
    real = by_cos[:128] + by_sin[128:]
    imag = by_cos[128:] - by_sin[:128]

    modes = split(
        jnp.concatenate(
            [green_a * real, green_a * imag, green_b * real, green_b * imag], axis=0
        )
    )
    by_cos = mm3(modes, cos_e, NT)
    by_sin = mm3(modes, sin_e, NT)

    def widen(x):
        return jnp.concatenate([x, x[:, :128]], axis=1)

    def back(at):
        real = widen(by_cos[at : at + 128] - by_sin[at + 128 : at + 256])
        imag = widen(by_sin[at : at + 128] + by_cos[at + 128 : at + 256])
        return real * cos_t - imag * sin_t, imag * cos_t + real * sin_t

    real_a, imag_a = back(0)
    real_b, imag_b = back(256)
    field_r = mm3(
        (dft_b_ref[0, :128], dft_b_ref[1, :128]),
        split(jnp.concatenate([real_a, -imag_a], axis=0)),
    )
    field_i = mm3(
        (dft_b_ref[0, 128:], dft_b_ref[1, 128:]),
        split(jnp.concatenate([-real_b, imag_b], axis=0)),
    )
    partial = jnp.sum(tiles[:128] * field_r + tiles[128:] * field_i, keepdims=True)
    partial = partial * (0.5 / (ND * ATOMS))
    lane = iota((ND, 128), 1)
    for t in range(5):
        piece = field_r[:, t * 128 : (t + 1) * 128]
        if t == 4:
            piece = jnp.where(lane == 127, partial, piece)
        out_two[:, t, :] = piece
        out_two[:, 5 + t, :] = field_i[:, t * 128 : (t + 1) * 128]

    def place(c, i):
        step = c * 2 + i // NN
        w = lax.rem(wide + step, NW)
        n = lax.rem(narrow + lax.rem(i, NN), NN)
        return w * NN + n, (w, n)

    for c in range(4):

        def one(i, carry):
            at, device = place(c, i)
            pltpu.make_async_remote_copy(
                src_ref=out_two.at[at],
                dst_ref=in_two.at[me],
                send_sem=send_sem.at[1],
                recv_sem=recv_sem.at[1 + c],
                device_id=device,
                device_id_type=MESH,
            ).start()
            return carry

        lax.fori_loop(1 if c == 0 else 0, 32, one, 0)
    in_two[me] = out_two[me]
    mix = (mix_ref[0], mix_ref[1])
    rows = [jnp.zeros((1, 256), F32)] * 4
    total = jnp.zeros((1, 1), F32)
    for c in range(4):
        size = 31 if c == 0 else 32
        pltpu.make_async_remote_copy(
            src_ref=out_two.at[pl.ds(0, size)],
            dst_ref=in_two.at[pl.ds(0, size)],
            send_sem=send_sem.at[1],
            recv_sem=recv_sem.at[1 + c],
            device_id=peer(1)[1],
            device_id_type=MESH,
        ).wait_recv()
        spans = [lax.rem(wide + (NW - 2 * c - i), NW) * NN for i in range(2)]
        spans = [pl.ds(pl.multiple_of(at, NN), NN) for at in spans]
        lower = [pl.ds(pl.multiple_of(at.start + ND, NN), NN) for at in spans]
        planes = jnp.concatenate(
            [
                jnp.concatenate([in_two[at, part * 5 + t, :] for t in range(5)], axis=1)
                for part in range(2)
                for at in spans
            ],
            axis=0,
        )
        inner = mm3(split(planes), mix)
        wave = jnp.concatenate([wave_ref[at, :] for at in spans + lower], axis=0)
        wave, wave_slope = wave[:, :256], wave[:, 256:]
        parts = [
            wave * inner[:, :256],
            -wave * inner[:, 256:512],
            -wave_slope * inner[:, :256],
            -wave * inner[:, 512:],
        ]
        rows = [r + jnp.sum(p, axis=0, keepdims=True) for r, p in zip(rows, parts)]
        total = total + jnp.sum(planes[:32, TILE - 1 : TILE], axis=0, keepdims=True)
    pltpu.make_async_remote_copy(
        src_ref=out_two.at[pl.ds(0, ND - 1)],
        dst_ref=in_two.at[pl.ds(0, ND - 1)],
        send_sem=send_sem.at[1],
        recv_sem=recv_sem.at[1],
        device_id=peer(1)[1],
        device_id_type=MESH,
    ).wait_send()
    atom = [r[:, :128] for r in rows]
    centroid = [r[:, 128:] * oxygen for r in rows]
    result_ref[8:24, :] = jnp.concatenate(
        atom + centroid + [jnp.broadcast_to(total, (8, ATOMS))], axis=0
    )


def deal_kernel(result_ref, dipole_ref, atom_ref, centroid_ref, energy_ref):
    for c in range(3):
        dipole_ref[c, 0, 0] = result_ref[c : c + 1, :]
    for c in range(4):
        atom_ref[c, 0, 0] = result_ref[8 + c : 9 + c, :]
        centroid_ref[c, 0, 0] = result_ref[12 + c : 13 + c, :]
    energy_ref[...] = result_ref[16:17, 0:1]


def local(
    positions,
    species,
    neighbours,
    e1w,
    e1b,
    e2w,
    e2b,
    e3w,
    e3b,
    f1w,
    f1b,
    f2w,
    f2b,
    f3w,
    f3b,
    fow,
):
    ghosts = halo(positions, species)
    *late, column = [jnp.asarray(t) for t in tables()]
    vmem = pl.BlockSpec(memory_space=pltpu.VMEM)
    anywhere = pl.BlockSpec(memory_space=pl.ANY)
    row = lambda x: x.reshape(1, -1)
    result = pl.pallas_call(
        main_kernel,
        out_shape=jax.ShapeDtypeStruct((24, ATOMS), F32),
        in_specs=[pl.BlockSpec(memory_space=pltpu.SMEM)] + [anywhere] * (len(EARLY) + len(LATE)),
        out_specs=vmem,
        scratch_shapes=[pltpu.VMEM(shape, dtype) for shape, dtype in EARLY + LATE]
        + [
            pltpu.VMEM((36, 8, ATOMS), F32),
            pltpu.VMEM((3, ATOMS, ATOMS), F32),
            pltpu.VMEM((4, ATOMS, ATOMS), F32),
            pltpu.VMEM((2, TILE, 768), BF16),
            pltpu.VMEM((CY, 512), F32),
            pltpu.VMEM((2, FOLD, MODES), F32),
            pltpu.VMEM((ND, ROWS, 128), F32),
            pltpu.VMEM((ND, ROWS, 128), F32),
            pltpu.VMEM((ND, ROWS, 128), F32),
            pltpu.VMEM((ND, ROWS, 128), F32),
            pltpu.SemaphoreType.DMA((len(EARLY) + len(LATE),)),
            pltpu.SemaphoreType.DMA((2,)),
            pltpu.SemaphoreType.DMA((5,)),
        ],
        compiler_params=pltpu.CompilerParams(
            collective_id=1, has_side_effects=True, vmem_limit_bytes=58 << 20
        ),
        name="main",
    )(
        column,
        ghosts,
        neighbours.reshape(ATOMS, ATOMS),
        e1w,
        e1b,
        e2w,
        row(e2b),
        e3w,
        row(e3b),
        row(f1b),
        row(f2b),
        row(f3b),
        f1w.T,
        f2w,
        f3w,
        fow.T,
        *late,
    )
    dipole, atom, centroid, energy = pl.pallas_call(
        deal_kernel,
        out_shape=(
            jax.ShapeDtypeStruct((3, 1, 1, 1, ATOMS), F32),
            jax.ShapeDtypeStruct((4, 1, 1, 1, ATOMS), F32),
            jax.ShapeDtypeStruct((4, 1, 1, 1, ATOMS), F32),
            jax.ShapeDtypeStruct((1, 1), F32),
        ),
        in_specs=[vmem],
        out_specs=(vmem,) * 4,
        name="deal",
    )(result)
    return dipole, atom, centroid, energy.reshape(())


def solution(mesh):
    return jax.shard_map(
        local,
        mesh=mesh,
        in_specs=(
            P(None, "wide", "narrow", None, None),
            P("wide", "narrow", None, None),
            P("wide", "narrow", None, None, None),
        )
        + (P(),) * 13,
        out_specs=(
            P(None, "wide", "narrow", None, None),
            P(None, "wide", "narrow", None, None),
            P(None, "wide", "narrow", None, None),
            P(),
        ),
        check_vma=False,
    )
```

```python
import functools
import math

import jax
import jax.numpy as jnp
import numpy as np
from jax import lax
from jax.experimental import pallas as pl
from jax.experimental.pallas import tpu as pltpu
from jax.sharding import PartitionSpec as P

NW, NN = 8, 16
ND = NW * NN
CX, CY, CZ = 32, 256, 16
TX, TZ = 32, 19
TILE = 640
FOLD = 512
ROWS = 10
SIDE = 4
UNROLL = 2
MODES = 512
ATOMS = 128
F32 = jnp.float32
BF16 = jnp.bfloat16
MESH = pl.DeviceIdType.MESH
HIGHEST = lax.Precision.HIGHEST
NT = (((1,), (1,)), ((), ()))
NNN = (((1,), (0,)), ((), ()))


def split(x):
    high = x.astype(BF16)
    return high, (x - high.astype(F32)).astype(BF16)


def mm(a, b, dims=NNN):
    return lax.dot_general(a, b, dims, preferred_element_type=F32)


def mm3(a, b, dims=NNN):
    return mm(a[0], b[0], dims) + mm(a[0], b[1], dims) + mm(a[1], b[0], dims)


def exact(a, b, dims=NNN):
    return lax.dot_general(a, b, dims, precision=HIGHEST, preferred_element_type=F32)


def iota(shape, dim):
    return lax.broadcasted_iota(jnp.int32, shape, dim)


def spline(offset):
    from_middle = offset - 2.0
    away = jnp.abs(from_middle)
    outer = jnp.maximum(2.0 - away, 0.0)
    inner = jnp.maximum(1.0 - away, 0.0)
    outer_square, inner_square = outer * outer, inner * inner
    value = (outer_square * outer - 4.0 * (inner_square * inner)) * (1.0 / 6.0)
    fall = 0.5 * outer_square - 2.0 * inner_square
    return value, jnp.where(from_middle > 0.0, -fall, fall)


def halo_kernel(positions_ref, species_ref, ghost_ref, own_ref, send_sem, recv_sem):
    wide = lax.axis_index("wide")
    narrow = lax.axis_index("narrow")
    steps = [(sx, sz) for sx in range(3) for sz in range(3) if (sx, sz) != (1, 1)]
    barrier = pltpu.get_barrier_semaphore()

    def device(sx, sz):
        return (lax.rem(wide + (NW + 1 - sx), NW), lax.rem(narrow + (NN + 1 - sz), NN))

    own_ref[...] = jnp.concatenate(
        [positions_ref[c, 0, 0] for c in range(3)]
        + [species_ref[0, 0].astype(F32), jnp.zeros((4, ATOMS), F32)],
        axis=0,
    )
    ghost_ref[4] = own_ref[...]
    for sx, sz in steps:
        pl.semaphore_signal(barrier, inc=1, device_id=device(sx, sz), device_id_type=MESH)
    pl.semaphore_wait(barrier, len(steps))
    copies = []
    for at, (sx, sz) in enumerate(steps):
        copy = pltpu.make_async_remote_copy(
            src_ref=own_ref,
            dst_ref=ghost_ref.at[sx * 3 + sz],
            send_sem=send_sem.at[at],
            recv_sem=recv_sem.at[at],
            device_id=device(sx, sz),
            device_id_type=MESH,
        )
        copy.start()
        copies.append(copy)
    for copy in copies:
        copy.wait()


def halo(positions, species):
    vmem = pl.BlockSpec(memory_space=pltpu.VMEM)
    return pl.pallas_call(
        halo_kernel,
        out_shape=jax.ShapeDtypeStruct((9, 8, ATOMS), F32),
        in_specs=[vmem, vmem],
        out_specs=vmem,
        scratch_shapes=[
            pltpu.VMEM((8, ATOMS), F32),
            pltpu.SemaphoreType.DMA((8,)),
            pltpu.SemaphoreType.DMA((8,)),
        ],
        compiler_params=pltpu.CompilerParams(collective_id=0, has_side_effects=True),
        name="halo",
    )(positions, species)


def spread_rows(rows, count):
    r = iota((rows, count), 0)
    c = iota((rows, count), 1)
    i = r & 31
    return jnp.where((i < 25) & (c == (r >> 5) * 25 + i), 1.0, 0.0).astype(F32)


def network(
    ghost_ref,
    near_ref,
    e1w_ref,
    e1b_ref,
    e2w_ref,
    e2b_ref,
    e3w_ref,
    e3b_ref,
    f1b_ref,
    f2b_ref,
    f3b_ref,
    f1w_ref,
    f2w_ref,
    f3w_ref,
    fow_ref,
    table_ref,
    own_ref,
    mat_ref,
    arrived,
):
    extent = (float(CX), float(CY), float(CZ))
    for k in range(9):
        shift = (float(k // 3 - 1), 0.0, float(k % 3 - 1))
        for c in range(3):
            table_ref[k * 4 + c] = jnp.broadcast_to(ghost_ref[k, c : c + 1, :] + shift[c], (8, ATOMS))
        table_ref[k * 4 + 3] = jnp.broadcast_to(ghost_ref[k, 3:4, :], (8, ATOMS))
    for c in range(3):
        own_ref[c] = jnp.broadcast_to(ghost_ref[4, c : c + 1, :], (ATOMS, ATOMS)).T

    pick1 = spread_rows(32, 25)
    pick2 = spread_rows(64, 50)
    pick3 = spread_rows(128, 100)

    def column(pick, row):
        return exact(pick, jnp.broadcast_to(row, (ATOMS, row.shape[1])), NT)

    w_oxygen = column(pick1, e1w_ref[0:1, :])
    w_hydrogen = column(pick1, e1w_ref[1:2, :])
    b_oxygen = column(pick1, e1b_ref[0:1, :])
    b_hydrogen = column(pick1, e1b_ref[1:2, :])
    bias2 = column(pick2, e2b_ref[...])
    bias3 = column(pick3, e3b_ref[...])
    w2 = exact(pick2, exact(pick1, e2w_ref[...]), NT)
    w3 = exact(pick3, exact(pick2, e3w_ref[...]), NT)
    last = iota((32, ATOMS), 0) == 31
    b_oxygen = jnp.where(last, 20.0, b_oxygen)
    b_hydrogen = jnp.where(last, 20.0, b_hydrogen)
    w2 = jnp.where(iota((64, 32), 1) == 31, bias2[:, :32], w2)
    w3 = jnp.where(iota((128, 64), 1) == 31, bias3[:, :64], w3)
    w2_high, w2_low = split(w2)
    w3_high, w3_low = split(w3)
    w2_all = jnp.concatenate([w2_high, w2_high, w2_low], axis=1)
    w3_all = jnp.concatenate([w3_high, w3_high, w3_low], axis=1)
    sublane = iota((8, ATOMS), 0)

    def geometry(g):
        rows = pl.ds(pl.multiple_of(g * 8, 8), 8)
        code = near_ref[rows, :]
        slot = code & 127
        offset = code >> 7
        brick = (offset * 11) >> 5
        step_y = (offset - 3 * brick - 1).astype(F32)
        parts = [jnp.zeros((8, ATOMS), F32)] * 4
        for k in range(9):
            here = brick == k
            for c in range(4):
                found = jnp.take_along_axis(table_ref[k * 4 + c], slot, axis=1)
                parts[c] = jnp.where(here, found, parts[c])
        parts[1] = parts[1] + step_y
        scaled = [(parts[c] - own_ref[c, rows, :]) * (extent[c] / 24.0) for c in range(3)]
        square = scaled[0] * scaled[0] + scaled[1] * scaled[1] + scaled[2] * scaled[2]
        smooth = 1.0 / (1.0 + square)
        scale = smooth * (1.0 / 128.0)
        return rows, smooth, parts[3], [scale] + [scale * scaled[c] for c in range(3)]

    def group(g, carry):
        sets = [geometry(g * SIDE + i) for i in range(SIDE)]
        pieces = []
        for _, smooth, kind, _ in sets:
            for b in range(8):
                s = jnp.broadcast_to(smooth[b : b + 1, :], (32, ATOMS))
                h = jnp.broadcast_to(kind[b : b + 1, :], (32, ATOMS)) > 0.5
                pieces.append(
                    jnp.where(h, w_hydrogen, w_oxygen) * s + jnp.where(h, b_hydrogen, b_oxygen)
                )
        one = jnp.tanh(jnp.concatenate(pieces, axis=1))
        high, low = split(one)
        two = jnp.tanh(mm(w2_all, jnp.concatenate([high, low, high], axis=0)))
        two = two + jnp.concatenate([one, one], axis=0)
        high, low = split(two)
        three = jnp.tanh(mm(w3_all, jnp.concatenate([high, low, high], axis=0)))
        three = three + jnp.concatenate([two, two], axis=0)
        high, low = split(three)
        for i, (rows, _, _, radial) in enumerate(sets):
            blocks = [
                jnp.concatenate([jnp.where(sublane == b, r, 0.0) for r in radial], axis=0)
                for b in range(8)
            ]
            r_high, r_low = split(jnp.concatenate(blocks, axis=1))
            mine = high[:, i * 1024 : (i + 1) * 1024]
            both = mm(jnp.concatenate([r_high, r_low], axis=0), mine, NT)
            found = (both[:32] + both[32:]) + mm(r_high, low[:, i * 1024 : (i + 1) * 1024], NT)
            for p in range(4):
                mat_ref[p, rows, :] = found[p * 8 : (p + 1) * 8]
        return carry

    lax.fori_loop(0, ATOMS // 8 // SIDE, group, 0, unroll=UNROLL)

    lane = iota((ATOMS, ATOMS), 1)
    entries = None
    matrix = [mat_ref[p] for p in range(4)]
    for p in range(4):
        tiled = jnp.take_along_axis(matrix[p], lane & 15, axis=1)
        term = []
        for t in range(13):
            d = jnp.minimum((lane >> 4) + 8 * t, 99)
            block = (d * 41) >> 10
            term.append(jnp.take_along_axis(matrix[p], d + 7 * block, axis=1) * tiled)
        term = jnp.concatenate(term, axis=1)
        entries = term if entries is None else entries + term
    arrived()
    hidden = mm3(split(entries[:, :1600]), split(f1w_ref[...]), NT)
    hidden = jnp.tanh(hidden + f1b_ref[...])
    hidden = hidden + jnp.tanh(mm3(split(hidden), split(f2w_ref[...])) + f2b_ref[...])
    hidden = hidden + jnp.tanh(mm3(split(hidden), split(f3w_ref[...])) + f3b_ref[...])
    coeffs = mm3(split(hidden), split(exact(pick3, fow_ref[...])), NT)
    result = jnp.zeros((ATOMS, ATOMS), F32)
    for c in range(3):
        total = jnp.sum(coeffs * matrix[1 + c], axis=1, keepdims=True)
        result = jnp.where(lane == c, total, result)
    return result.T[:8]


def np_split(x):
    x = np.asarray(x, np.float32)
    high = x.astype(jnp.bfloat16)
    low = (x - high.astype(np.float32)).astype(jnp.bfloat16)
    return np.stack([high, low])


@functools.lru_cache(None)
def tables():
    m = np.arange(128)[:, None]
    y = np.arange(CY)[None, :]
    angle = 2 * np.pi * (m * y % CY) / CY
    lower = -np.sin(angle)
    lower[0] = 1 - 2 * (y[0] % 2)
    dft_y = np_split(np.concatenate([np.cos(angle), lower]))
    j, k = np.divmod(np.arange(ND), NN)
    phi = 2 * np.pi * ((2 * j[:, None] * j[None] + k[:, None] * k[None]) % 16) / 16
    cos, sin = np.cos(phi), np.sin(phi)
    dft_b = np_split(np.block([[cos, sin], [-sin, cos]]))
    z, x = np.divmod(np.arange(TILE), TX)
    turn = 2 * np.pi * ((j[:, None] * (x - 1)[None] + k[:, None] * (z - 3)[None]) % 256) / 256
    twiddle = np.stack([np.cos(turn), np.sin(turn)]).astype(np.float32)
    v, u = np.divmod(np.arange(MODES), 32)
    ax = 2 * np.pi * ((np.arange(TX)[:, None] - 1) * u[None] % 32) / 32
    az = 2 * np.pi * ((np.arange(16)[:, None] - 3) * v[None] % 16) / 16
    fac_x = np.stack([np.cos(ax), np.sin(ax)]).astype(np.float32)
    fac_z = np.stack([np.cos(az), np.sin(az)]).astype(np.float32)

    def fold(i, n):
        return np.where(2 * i >= n, i - n, i) / n

    def modulus(i, n):
        return 36.0 / (4 + 2 * np.cos(2 * np.pi * i / n)) ** 2

    def decay(f):
        return np.exp(-np.pi**2 * f * f / 0.81)

    mx = j[:, None] + 8 * u[None]
    mz = k[:, None] + 16 * v[None]
    fx, fz = fold(mx, 256), fold(mz, 256)
    scale = 0.25 / (np.pi * 256.0**3)
    plane = scale * decay(fx) * decay(fz) * modulus(mx, 256) * modulus(mz, 256)
    green = np.stack([plane, fx * fx + fz * fz]).astype(np.float32)
    my = np.arange(129)
    fy = fold(my, 256)
    column = np.stack([decay(fy) * modulus(my, 256), fy * fy]).astype(np.float32)
    return dft_y, dft_b, twiddle, fac_x, fac_z, green, column


EARLY = (
    ((9, 8, ATOMS), F32),
    ((ATOMS, ATOMS), jnp.int32),
    ((2, 25), F32),
    ((2, 25), F32),
    ((25, 50), F32),
    ((1, 50), F32),
    ((50, 100), F32),
    ((1, 100), F32),
    ((1, 240), F32),
    ((1, 240), F32),
    ((1, 240), F32),
)
LATE = (
    ((240, 1600), F32),
    ((240, 240), F32),
    ((240, 240), F32),
    ((100, 240), F32),
    ((2, 256, CY), BF16),
    ((2, 256, 256), BF16),
    ((2, ND, TILE), F32),
    ((2, TX, MODES), F32),
    ((2, 16, MODES), F32),
    ((2, ND, MODES), F32),
)


def main_kernel(*refs):
    count = len(EARLY) + len(LATE)
    column_ref = refs[0]
    far = refs[1 : 1 + count]
    result_ref = refs[1 + count]
    near = refs[2 + count : 2 + 2 * count]
    (
        ghost_ref,
        near_ref,
        e1w_ref,
        e1b_ref,
        e2w_ref,
        e2b_ref,
        e3w_ref,
        e3b_ref,
        f1b_ref,
        f2b_ref,
        f3b_ref,
    ) = near[: len(EARLY)]
    (
        table_ref,
        home_ref,
        mat_ref,
        mix_ref,
        wave_ref,
        tab_ref,
        plane_ref,
        field_ref,
        out_one,
        in_one,
        out_two,
        in_two,
        late_sem,
        send_sem,
        recv_sem,
    ) = refs[2 + 2 * count :]
    f1w_ref, f2w_ref, f3w_ref, fow_ref = near[len(EARLY) : len(EARLY) + 4]
    dft_y_ref, dft_b_ref, twiddle_ref, fac_x_ref, fac_z_ref, green_ref = near[len(EARLY) + 4 :]
    fetch = [pltpu.make_async_copy(far[i], near[i], late_sem.at[i]) for i in range(count)]
    for copy in fetch:
        copy.start()
    wide = lax.axis_index("wide")
    narrow = lax.axis_index("narrow")
    me = wide * NN + narrow
    barrier = pltpu.get_barrier_semaphore()

    def peer(d):
        at = lax.rem(me + d, ND)
        return at, (at // NN, lax.rem(at, NN))

    def greet(d, carry):
        pl.semaphore_signal(barrier, inc=1, device_id=peer(d)[1], device_id_type=MESH)
        return carry

    lax.fori_loop(1, ND, greet, 0)

    def arrived():
        for copy in fetch[len(EARLY) :]:
            copy.wait()

    for copy in fetch[: len(EARLY)]:
        copy.wait()
    dip = network(
        ghost_ref,
        near_ref,
        e1w_ref,
        e1b_ref,
        e2w_ref,
        e2b_ref,
        e3w_ref,
        e3b_ref,
        f1b_ref,
        f2b_ref,
        f3b_ref,
        f1w_ref,
        f2w_ref,
        f3w_ref,
        fow_ref,
        table_ref,
        home_ref,
        mat_ref,
        arrived,
    )

    kind = ghost_ref[4, 3:4, :]
    oxygen = 1.0 - kind
    result_ref[0:8, :] = dip * oxygen
    shift = 0.5 * jnp.tanh(dip)

    def sites(c, extent):
        atom = ghost_ref[4, c : c + 1, :] * float(extent)
        return jnp.concatenate([atom, atom + shift[c : c + 1, :]], axis=1)

    charge = jnp.concatenate([6.0 * oxygen + kind, -8.0 * oxygen], axis=1)
    off_x = sites(0, CX) - (iota((TX, 256), 0).astype(F32) - 1.0)
    off_z = sites(2, CZ) - (iota((24, 256), 0).astype(F32) - 3.0)
    off_y = sites(1, CY) - iota((CY, 256), 0).astype(F32)
    wx, sx = spline(off_x)
    wz, sz = spline(off_z)
    wy, sy = spline(off_y)
    dft_y = (dft_y_ref[0], dft_y_ref[1])
    wave = mm3(dft_y, split(wy))
    wave_ref[:, :256] = wave
    wave_ref[:, 256:] = sy
    rest = jnp.zeros((TILE - TX * TZ, 256), F32)

    def blend(at, left, right):
        full = jnp.concatenate([left[z : z + 1, :] * right for z in range(TZ)] + [rest], axis=0)
        high, low = split(full)
        mix_ref[0, :, at * 256 : (at + 1) * 256] = high
        mix_ref[1, :, at * 256 : (at + 1) * 256] = low
        return high, low

    spread = mm3(split(wave * charge), blend(0, wz, wx), NT)
    for part in range(2):
        for t in range(5):
            out_one[:, part * 5 + t, :] = spread[part * 128 : (part + 1) * 128, t * 128 : (t + 1) * 128]

    pl.semaphore_wait(barrier, ND - 1)

    def exchange(out_ref, in_ref, s):
        def one(d, carry):
            at, device = peer(d)
            pltpu.make_async_remote_copy(
                src_ref=out_ref.at[at],
                dst_ref=in_ref.at[me],
                send_sem=send_sem.at[s],
                recv_sem=recv_sem.at[s],
                device_id=device,
                device_id_type=MESH,
            ).start()
            return carry

        lax.fori_loop(1, ND, one, 0)
        in_ref[me] = out_ref[me]

    def settle(out_ref, in_ref, s):
        whole = pltpu.make_async_remote_copy(
            src_ref=out_ref.at[pl.ds(0, ND - 1)],
            dst_ref=in_ref.at[pl.ds(0, ND - 1)],
            send_sem=send_sem.at[s],
            recv_sem=recv_sem.at[s],
            device_id=peer(1)[1],
            device_id_type=MESH,
        )
        whole.wait_send()
        whole.wait_recv()

    exchange(out_one, in_one, 0)

    blend(1, wz, sx)
    blend(2, sz, wx)
    wave_ref[:, 256:] = mm3(dft_y, split(wave_ref[:, 256:]))

    def build(z, carry):
        cz = fac_z_ref[0, pl.ds(z, 1), :]
        zz = fac_z_ref[1, pl.ds(z, 1), :]
        cx, xx = fac_x_ref[0], fac_x_ref[1]
        rows = pl.ds(pl.multiple_of(z * TX, 8), TX)
        for at, value in enumerate((cx * cz - xx * zz, xx * cz + cx * zz)):
            high, low = split(value)
            tab_ref[at, 0, rows, :] = high
            tab_ref[at, 1, rows, :] = low
        return carry

    lax.fori_loop(0, 16, build, 0)

    def tile_tables():
        return [(tab_ref[at, 0], tab_ref[at, 1]) for at in range(2)]


    def influence(at, weight):
        total = green_ref[1] + column_ref[1, at]
        inverse = jnp.where(total == 0.0, 0.0, 1.0 / jnp.where(total == 0.0, 1.0, total))
        return green_ref[0] * (inverse * (column_ref[0, at] * weight))

    first = me == 0
    weight = jnp.where(first, 1.0, 2.0)
    plane_ref[2] = influence(me, weight)
    plane_ref[3] = influence(jnp.where(first, 128, me), weight)
    settle(out_one, in_one, 0)

    def gathered(in_ref):
        return jnp.concatenate(
            [
                jnp.concatenate([in_ref[:, part * 5 + t, :] for t in range(5)], axis=1)
                for part in range(2)
            ],
            axis=0,
        )

    tiles = gathered(in_one)
    bricks = mm3((dft_b_ref[0], dft_b_ref[1]), split(tiles))
    real, imag = bricks[:128], bricks[128:]
    cos_t, sin_t = twiddle_ref[0], twiddle_ref[1]
    turned = jnp.concatenate(
        [real * cos_t + imag * sin_t, imag * cos_t - real * sin_t], axis=0
    )
    turned = jnp.concatenate(
        [turned[:, :128] + turned[:, FOLD:], turned[:, 128:FOLD]], axis=1
    )
    turned = split(turned)
    cos_e, sin_e = tile_tables()
    by_cos = mm3(turned, cos_e)
    by_sin = mm3(turned, sin_e)
    plane_ref[0] = by_cos[:128] + by_sin[128:]
    plane_ref[1] = by_cos[128:] - by_sin[:128]

    def inverse(at):
        cos_e, sin_e = tile_tables()
        green = plane_ref[at]
        modes = split(jnp.concatenate([green * plane_ref[0], green * plane_ref[1]], axis=0))
        by_cos = mm3(modes, cos_e, NT)
        by_sin = mm3(modes, sin_e, NT)
        real = by_cos[:128] - by_sin[128:]
        imag = by_sin[:128] + by_cos[128:]
        real = jnp.concatenate([real, real[:, :128]], axis=1)
        imag = jnp.concatenate([imag, imag[:, :128]], axis=1)
        cos_t, sin_t = twiddle_ref[0], twiddle_ref[1]
        real, imag = real * cos_t - imag * sin_t, imag * cos_t + real * sin_t
        return split(jnp.concatenate([real, -imag], axis=0))

    @pl.when(me != 0)
    def _():
        both = mm3((dft_b_ref[0], dft_b_ref[1]), inverse(2))
        field_ref[0] = both[:128]
        field_ref[1] = -both[128:]

    @pl.when(me == 0)
    def _():
        field_ref[0] = mm3((dft_b_ref[0, :128], dft_b_ref[1, :128]), inverse(2))
        field_ref[1] = -mm3((dft_b_ref[0, 128:], dft_b_ref[1, 128:]), inverse(3))

    field_r, field_i = field_ref[0], field_ref[1]
    partial = jnp.sum(tiles[:128] * field_r + tiles[128:] * field_i, keepdims=True)
    partial = partial * (0.5 / (ND * ATOMS))
    lane = iota((ND, 128), 1)
    for t in range(5):
        piece = field_r[:, t * 128 : (t + 1) * 128]
        if t == 4:
            piece = jnp.where(lane == 127, partial, piece)
        out_two[:, t, :] = piece
        out_two[:, 5 + t, :] = field_i[:, t * 128 : (t + 1) * 128]

    def place(c, i):
        step = c * 2 + i // NN
        w = lax.rem(wide + step, NW)
        n = lax.rem(narrow + lax.rem(i, NN), NN)
        return w * NN + n, (w, n)

    for c in range(4):

        def one(i, carry):
            at, device = place(c, i)
            pltpu.make_async_remote_copy(
                src_ref=out_two.at[at],
                dst_ref=in_two.at[me],
                send_sem=send_sem.at[1],
                recv_sem=recv_sem.at[1 + c],
                device_id=device,
                device_id_type=MESH,
            ).start()
            return carry

        lax.fori_loop(1 if c == 0 else 0, 32, one, 0)
    in_two[me] = out_two[me]
    mix = (mix_ref[0], mix_ref[1])
    rows = [jnp.zeros((1, 256), F32)] * 4
    total = jnp.zeros((1, 1), F32)
    for c in range(4):
        size = 31 if c == 0 else 32
        pltpu.make_async_remote_copy(
            src_ref=out_two.at[pl.ds(0, size)],
            dst_ref=in_two.at[pl.ds(0, size)],
            send_sem=send_sem.at[1],
            recv_sem=recv_sem.at[1 + c],
            device_id=peer(1)[1],
            device_id_type=MESH,
        ).wait_recv()
        spans = [lax.rem(wide + (NW - 2 * c - i), NW) * NN for i in range(2)]
        spans = [pl.ds(pl.multiple_of(at, NN), NN) for at in spans]
        lower = [pl.ds(pl.multiple_of(at.start + ND, NN), NN) for at in spans]
        planes = jnp.concatenate(
            [
                jnp.concatenate([in_two[at, part * 5 + t, :] for t in range(5)], axis=1)
                for part in range(2)
                for at in spans
            ],
            axis=0,
        )
        inner = mm3(split(planes), mix)
        wave = jnp.concatenate([wave_ref[at, :] for at in spans + lower], axis=0)
        wave, wave_slope = wave[:, :256], wave[:, 256:]
        parts = [
            wave * inner[:, :256],
            -wave * inner[:, 256:512],
            -wave_slope * inner[:, :256],
            -wave * inner[:, 512:],
        ]
        rows = [r + jnp.sum(p, axis=0, keepdims=True) for r, p in zip(rows, parts)]
        total = total + jnp.sum(planes[:32, TILE - 1 : TILE], axis=0, keepdims=True)
    pltpu.make_async_remote_copy(
        src_ref=out_two.at[pl.ds(0, ND - 1)],
        dst_ref=in_two.at[pl.ds(0, ND - 1)],
        send_sem=send_sem.at[1],
        recv_sem=recv_sem.at[1],
        device_id=peer(1)[1],
        device_id_type=MESH,
    ).wait_send()
    atom = [r[:, :128] for r in rows]
    centroid = [r[:, 128:] * oxygen for r in rows]
    result_ref[8:24, :] = jnp.concatenate(
        atom + centroid + [jnp.broadcast_to(total, (8, ATOMS))], axis=0
    )


def deal_kernel(result_ref, dipole_ref, atom_ref, centroid_ref, energy_ref):
    for c in range(3):
        dipole_ref[c, 0, 0] = result_ref[c : c + 1, :]
    for c in range(4):
        atom_ref[c, 0, 0] = result_ref[8 + c : 9 + c, :]
        centroid_ref[c, 0, 0] = result_ref[12 + c : 13 + c, :]
    energy_ref[...] = result_ref[16:17, 0:1]


def local(
    positions,
    species,
    neighbours,
    e1w,
    e1b,
    e2w,
    e2b,
    e3w,
    e3b,
    f1w,
    f1b,
    f2w,
    f2b,
    f3w,
    f3b,
    fow,
):
    ghosts = halo(positions, species)
    *late, column = [jnp.asarray(t) for t in tables()]
    vmem = pl.BlockSpec(memory_space=pltpu.VMEM)
    anywhere = pl.BlockSpec(memory_space=pl.ANY)
    row = lambda x: x.reshape(1, -1)
    result = pl.pallas_call(
        main_kernel,
        out_shape=jax.ShapeDtypeStruct((24, ATOMS), F32),
        in_specs=[pl.BlockSpec(memory_space=pltpu.SMEM)] + [anywhere] * (len(EARLY) + len(LATE)),
        out_specs=vmem,
        scratch_shapes=[pltpu.VMEM(shape, dtype) for shape, dtype in EARLY + LATE]
        + [
            pltpu.VMEM((36, 8, ATOMS), F32),
            pltpu.VMEM((3, ATOMS, ATOMS), F32),
            pltpu.VMEM((4, ATOMS, ATOMS), F32),
            pltpu.VMEM((2, TILE, 768), BF16),
            pltpu.VMEM((CY, 512), F32),
            pltpu.VMEM((2, 2, FOLD, MODES), BF16),
            pltpu.VMEM((4, ND, MODES), F32),
            pltpu.VMEM((2, ND, TILE), F32),
            pltpu.VMEM((ND, ROWS, 128), F32),
            pltpu.VMEM((ND, ROWS, 128), F32),
            pltpu.VMEM((ND, ROWS, 128), F32),
            pltpu.VMEM((ND, ROWS, 128), F32),
            pltpu.SemaphoreType.DMA((len(EARLY) + len(LATE),)),
            pltpu.SemaphoreType.DMA((2,)),
            pltpu.SemaphoreType.DMA((5,)),
        ],
        compiler_params=pltpu.CompilerParams(
            collective_id=1, has_side_effects=True, vmem_limit_bytes=58 << 20
        ),
        name="main",
    )(
        column,
        ghosts,
        neighbours.reshape(ATOMS, ATOMS),
        e1w,
        e1b,
        e2w,
        row(e2b),
        e3w,
        row(e3b),
        row(f1b),
        row(f2b),
        row(f3b),
        f1w.T,
        f2w,
        f3w,
        fow.T,
        *late,
    )
    dipole, atom, centroid, energy = pl.pallas_call(
        deal_kernel,
        out_shape=(
            jax.ShapeDtypeStruct((3, 1, 1, 1, ATOMS), F32),
            jax.ShapeDtypeStruct((4, 1, 1, 1, ATOMS), F32),
            jax.ShapeDtypeStruct((4, 1, 1, 1, ATOMS), F32),
            jax.ShapeDtypeStruct((1, 1), F32),
        ),
        in_specs=[vmem],
        out_specs=(vmem,) * 4,
        name="deal",
    )(result)
    return dipole, atom, centroid, energy.reshape(())


def solution(mesh):
    return jax.shard_map(
        local,
        mesh=mesh,
        in_specs=(
            P(None, "wide", "narrow", None, None),
            P("wide", "narrow", None, None),
            P("wide", "narrow", None, None, None),
        )
        + (P(),) * 13,
        out_specs=(
            P(None, "wide", "narrow", None, None),
            P(None, "wide", "narrow", None, None),
            P(None, "wide", "narrow", None, None),
            P(),
        ),
        check_vma=False,
    )
```

```python
import functools
import math

import jax
import jax.numpy as jnp
import numpy as np
from jax import lax
from jax.experimental import pallas as pl
from jax.experimental.pallas import tpu as pltpu
from jax.sharding import PartitionSpec as P

NW, NN = 8, 16
ND = NW * NN
CX, CY, CZ = 32, 256, 16
TX, TZ = 32, 19
TILE = 640
FOLD = 512
ROWS = 10
SIDE = 4
UNROLL = 2
MODES = 512
ATOMS = 128
F32 = jnp.float32
BF16 = jnp.bfloat16
MESH = pl.DeviceIdType.MESH
HIGHEST = lax.Precision.HIGHEST
NT = (((1,), (1,)), ((), ()))
NNN = (((1,), (0,)), ((), ()))


def split(x):
    high = x.astype(BF16)
    return high, (x - high.astype(F32)).astype(BF16)


def mm(a, b, dims=NNN):
    return lax.dot_general(a, b, dims, preferred_element_type=F32)


def mm3(a, b, dims=NNN):
    return mm(a[0], b[0], dims) + mm(a[0], b[1], dims) + mm(a[1], b[0], dims)


def exact(a, b, dims=NNN):
    return lax.dot_general(a, b, dims, precision=HIGHEST, preferred_element_type=F32)


def iota(shape, dim):
    return lax.broadcasted_iota(jnp.int32, shape, dim)


def spline(offset):
    from_middle = offset - 2.0
    away = jnp.abs(from_middle)
    outer = jnp.maximum(2.0 - away, 0.0)
    inner = jnp.maximum(1.0 - away, 0.0)
    outer_square, inner_square = outer * outer, inner * inner
    value = (outer_square * outer - 4.0 * (inner_square * inner)) * (1.0 / 6.0)
    fall = 0.5 * outer_square - 2.0 * inner_square
    return value, jnp.where(from_middle > 0.0, -fall, fall)


def halo_kernel(positions_ref, species_ref, ghost_ref, own_ref, send_sem, recv_sem):
    wide = lax.axis_index("wide")
    narrow = lax.axis_index("narrow")
    steps = [(sx, sz) for sx in range(3) for sz in range(3) if (sx, sz) != (1, 1)]
    barrier = pltpu.get_barrier_semaphore()

    def device(sx, sz):
        return (lax.rem(wide + (NW + 1 - sx), NW), lax.rem(narrow + (NN + 1 - sz), NN))

    own_ref[...] = jnp.concatenate(
        [positions_ref[c, 0, 0] for c in range(3)]
        + [species_ref[0, 0].astype(F32), jnp.zeros((4, ATOMS), F32)],
        axis=0,
    )
    ghost_ref[4] = own_ref[...]
    for sx, sz in steps:
        pl.semaphore_signal(barrier, inc=1, device_id=device(sx, sz), device_id_type=MESH)
    pl.semaphore_wait(barrier, len(steps))
    copies = []
    for at, (sx, sz) in enumerate(steps):
        copy = pltpu.make_async_remote_copy(
            src_ref=own_ref,
            dst_ref=ghost_ref.at[sx * 3 + sz],
            send_sem=send_sem.at[at],
            recv_sem=recv_sem.at[at],
            device_id=device(sx, sz),
            device_id_type=MESH,
        )
        copy.start()
        copies.append(copy)
    for copy in copies:
        copy.wait()


def halo(positions, species):
    vmem = pl.BlockSpec(memory_space=pltpu.VMEM)
    return pl.pallas_call(
        halo_kernel,
        out_shape=jax.ShapeDtypeStruct((9, 8, ATOMS), F32),
        in_specs=[vmem, vmem],
        out_specs=vmem,
        scratch_shapes=[
            pltpu.VMEM((8, ATOMS), F32),
            pltpu.SemaphoreType.DMA((8,)),
            pltpu.SemaphoreType.DMA((8,)),
        ],
        compiler_params=pltpu.CompilerParams(collective_id=0, has_side_effects=True),
        name="halo",
    )(positions, species)


def spread_rows(rows, count):
    r = iota((rows, count), 0)
    c = iota((rows, count), 1)
    i = r & 31
    return jnp.where((i < 25) & (c == (r >> 5) * 25 + i), 1.0, 0.0).astype(F32)


def network(
    ghost_ref,
    near_ref,
    e1w_ref,
    e1b_ref,
    e2w_ref,
    e2b_ref,
    e3w_ref,
    e3b_ref,
    f1b_ref,
    f2b_ref,
    f3b_ref,
    f1w_ref,
    f2w_ref,
    f3w_ref,
    fow_ref,
    table_ref,
    own_ref,
    mat_ref,
    arrived,
):
    extent = (float(CX), float(CY), float(CZ))
    for k in range(9):
        shift = (float(k // 3 - 1), 0.0, float(k % 3 - 1))
        for c in range(3):
            table_ref[k * 4 + c] = jnp.broadcast_to(ghost_ref[k, c : c + 1, :] + shift[c], (8, ATOMS))
        table_ref[k * 4 + 3] = jnp.broadcast_to(ghost_ref[k, 3:4, :], (8, ATOMS))
    for c in range(3):
        own_ref[c] = jnp.broadcast_to(ghost_ref[4, c : c + 1, :], (ATOMS, ATOMS)).T

    pick1 = spread_rows(32, 25)
    pick2 = spread_rows(64, 50)
    pick3 = spread_rows(128, 100)

    def column(pick, row):
        return exact(pick, jnp.broadcast_to(row, (ATOMS, row.shape[1])), NT)

    w_oxygen = column(pick1, e1w_ref[0:1, :])
    w_hydrogen = column(pick1, e1w_ref[1:2, :])
    b_oxygen = column(pick1, e1b_ref[0:1, :])
    b_hydrogen = column(pick1, e1b_ref[1:2, :])
    bias2 = column(pick2, e2b_ref[...])
    bias3 = column(pick3, e3b_ref[...])
    w2 = exact(pick2, exact(pick1, e2w_ref[...]), NT)
    w3 = exact(pick3, exact(pick2, e3w_ref[...]), NT)
    last = iota((32, ATOMS), 0) == 31
    b_oxygen = jnp.where(last, 20.0, b_oxygen)
    b_hydrogen = jnp.where(last, 20.0, b_hydrogen)
    w2 = jnp.where(iota((64, 32), 1) == 31, bias2[:, :32], w2)
    w3 = jnp.where(iota((128, 64), 1) == 31, bias3[:, :64], w3)
    w2_high, w2_low = split(w2)
    w3_high, w3_low = split(w3)
    w2_all = jnp.concatenate([w2_high, w2_high, w2_low], axis=1)
    w3_all = jnp.concatenate([w3_high, w3_high, w3_low], axis=1)
    sublane = iota((8, ATOMS), 0)

    def geometry(g):
        rows = pl.ds(pl.multiple_of(g * 8, 8), 8)
        code = near_ref[rows, :]
        slot = code & 127
        offset = code >> 7
        brick = (offset * 11) >> 5
        step_y = (offset - 3 * brick - 1).astype(F32)
        parts = [jnp.zeros((8, ATOMS), F32)] * 4
        for k in range(9):
            here = brick == k
            for c in range(4):
                found = jnp.take_along_axis(table_ref[k * 4 + c], slot, axis=1)
                parts[c] = jnp.where(here, found, parts[c])
        parts[1] = parts[1] + step_y
        scaled = [(parts[c] - own_ref[c, rows, :]) * (extent[c] / 24.0) for c in range(3)]
        square = scaled[0] * scaled[0] + scaled[1] * scaled[1] + scaled[2] * scaled[2]
        smooth = 1.0 / (1.0 + square)
        scale = smooth * (1.0 / 128.0)
        return rows, smooth, parts[3], [scale] + [scale * scaled[c] for c in range(3)]

    def group(g, carry):
        sets = [geometry(g * SIDE + i) for i in range(SIDE)]
        pieces = []
        for _, smooth, kind, _ in sets:
            for b in range(8):
                s = jnp.broadcast_to(smooth[b : b + 1, :], (32, ATOMS))
                h = jnp.broadcast_to(kind[b : b + 1, :], (32, ATOMS)) > 0.5
                pieces.append(
                    jnp.where(h, w_hydrogen, w_oxygen) * s + jnp.where(h, b_hydrogen, b_oxygen)
                )
        one = jnp.tanh(jnp.concatenate(pieces, axis=1))
        high, low = split(one)
        two = jnp.tanh(mm(w2_all, jnp.concatenate([high, low, high], axis=0)))
        two = two + jnp.concatenate([one, one], axis=0)
        high, low = split(two)
        three = jnp.tanh(mm(w3_all, jnp.concatenate([high, low, high], axis=0)))
        three = three + jnp.concatenate([two, two], axis=0)
        high, low = split(three)
        for i, (rows, _, _, radial) in enumerate(sets):
            blocks = [
                jnp.concatenate([jnp.where(sublane == b, r, 0.0) for r in radial], axis=0)
                for b in range(8)
            ]
            r_high, r_low = split(jnp.concatenate(blocks, axis=1))
            mine = high[:, i * 1024 : (i + 1) * 1024]
            both = mm(jnp.concatenate([r_high, r_low], axis=0), mine, NT)
            found = (both[:32] + both[32:]) + mm(r_high, low[:, i * 1024 : (i + 1) * 1024], NT)
            for p in range(4):
                mat_ref[p, rows, :] = found[p * 8 : (p + 1) * 8]
        return carry

    lax.fori_loop(0, ATOMS // 8 // SIDE, group, 0, unroll=UNROLL)

    lane = iota((ATOMS, ATOMS), 1)
    entries = None
    matrix = [mat_ref[p] for p in range(4)]
    for p in range(4):
        tiled = jnp.take_along_axis(matrix[p], lane & 15, axis=1)
        term = []
        for t in range(13):
            d = jnp.minimum((lane >> 4) + 8 * t, 99)
            block = (d * 41) >> 10
            term.append(jnp.take_along_axis(matrix[p], d + 7 * block, axis=1) * tiled)
        term = jnp.concatenate(term, axis=1)
        entries = term if entries is None else entries + term
    arrived()
    hidden = mm3(split(entries[:, :1600]), split(f1w_ref[...]), NT)
    hidden = jnp.tanh(hidden + f1b_ref[...])
    hidden = hidden + jnp.tanh(mm3(split(hidden), split(f2w_ref[...])) + f2b_ref[...])
    hidden = hidden + jnp.tanh(mm3(split(hidden), split(f3w_ref[...])) + f3b_ref[...])
    coeffs = mm3(split(hidden), split(exact(pick3, fow_ref[...])), NT)
    result = jnp.zeros((ATOMS, ATOMS), F32)
    for c in range(3):
        total = jnp.sum(coeffs * matrix[1 + c], axis=1, keepdims=True)
        result = jnp.where(lane == c, total, result)
    return result.T[:8]


def np_split(x):
    x = np.asarray(x, np.float32)
    high = x.astype(jnp.bfloat16)
    low = (x - high.astype(np.float32)).astype(jnp.bfloat16)
    return np.stack([high, low])


@functools.lru_cache(None)
def tables():
    m = np.arange(128)[:, None]
    y = np.arange(CY)[None, :]
    angle = 2 * np.pi * (m * y % CY) / CY
    lower = -np.sin(angle)
    lower[0] = 1 - 2 * (y[0] % 2)
    dft_y = np_split(np.concatenate([np.cos(angle), lower]))
    j, k = np.divmod(np.arange(ND), NN)
    phi = 2 * np.pi * ((2 * j[:, None] * j[None] + k[:, None] * k[None]) % 16) / 16
    cos, sin = np.cos(phi), np.sin(phi)
    dft_b = np_split(np.block([[cos, sin], [-sin, cos]]))
    z, x = np.divmod(np.arange(TILE), TX)
    turn = 2 * np.pi * ((j[:, None] * (x - 1)[None] + k[:, None] * (z - 3)[None]) % 256) / 256
    twiddle = np.stack([np.cos(turn), np.sin(turn)]).astype(np.float32)
    v, u = np.divmod(np.arange(MODES), 32)
    ax = 2 * np.pi * ((np.arange(TX)[:, None] - 1) * u[None] % 32) / 32
    az = 2 * np.pi * ((np.arange(16)[:, None] - 3) * v[None] % 16) / 16
    fac_x = np.stack([np.cos(ax), np.sin(ax)]).astype(np.float32)
    fac_z = np.stack([np.cos(az), np.sin(az)]).astype(np.float32)

    def fold(i, n):
        return np.where(2 * i >= n, i - n, i) / n

    def modulus(i, n):
        return 36.0 / (4 + 2 * np.cos(2 * np.pi * i / n)) ** 2

    def decay(f):
        return np.exp(-np.pi**2 * f * f / 0.81)

    mx = j[:, None] + 8 * u[None]
    mz = k[:, None] + 16 * v[None]
    fx, fz = fold(mx, 256), fold(mz, 256)
    scale = 0.25 / (np.pi * 256.0**3)
    plane = scale * decay(fx) * decay(fz) * modulus(mx, 256) * modulus(mz, 256)
    green = np.stack([plane, fx * fx + fz * fz]).astype(np.float32)
    my = np.arange(129)
    fy = fold(my, 256)
    column = np.stack([decay(fy) * modulus(my, 256), fy * fy]).astype(np.float32)
    return dft_y, dft_b, twiddle, fac_x, fac_z, green, column


EARLY = (
    ((9, 8, ATOMS), F32),
    ((ATOMS, ATOMS), jnp.int32),
    ((2, 25), F32),
    ((2, 25), F32),
    ((25, 50), F32),
    ((1, 50), F32),
    ((50, 100), F32),
    ((1, 100), F32),
    ((1, 240), F32),
    ((1, 240), F32),
    ((1, 240), F32),
)
LATE = (
    ((240, 1600), F32),
    ((240, 240), F32),
    ((240, 240), F32),
    ((100, 240), F32),
    ((2, 256, CY), BF16),
    ((2, 256, 256), BF16),
    ((2, ND, TILE), F32),
    ((2, TX, MODES), F32),
    ((2, 16, MODES), F32),
    ((2, ND, MODES), F32),
)


def main_kernel(*refs):
    count = len(EARLY) + len(LATE)
    column_ref = refs[0]
    far = refs[1 : 1 + count]
    result_ref = refs[1 + count]
    near = refs[2 + count : 2 + 2 * count]
    (
        ghost_ref,
        near_ref,
        e1w_ref,
        e1b_ref,
        e2w_ref,
        e2b_ref,
        e3w_ref,
        e3b_ref,
        f1b_ref,
        f2b_ref,
        f3b_ref,
    ) = near[: len(EARLY)]
    (
        table_ref,
        home_ref,
        mat_ref,
        mix_ref,
        wave_ref,
        tab_ref,
        plane_ref,
        field_ref,
        out_one,
        in_one,
        out_two,
        in_two,
        late_sem,
        send_sem,
        recv_sem,
    ) = refs[2 + 2 * count :]
    f1w_ref, f2w_ref, f3w_ref, fow_ref = near[len(EARLY) : len(EARLY) + 4]
    dft_y_ref, dft_b_ref, twiddle_ref, fac_x_ref, fac_z_ref, green_ref = near[len(EARLY) + 4 :]
    fetch = [pltpu.make_async_copy(far[i], near[i], late_sem.at[i]) for i in range(count)]
    for copy in fetch:
        copy.start()
    wide = lax.axis_index("wide")
    narrow = lax.axis_index("narrow")
    me = wide * NN + narrow
    barrier = pltpu.get_barrier_semaphore()

    def everyone(act):
        def close(i, carry):
            act(0, i + 1)
            return carry

        def distant(i, carry):
            act(1 + i // NN, lax.rem(i, NN))
            return carry

        lax.fori_loop(0, NN - 1, close, 0, unroll=5)
        lax.fori_loop(0, (NW - 1) * NN, distant, 0, unroll=8)

    def device(step_w, step_n):
        return lax.rem(wide + step_w, NW), lax.rem(narrow + step_n, NN)

    def greet(step_w, step_n):
        pl.semaphore_signal(
            barrier, inc=1, device_id=device(step_w, step_n), device_id_type=MESH
        )

    everyone(greet)

    def arrived():
        for copy in fetch[len(EARLY) :]:
            copy.wait()

    for copy in fetch[: len(EARLY)]:
        copy.wait()
    dip = network(
        ghost_ref,
        near_ref,
        e1w_ref,
        e1b_ref,
        e2w_ref,
        e2b_ref,
        e3w_ref,
        e3b_ref,
        f1b_ref,
        f2b_ref,
        f3b_ref,
        f1w_ref,
        f2w_ref,
        f3w_ref,
        fow_ref,
        table_ref,
        home_ref,
        mat_ref,
        arrived,
    )

    kind = ghost_ref[4, 3:4, :]
    oxygen = 1.0 - kind
    result_ref[0:8, :] = dip * oxygen
    shift = 0.5 * jnp.tanh(dip)

    def sites(c, extent):
        atom = ghost_ref[4, c : c + 1, :] * float(extent)
        return jnp.concatenate([atom, atom + shift[c : c + 1, :]], axis=1)

    charge = jnp.concatenate([6.0 * oxygen + kind, -8.0 * oxygen], axis=1)
    off_x = sites(0, CX) - (iota((TX, 256), 0).astype(F32) - 1.0)
    off_z = sites(2, CZ) - (iota((24, 256), 0).astype(F32) - 3.0)
    off_y = sites(1, CY) - iota((CY, 256), 0).astype(F32)
    wx, sx = spline(off_x)
    wz, sz = spline(off_z)
    wy, sy = spline(off_y)
    dft_y = (dft_y_ref[0], dft_y_ref[1])
    wave = mm3(dft_y, split(wy))
    wave_ref[:, :256] = wave
    wave_ref[:, 256:] = sy
    rest = jnp.zeros((TILE - TX * TZ, 256), F32)

    def blend(at, left, right):
        full = jnp.concatenate([left[z : z + 1, :] * right for z in range(TZ)] + [rest], axis=0)
        high, low = split(full)
        mix_ref[0, :, at * 256 : (at + 1) * 256] = high
        mix_ref[1, :, at * 256 : (at + 1) * 256] = low
        return high, low

    spread = mm3(split(wave * charge), blend(0, wz, wx), NT)
    for part in range(2):
        for t in range(5):
            out_one[:, part * 5 + t, :] = spread[part * 128 : (part + 1) * 128, t * 128 : (t + 1) * 128]

    pl.semaphore_wait(barrier, ND - 1)

    def exchange(out_ref, in_ref, s, slot):
        def one(step_w, step_n):
            w, n = device(step_w, step_n)
            pltpu.make_async_remote_copy(
                src_ref=out_ref.at[w * NN + n],
                dst_ref=in_ref.at[me],
                send_sem=send_sem.at[s],
                recv_sem=recv_sem.at[slot(step_w)],
                device_id=(w, n),
                device_id_type=MESH,
            ).start()

        everyone(one)
        in_ref[me] = out_ref[me]

    def settle(out_ref, in_ref, s):
        whole = pltpu.make_async_remote_copy(
            src_ref=out_ref.at[pl.ds(0, ND - 1)],
            dst_ref=in_ref.at[pl.ds(0, ND - 1)],
            send_sem=send_sem.at[s],
            recv_sem=recv_sem.at[s],
            device_id=device(0, 1),
            device_id_type=MESH,
        )
        whole.wait_send()
        whole.wait_recv()

    exchange(out_one, in_one, 0, lambda step_w: 0)

    blend(1, wz, sx)
    blend(2, sz, wx)
    wave_ref[:, 256:] = mm3(dft_y, split(wave_ref[:, 256:]))

    def build(z, carry):
        cz = fac_z_ref[0, pl.ds(z, 1), :]
        zz = fac_z_ref[1, pl.ds(z, 1), :]
        cx, xx = fac_x_ref[0], fac_x_ref[1]
        rows = pl.ds(pl.multiple_of(z * TX, 8), TX)
        for at, value in enumerate((cx * cz - xx * zz, xx * cz + cx * zz)):
            high, low = split(value)
            tab_ref[at, 0, rows, :] = high
            tab_ref[at, 1, rows, :] = low
        return carry

    lax.fori_loop(0, 16, build, 0)

    def tile_tables():
        return [(tab_ref[at, 0], tab_ref[at, 1]) for at in range(2)]


    def influence(at, weight):
        total = green_ref[1] + column_ref[1, at]
        inverse = jnp.where(total == 0.0, 0.0, 1.0 / jnp.where(total == 0.0, 1.0, total))
        return green_ref[0] * (inverse * (column_ref[0, at] * weight))

    first = me == 0
    weight = jnp.where(first, 1.0, 2.0)
    plane_ref[2] = influence(me, weight)
    plane_ref[3] = influence(jnp.where(first, 128, me), weight)
    settle(out_one, in_one, 0)

    def gathered(in_ref):
        return jnp.concatenate(
            [
                jnp.concatenate([in_ref[:, part * 5 + t, :] for t in range(5)], axis=1)
                for part in range(2)
            ],
            axis=0,
        )

    tiles = gathered(in_one)
    bricks = mm3((dft_b_ref[0], dft_b_ref[1]), split(tiles))
    real, imag = bricks[:128], bricks[128:]
    cos_t, sin_t = twiddle_ref[0], twiddle_ref[1]
    turned = jnp.concatenate(
        [real * cos_t + imag * sin_t, imag * cos_t - real * sin_t], axis=0
    )
    turned = jnp.concatenate(
        [turned[:, :128] + turned[:, FOLD:], turned[:, 128:FOLD]], axis=1
    )
    turned = split(turned)
    cos_e, sin_e = tile_tables()
    by_cos = mm3(turned, cos_e)
    by_sin = mm3(turned, sin_e)
    plane_ref[0] = by_cos[:128] + by_sin[128:]
    plane_ref[1] = by_cos[128:] - by_sin[:128]

    def inverse(at):
        cos_e, sin_e = tile_tables()
        green = plane_ref[at]
        modes = split(jnp.concatenate([green * plane_ref[0], green * plane_ref[1]], axis=0))
        by_cos = mm3(modes, cos_e, NT)
        by_sin = mm3(modes, sin_e, NT)
        real = by_cos[:128] - by_sin[128:]
        imag = by_sin[:128] + by_cos[128:]
        real = jnp.concatenate([real, real[:, :128]], axis=1)
        imag = jnp.concatenate([imag, imag[:, :128]], axis=1)
        cos_t, sin_t = twiddle_ref[0], twiddle_ref[1]
        real, imag = real * cos_t - imag * sin_t, imag * cos_t + real * sin_t
        return split(jnp.concatenate([real, -imag], axis=0))

    @pl.when(me != 0)
    def _():
        both = mm3((dft_b_ref[0], dft_b_ref[1]), inverse(2))
        field_ref[0] = both[:128]
        field_ref[1] = -both[128:]

    @pl.when(me == 0)
    def _():
        field_ref[0] = mm3((dft_b_ref[0, :128], dft_b_ref[1, :128]), inverse(2))
        field_ref[1] = -mm3((dft_b_ref[0, 128:], dft_b_ref[1, 128:]), inverse(3))

    field_r, field_i = field_ref[0], field_ref[1]
    partial = jnp.sum(tiles[:128] * field_r + tiles[128:] * field_i, keepdims=True)
    partial = partial * (0.5 / (ND * ATOMS))
    lane = iota((ND, 128), 1)
    for t in range(5):
        piece = field_r[:, t * 128 : (t + 1) * 128]
        if t == 4:
            piece = jnp.where(lane == 127, partial, piece)
        out_two[:, t, :] = piece
        out_two[:, 5 + t, :] = field_i[:, t * 128 : (t + 1) * 128]

    exchange(out_two, in_two, 1, lambda step_w: 1 + step_w // 2)
    mix = (mix_ref[0], mix_ref[1])
    rows = [jnp.zeros((1, 256), F32)] * 4
    total = jnp.zeros((1, 1), F32)
    for c in range(4):
        size = 31 if c == 0 else 32
        pltpu.make_async_remote_copy(
            src_ref=out_two.at[pl.ds(0, size)],
            dst_ref=in_two.at[pl.ds(0, size)],
            send_sem=send_sem.at[1],
            recv_sem=recv_sem.at[1 + c],
            device_id=device(0, 1),
            device_id_type=MESH,
        ).wait_recv()
        spans = [lax.rem(wide + (NW - 2 * c - i), NW) * NN for i in range(2)]
        spans = [pl.ds(pl.multiple_of(at, NN), NN) for at in spans]
        lower = [pl.ds(pl.multiple_of(at.start + ND, NN), NN) for at in spans]
        planes = jnp.concatenate(
            [
                jnp.concatenate([in_two[at, part * 5 + t, :] for t in range(5)], axis=1)
                for part in range(2)
                for at in spans
            ],
            axis=0,
        )
        inner = mm3(split(planes), mix)
        wave = jnp.concatenate([wave_ref[at, :] for at in spans + lower], axis=0)
        wave, wave_slope = wave[:, :256], wave[:, 256:]
        parts = [
            wave * inner[:, :256],
            -wave * inner[:, 256:512],
            -wave_slope * inner[:, :256],
            -wave * inner[:, 512:],
        ]
        rows = [r + jnp.sum(p, axis=0, keepdims=True) for r, p in zip(rows, parts)]
        total = total + jnp.sum(planes[:32, TILE - 1 : TILE], axis=0, keepdims=True)
    pltpu.make_async_remote_copy(
        src_ref=out_two.at[pl.ds(0, ND - 1)],
        dst_ref=in_two.at[pl.ds(0, ND - 1)],
        send_sem=send_sem.at[1],
        recv_sem=recv_sem.at[1],
        device_id=device(0, 1),
        device_id_type=MESH,
    ).wait_send()
    atom = [r[:, :128] for r in rows]
    centroid = [r[:, 128:] * oxygen for r in rows]
    result_ref[8:24, :] = jnp.concatenate(
        atom + centroid + [jnp.broadcast_to(total, (8, ATOMS))], axis=0
    )


def deal_kernel(result_ref, dipole_ref, atom_ref, centroid_ref, energy_ref):
    for c in range(3):
        dipole_ref[c, 0, 0] = result_ref[c : c + 1, :]
    for c in range(4):
        atom_ref[c, 0, 0] = result_ref[8 + c : 9 + c, :]
        centroid_ref[c, 0, 0] = result_ref[12 + c : 13 + c, :]
    energy_ref[...] = result_ref[16:17, 0:1]


def local(
    positions,
    species,
    neighbours,
    e1w,
    e1b,
    e2w,
    e2b,
    e3w,
    e3b,
    f1w,
    f1b,
    f2w,
    f2b,
    f3w,
    f3b,
    fow,
):
    ghosts = halo(positions, species)
    *late, column = [jnp.asarray(t) for t in tables()]
    vmem = pl.BlockSpec(memory_space=pltpu.VMEM)
    anywhere = pl.BlockSpec(memory_space=pl.ANY)
    row = lambda x: x.reshape(1, -1)
    result = pl.pallas_call(
        main_kernel,
        out_shape=jax.ShapeDtypeStruct((24, ATOMS), F32),
        in_specs=[pl.BlockSpec(memory_space=pltpu.SMEM)] + [anywhere] * (len(EARLY) + len(LATE)),
        out_specs=vmem,
        scratch_shapes=[pltpu.VMEM(shape, dtype) for shape, dtype in EARLY + LATE]
        + [
            pltpu.VMEM((36, 8, ATOMS), F32),
            pltpu.VMEM((3, ATOMS, ATOMS), F32),
            pltpu.VMEM((4, ATOMS, ATOMS), F32),
            pltpu.VMEM((2, TILE, 768), BF16),
            pltpu.VMEM((CY, 512), F32),
            pltpu.VMEM((2, 2, FOLD, MODES), BF16),
            pltpu.VMEM((4, ND, MODES), F32),
            pltpu.VMEM((2, ND, TILE), F32),
            pltpu.VMEM((ND, ROWS, 128), F32),
            pltpu.VMEM((ND, ROWS, 128), F32),
            pltpu.VMEM((ND, ROWS, 128), F32),
            pltpu.VMEM((ND, ROWS, 128), F32),
            pltpu.SemaphoreType.DMA((len(EARLY) + len(LATE),)),
            pltpu.SemaphoreType.DMA((2,)),
            pltpu.SemaphoreType.DMA((5,)),
        ],
        compiler_params=pltpu.CompilerParams(
            collective_id=1, has_side_effects=True, vmem_limit_bytes=58 << 20
        ),
        name="main",
    )(
        column,
        ghosts,
        neighbours.reshape(ATOMS, ATOMS),
        e1w,
        e1b,
        e2w,
        row(e2b),
        e3w,
        row(e3b),
        row(f1b),
        row(f2b),
        row(f3b),
        f1w.T,
        f2w,
        f3w,
        fow.T,
        *late,
    )
    dipole, atom, centroid, energy = pl.pallas_call(
        deal_kernel,
        out_shape=(
            jax.ShapeDtypeStruct((3, 1, 1, 1, ATOMS), F32),
            jax.ShapeDtypeStruct((4, 1, 1, 1, ATOMS), F32),
            jax.ShapeDtypeStruct((4, 1, 1, 1, ATOMS), F32),
            jax.ShapeDtypeStruct((1, 1), F32),
        ),
        in_specs=[vmem],
        out_specs=(vmem,) * 4,
        name="deal",
    )(result)
    return dipole, atom, centroid, energy.reshape(())


def solution(mesh):
    return jax.shard_map(
        local,
        mesh=mesh,
        in_specs=(
            P(None, "wide", "narrow", None, None),
            P("wide", "narrow", None, None),
            P("wide", "narrow", None, None, None),
        )
        + (P(),) * 13,
        out_specs=(
            P(None, "wide", "narrow", None, None),
            P(None, "wide", "narrow", None, None),
            P(None, "wide", "narrow", None, None),
            P(),
        ),
        check_vma=False,
    )
```

```python
import functools
import math

import jax
import jax.numpy as jnp
import numpy as np
from jax import lax
from jax.experimental import pallas as pl
from jax.experimental.pallas import tpu as pltpu
from jax.sharding import PartitionSpec as P

NW, NN = 8, 16
ND = NW * NN
CX, CY, CZ = 32, 256, 16
TX, TZ = 32, 19
TILE = 640
FOLD = 512
ROWS = 10
SIDE = 8
UNROLL = 1
MODES = 512
ATOMS = 128
F32 = jnp.float32
BF16 = jnp.bfloat16
MESH = pl.DeviceIdType.MESH
HIGHEST = lax.Precision.HIGHEST
NT = (((1,), (1,)), ((), ()))
NNN = (((1,), (0,)), ((), ()))


def split(x):
    high = x.astype(BF16)
    return high, (x - high.astype(F32)).astype(BF16)


def mm(a, b, dims=NNN):
    return lax.dot_general(a, b, dims, preferred_element_type=F32)


def mm3(a, b, dims=NNN):
    return mm(a[0], b[0], dims) + mm(a[0], b[1], dims) + mm(a[1], b[0], dims)


def exact(a, b, dims=NNN):
    return lax.dot_general(a, b, dims, precision=HIGHEST, preferred_element_type=F32)


def iota(shape, dim):
    return lax.broadcasted_iota(jnp.int32, shape, dim)


def spline(offset):
    from_middle = offset - 2.0
    away = jnp.abs(from_middle)
    outer = jnp.maximum(2.0 - away, 0.0)
    inner = jnp.maximum(1.0 - away, 0.0)
    outer_square, inner_square = outer * outer, inner * inner
    value = (outer_square * outer - 4.0 * (inner_square * inner)) * (1.0 / 6.0)
    fall = 0.5 * outer_square - 2.0 * inner_square
    return value, jnp.where(from_middle > 0.0, -fall, fall)


def halo_kernel(positions_ref, species_ref, ghost_ref, own_ref, send_sem, recv_sem):
    wide = lax.axis_index("wide")
    narrow = lax.axis_index("narrow")
    steps = [(sx, sz) for sx in range(3) for sz in range(3) if (sx, sz) != (1, 1)]
    barrier = pltpu.get_barrier_semaphore()

    def device(sx, sz):
        return (lax.rem(wide + (NW + 1 - sx), NW), lax.rem(narrow + (NN + 1 - sz), NN))

    own_ref[...] = jnp.concatenate(
        [positions_ref[c, 0, 0] for c in range(3)]
        + [species_ref[0, 0].astype(F32), jnp.zeros((4, ATOMS), F32)],
        axis=0,
    )
    ghost_ref[4] = own_ref[...]
    for sx, sz in steps:
        pl.semaphore_signal(barrier, inc=1, device_id=device(sx, sz), device_id_type=MESH)
    pl.semaphore_wait(barrier, len(steps))
    copies = []
    for at, (sx, sz) in enumerate(steps):
        copy = pltpu.make_async_remote_copy(
            src_ref=own_ref,
            dst_ref=ghost_ref.at[sx * 3 + sz],
            send_sem=send_sem.at[at],
            recv_sem=recv_sem.at[at],
            device_id=device(sx, sz),
            device_id_type=MESH,
        )
        copy.start()
        copies.append(copy)
    for copy in copies:
        copy.wait()


def halo(positions, species):
    vmem = pl.BlockSpec(memory_space=pltpu.VMEM)
    return pl.pallas_call(
        halo_kernel,
        out_shape=jax.ShapeDtypeStruct((9, 8, ATOMS), F32),
        in_specs=[vmem, vmem],
        out_specs=vmem,
        scratch_shapes=[
            pltpu.VMEM((8, ATOMS), F32),
            pltpu.SemaphoreType.DMA((8,)),
            pltpu.SemaphoreType.DMA((8,)),
        ],
        compiler_params=pltpu.CompilerParams(collective_id=0, has_side_effects=True),
        name="halo",
    )(positions, species)


def spread_rows(rows, count):
    r = iota((rows, count), 0)
    c = iota((rows, count), 1)
    i = r & 31
    return jnp.where((i < 25) & (c == (r >> 5) * 25 + i), 1.0, 0.0).astype(F32)


def network(
    ghost_ref,
    near_ref,
    e1w_ref,
    e1b_ref,
    e2w_ref,
    e2b_ref,
    e3w_ref,
    e3b_ref,
    f1b_ref,
    f2b_ref,
    f3b_ref,
    f1w_ref,
    f2w_ref,
    f3w_ref,
    fow_ref,
    table_ref,
    own_ref,
    mat_ref,
    arrived,
):
    extent = (float(CX), float(CY), float(CZ))
    for k in range(9):
        shift = (float(k // 3 - 1), 0.0, float(k % 3 - 1))
        for c in range(3):
            table_ref[k * 4 + c] = jnp.broadcast_to(ghost_ref[k, c : c + 1, :] + shift[c], (8, ATOMS))
        table_ref[k * 4 + 3] = jnp.broadcast_to(ghost_ref[k, 3:4, :], (8, ATOMS))
    for c in range(3):
        own_ref[c] = jnp.broadcast_to(ghost_ref[4, c : c + 1, :], (ATOMS, ATOMS)).T

    pick1 = spread_rows(32, 25)
    pick2 = spread_rows(64, 50)
    pick3 = spread_rows(128, 100)

    def column(pick, row):
        return exact(pick, jnp.broadcast_to(row, (ATOMS, row.shape[1])), NT)

    w_oxygen = column(pick1, e1w_ref[0:1, :])
    w_hydrogen = column(pick1, e1w_ref[1:2, :])
    b_oxygen = column(pick1, e1b_ref[0:1, :])
    b_hydrogen = column(pick1, e1b_ref[1:2, :])
    bias2 = column(pick2, e2b_ref[...])
    bias3 = column(pick3, e3b_ref[...])
    w2 = exact(pick2, exact(pick1, e2w_ref[...]), NT)
    w3 = exact(pick3, exact(pick2, e3w_ref[...]), NT)
    last = iota((32, ATOMS), 0) == 31
    b_oxygen = jnp.where(last, 20.0, b_oxygen)
    b_hydrogen = jnp.where(last, 20.0, b_hydrogen)
    w2 = jnp.where(iota((64, 32), 1) == 31, bias2[:, :32], w2)
    w3 = jnp.where(iota((128, 64), 1) == 31, bias3[:, :64], w3)
    w2_high, w2_low = split(w2)
    w3_high, w3_low = split(w3)
    w2_all = jnp.concatenate([w2_high, w2_high, w2_low], axis=1)
    w3_all = jnp.concatenate([w3_high, w3_high, w3_low], axis=1)
    sublane = iota((8, ATOMS), 0)

    def geometry(g):
        rows = pl.ds(pl.multiple_of(g * 8, 8), 8)
        code = near_ref[rows, :]
        slot = code & 127
        offset = code >> 7
        brick = (offset * 11) >> 5
        step_y = (offset - 3 * brick - 1).astype(F32)
        parts = [jnp.zeros((8, ATOMS), F32)] * 4
        for k in range(9):
            here = brick == k
            for c in range(4):
                found = jnp.take_along_axis(table_ref[k * 4 + c], slot, axis=1)
                parts[c] = jnp.where(here, found, parts[c])
        parts[1] = parts[1] + step_y
        scaled = [(parts[c] - own_ref[c, rows, :]) * (extent[c] / 24.0) for c in range(3)]
        square = scaled[0] * scaled[0] + scaled[1] * scaled[1] + scaled[2] * scaled[2]
        smooth = 1.0 / (1.0 + square)
        scale = smooth * (1.0 / 128.0)
        return rows, smooth, parts[3], [scale] + [scale * scaled[c] for c in range(3)]

    def group(g, carry):
        sets = [geometry(g * SIDE + i) for i in range(SIDE)]
        pieces = []
        for _, smooth, kind, _ in sets:
            for b in range(8):
                s = jnp.broadcast_to(smooth[b : b + 1, :], (32, ATOMS))
                h = jnp.broadcast_to(kind[b : b + 1, :], (32, ATOMS)) > 0.5
                pieces.append(
                    jnp.where(h, w_hydrogen, w_oxygen) * s + jnp.where(h, b_hydrogen, b_oxygen)
                )
        one = jnp.tanh(jnp.concatenate(pieces, axis=1))
        high, low = split(one)
        two = jnp.tanh(mm(w2_all, jnp.concatenate([high, low, high], axis=0)))
        two = two + jnp.concatenate([one, one], axis=0)
        high, low = split(two)
        three = jnp.tanh(mm(w3_all, jnp.concatenate([high, low, high], axis=0)))
        three = three + jnp.concatenate([two, two], axis=0)
        high, low = split(three)
        for i, (rows, _, _, radial) in enumerate(sets):
            blocks = [
                jnp.concatenate([jnp.where(sublane == b, r, 0.0) for r in radial], axis=0)
                for b in range(8)
            ]
            r_high, r_low = split(jnp.concatenate(blocks, axis=1))
            mine = high[:, i * 1024 : (i + 1) * 1024]
            both = mm(jnp.concatenate([r_high, r_low], axis=0), mine, NT)
            found = (both[:32] + both[32:]) + mm(r_high, low[:, i * 1024 : (i + 1) * 1024], NT)
            for p in range(4):
                mat_ref[p, rows, :] = found[p * 8 : (p + 1) * 8]
        return carry

    lax.fori_loop(0, ATOMS // 8 // SIDE, group, 0, unroll=UNROLL)

    lane = iota((ATOMS, ATOMS), 1)
    entries = None
    matrix = [mat_ref[p] for p in range(4)]
    for p in range(4):
        tiled = jnp.take_along_axis(matrix[p], lane & 15, axis=1)
        term = []
        for t in range(13):
            d = jnp.minimum((lane >> 4) + 8 * t, 99)
            block = (d * 41) >> 10
            term.append(jnp.take_along_axis(matrix[p], d + 7 * block, axis=1) * tiled)
        term = jnp.concatenate(term, axis=1)
        entries = term if entries is None else entries + term
    arrived()
    hidden = mm3(split(entries[:, :1600]), split(f1w_ref[...]), NT)
    hidden = jnp.tanh(hidden + f1b_ref[...])
    hidden = hidden + jnp.tanh(mm3(split(hidden), split(f2w_ref[...])) + f2b_ref[...])
    hidden = hidden + jnp.tanh(mm3(split(hidden), split(f3w_ref[...])) + f3b_ref[...])
    coeffs = mm3(split(hidden), split(exact(pick3, fow_ref[...])), NT)
    result = jnp.zeros((ATOMS, ATOMS), F32)
    for c in range(3):
        total = jnp.sum(coeffs * matrix[1 + c], axis=1, keepdims=True)
        result = jnp.where(lane == c, total, result)
    return result.T[:8]


def np_split(x):
    x = np.asarray(x, np.float32)
    high = x.astype(jnp.bfloat16)
    low = (x - high.astype(np.float32)).astype(jnp.bfloat16)
    return np.stack([high, low])


@functools.lru_cache(None)
def tables():
    m = np.arange(128)[:, None]
    y = np.arange(CY)[None, :]
    angle = 2 * np.pi * (m * y % CY) / CY
    lower = -np.sin(angle)
    lower[0] = 1 - 2 * (y[0] % 2)
    dft_y = np_split(np.concatenate([np.cos(angle), lower]))
    j, k = np.divmod(np.arange(ND), NN)
    phi = 2 * np.pi * ((2 * j[:, None] * j[None] + k[:, None] * k[None]) % 16) / 16
    cos, sin = np.cos(phi), np.sin(phi)
    dft_b = np_split(np.block([[cos, sin], [-sin, cos]]))
    z, x = np.divmod(np.arange(TILE), TX)
    turn = 2 * np.pi * ((j[:, None] * (x - 1)[None] + k[:, None] * (z - 3)[None]) % 256) / 256
    twiddle = np.stack([np.cos(turn), np.sin(turn)]).astype(np.float32)
    v, u = np.divmod(np.arange(MODES), 32)
    ax = 2 * np.pi * ((np.arange(TX)[:, None] - 1) * u[None] % 32) / 32
    az = 2 * np.pi * ((np.arange(16)[:, None] - 3) * v[None] % 16) / 16
    fac_x = np.stack([np.cos(ax), np.sin(ax)]).astype(np.float32)
    fac_z = np.stack([np.cos(az), np.sin(az)]).astype(np.float32)

    def fold(i, n):
        return np.where(2 * i >= n, i - n, i) / n

    def modulus(i, n):
        return 36.0 / (4 + 2 * np.cos(2 * np.pi * i / n)) ** 2

    def decay(f):
        return np.exp(-np.pi**2 * f * f / 0.81)

    mx = j[:, None] + 8 * u[None]
    mz = k[:, None] + 16 * v[None]
    fx, fz = fold(mx, 256), fold(mz, 256)
    scale = 0.25 / (np.pi * 256.0**3)
    plane = scale * decay(fx) * decay(fz) * modulus(mx, 256) * modulus(mz, 256)
    green = np.stack([plane, fx * fx + fz * fz]).astype(np.float32)
    my = np.arange(129)
    fy = fold(my, 256)
    column = np.stack([decay(fy) * modulus(my, 256), fy * fy]).astype(np.float32)
    return dft_y, dft_b, twiddle, fac_x, fac_z, green, column


EARLY = (
    ((9, 8, ATOMS), F32),
    ((ATOMS, ATOMS), jnp.int32),
    ((2, 25), F32),
    ((2, 25), F32),
    ((25, 50), F32),
    ((1, 50), F32),
    ((50, 100), F32),
    ((1, 100), F32),
    ((1, 240), F32),
    ((1, 240), F32),
    ((1, 240), F32),
)
LATE = (
    ((240, 1600), F32),
    ((240, 240), F32),
    ((240, 240), F32),
    ((100, 240), F32),
    ((2, 256, CY), BF16),
    ((2, 256, 256), BF16),
    ((2, ND, TILE), F32),
    ((2, TX, MODES), F32),
    ((2, 16, MODES), F32),
    ((2, ND, MODES), F32),
)


def main_kernel(*refs):
    count = len(EARLY) + len(LATE)
    column_ref = refs[0]
    far = refs[1 : 1 + count]
    result_ref = refs[1 + count]
    near = refs[2 + count : 2 + 2 * count]
    (
        ghost_ref,
        near_ref,
        e1w_ref,
        e1b_ref,
        e2w_ref,
        e2b_ref,
        e3w_ref,
        e3b_ref,
        f1b_ref,
        f2b_ref,
        f3b_ref,
    ) = near[: len(EARLY)]
    (
        table_ref,
        home_ref,
        mat_ref,
        mix_ref,
        wave_ref,
        tab_ref,
        plane_ref,
        field_ref,
        out_one,
        in_one,
        out_two,
        in_two,
        late_sem,
        send_sem,
        recv_sem,
    ) = refs[2 + 2 * count :]
    f1w_ref, f2w_ref, f3w_ref, fow_ref = near[len(EARLY) : len(EARLY) + 4]
    dft_y_ref, dft_b_ref, twiddle_ref, fac_x_ref, fac_z_ref, green_ref = near[len(EARLY) + 4 :]
    fetch = [pltpu.make_async_copy(far[i], near[i], late_sem.at[i]) for i in range(count)]
    for copy in fetch:
        copy.start()
    wide = lax.axis_index("wide")
    narrow = lax.axis_index("narrow")
    me = wide * NN + narrow
    barrier = pltpu.get_barrier_semaphore()

    def everyone(act):
        def close(i, carry):
            act(0, i + 1)
            return carry

        def distant(i, carry):
            act(1 + i // NN, lax.rem(i, NN))
            return carry

        lax.fori_loop(0, NN - 1, close, 0, unroll=5)
        lax.fori_loop(0, (NW - 1) * NN, distant, 0, unroll=8)

    def device(step_w, step_n):
        return lax.rem(wide + step_w, NW), lax.rem(narrow + step_n, NN)

    def greet(step_w, step_n):
        pl.semaphore_signal(
            barrier, inc=1, device_id=device(step_w, step_n), device_id_type=MESH
        )

    everyone(greet)

    def arrived():
        for copy in fetch[len(EARLY) :]:
            copy.wait()

    for copy in fetch[: len(EARLY)]:
        copy.wait()
    dip = network(
        ghost_ref,
        near_ref,
        e1w_ref,
        e1b_ref,
        e2w_ref,
        e2b_ref,
        e3w_ref,
        e3b_ref,
        f1b_ref,
        f2b_ref,
        f3b_ref,
        f1w_ref,
        f2w_ref,
        f3w_ref,
        fow_ref,
        table_ref,
        home_ref,
        mat_ref,
        arrived,
    )

    kind = ghost_ref[4, 3:4, :]
    oxygen = 1.0 - kind
    result_ref[0:8, :] = dip * oxygen
    shift = 0.5 * jnp.tanh(dip)

    def sites(c, extent):
        atom = ghost_ref[4, c : c + 1, :] * float(extent)
        return jnp.concatenate([atom, atom + shift[c : c + 1, :]], axis=1)

    charge = jnp.concatenate([6.0 * oxygen + kind, -8.0 * oxygen], axis=1)
    off_x = sites(0, CX) - (iota((TX, 256), 0).astype(F32) - 1.0)
    off_z = sites(2, CZ) - (iota((24, 256), 0).astype(F32) - 3.0)
    off_y = sites(1, CY) - iota((CY, 256), 0).astype(F32)
    wx, sx = spline(off_x)
    wz, sz = spline(off_z)
    wy, sy = spline(off_y)
    dft_y = (dft_y_ref[0], dft_y_ref[1])
    wave = mm3(dft_y, split(wy))
    wave_ref[:, :256] = wave
    wave_ref[:, 256:] = sy
    rest = jnp.zeros((TILE - TX * TZ, 256), F32)

    def blend(at, left, right):
        full = jnp.concatenate([left[z : z + 1, :] * right for z in range(TZ)] + [rest], axis=0)
        high, low = split(full)
        mix_ref[0, :, at * 256 : (at + 1) * 256] = high
        mix_ref[1, :, at * 256 : (at + 1) * 256] = low
        return high, low

    spread = mm3(split(wave * charge), blend(0, wz, wx), NT)
    for part in range(2):
        for t in range(5):
            out_one[:, part * 5 + t, :] = spread[part * 128 : (part + 1) * 128, t * 128 : (t + 1) * 128]

    pl.semaphore_wait(barrier, ND - 1)

    def exchange(out_ref, in_ref, s, slot):
        def one(step_w, step_n):
            w, n = device(step_w, step_n)
            pltpu.make_async_remote_copy(
                src_ref=out_ref.at[w * NN + n],
                dst_ref=in_ref.at[me],
                send_sem=send_sem.at[s],
                recv_sem=recv_sem.at[slot(step_w)],
                device_id=(w, n),
                device_id_type=MESH,
            ).start()

        everyone(one)
        in_ref[me] = out_ref[me]

    def settle(out_ref, in_ref, s):
        whole = pltpu.make_async_remote_copy(
            src_ref=out_ref.at[pl.ds(0, ND - 1)],
            dst_ref=in_ref.at[pl.ds(0, ND - 1)],
            send_sem=send_sem.at[s],
            recv_sem=recv_sem.at[s],
            device_id=device(0, 1),
            device_id_type=MESH,
        )
        whole.wait_send()
        whole.wait_recv()

    exchange(out_one, in_one, 0, lambda step_w: 0)

    blend(1, wz, sx)
    blend(2, sz, wx)
    wave_ref[:, 256:] = mm3(dft_y, split(wave_ref[:, 256:]))

    def build(z, carry):
        cz = fac_z_ref[0, pl.ds(z, 1), :]
        zz = fac_z_ref[1, pl.ds(z, 1), :]
        cx, xx = fac_x_ref[0], fac_x_ref[1]
        rows = pl.ds(pl.multiple_of(z * TX, 8), TX)
        for at, value in enumerate((cx * cz - xx * zz, xx * cz + cx * zz)):
            high, low = split(value)
            tab_ref[at, 0, rows, :] = high
            tab_ref[at, 1, rows, :] = low
        return carry

    lax.fori_loop(0, 16, build, 0)

    def tile_tables():
        return [(tab_ref[at, 0], tab_ref[at, 1]) for at in range(2)]


    def influence(at, weight):
        total = green_ref[1] + column_ref[1, at]
        inverse = jnp.where(total == 0.0, 0.0, 1.0 / jnp.where(total == 0.0, 1.0, total))
        return green_ref[0] * (inverse * (column_ref[0, at] * weight))

    first = me == 0
    weight = jnp.where(first, 1.0, 2.0)
    plane_ref[2] = influence(me, weight)
    plane_ref[3] = influence(jnp.where(first, 128, me), weight)
    settle(out_one, in_one, 0)

    def gathered(in_ref):
        return jnp.concatenate(
            [
                jnp.concatenate([in_ref[:, part * 5 + t, :] for t in range(5)], axis=1)
                for part in range(2)
            ],
            axis=0,
        )

    tiles = gathered(in_one)
    bricks = mm3((dft_b_ref[0], dft_b_ref[1]), split(tiles))
    real, imag = bricks[:128], bricks[128:]
    cos_t, sin_t = twiddle_ref[0], twiddle_ref[1]
    turned = jnp.concatenate(
        [real * cos_t + imag * sin_t, imag * cos_t - real * sin_t], axis=0
    )
    turned = jnp.concatenate(
        [turned[:, :128] + turned[:, FOLD:], turned[:, 128:FOLD]], axis=1
    )
    turned = split(turned)
    cos_e, sin_e = tile_tables()
    by_cos = mm3(turned, cos_e)
    by_sin = mm3(turned, sin_e)
    plane_ref[0] = by_cos[:128] + by_sin[128:]
    plane_ref[1] = by_cos[128:] - by_sin[:128]

    def inverse(at):
        cos_e, sin_e = tile_tables()
        green = plane_ref[at]
        modes = split(jnp.concatenate([green * plane_ref[0], green * plane_ref[1]], axis=0))
        by_cos = mm3(modes, cos_e, NT)
        by_sin = mm3(modes, sin_e, NT)
        real = by_cos[:128] - by_sin[128:]
        imag = by_sin[:128] + by_cos[128:]
        real = jnp.concatenate([real, real[:, :128]], axis=1)
        imag = jnp.concatenate([imag, imag[:, :128]], axis=1)
        cos_t, sin_t = twiddle_ref[0], twiddle_ref[1]
        real, imag = real * cos_t - imag * sin_t, imag * cos_t + real * sin_t
        return split(jnp.concatenate([real, -imag], axis=0))

    @pl.when(me != 0)
    def _():
        both = mm3((dft_b_ref[0], dft_b_ref[1]), inverse(2))
        field_ref[0] = both[:128]
        field_ref[1] = -both[128:]

    @pl.when(me == 0)
    def _():
        field_ref[0] = mm3((dft_b_ref[0, :128], dft_b_ref[1, :128]), inverse(2))
        field_ref[1] = -mm3((dft_b_ref[0, 128:], dft_b_ref[1, 128:]), inverse(3))

    field_r, field_i = field_ref[0], field_ref[1]
    partial = jnp.sum(tiles[:128] * field_r + tiles[128:] * field_i, keepdims=True)
    partial = partial * (0.5 / (ND * ATOMS))
    lane = iota((ND, 128), 1)
    for t in range(5):
        piece = field_r[:, t * 128 : (t + 1) * 128]
        if t == 4:
            piece = jnp.where(lane == 127, partial, piece)
        out_two[:, t, :] = piece
        out_two[:, 5 + t, :] = field_i[:, t * 128 : (t + 1) * 128]

    exchange(out_two, in_two, 1, lambda step_w: 1 + step_w // 2)
    mix = (mix_ref[0], mix_ref[1])
    rows = [jnp.zeros((1, 256), F32)] * 4
    total = jnp.zeros((1, 1), F32)
    for c in range(4):
        size = 31 if c == 0 else 32
        pltpu.make_async_remote_copy(
            src_ref=out_two.at[pl.ds(0, size)],
            dst_ref=in_two.at[pl.ds(0, size)],
            send_sem=send_sem.at[1],
            recv_sem=recv_sem.at[1 + c],
            device_id=device(0, 1),
            device_id_type=MESH,
        ).wait_recv()
        spans = [lax.rem(wide + (NW - 2 * c - i), NW) * NN for i in range(2)]
        spans = [pl.ds(pl.multiple_of(at, NN), NN) for at in spans]
        lower = [pl.ds(pl.multiple_of(at.start + ND, NN), NN) for at in spans]
        planes = jnp.concatenate(
            [
                jnp.concatenate([in_two[at, part * 5 + t, :] for t in range(5)], axis=1)
                for part in range(2)
                for at in spans
            ],
            axis=0,
        )
        inner = mm3(split(planes), mix)
        wave = jnp.concatenate([wave_ref[at, :] for at in spans + lower], axis=0)
        wave, wave_slope = wave[:, :256], wave[:, 256:]
        parts = [
            wave * inner[:, :256],
            -wave * inner[:, 256:512],
            -wave_slope * inner[:, :256],
            -wave * inner[:, 512:],
        ]
        rows = [r + jnp.sum(p, axis=0, keepdims=True) for r, p in zip(rows, parts)]
        total = total + jnp.sum(planes[:32, TILE - 1 : TILE], axis=0, keepdims=True)
    pltpu.make_async_remote_copy(
        src_ref=out_two.at[pl.ds(0, ND - 1)],
        dst_ref=in_two.at[pl.ds(0, ND - 1)],
        send_sem=send_sem.at[1],
        recv_sem=recv_sem.at[1],
        device_id=device(0, 1),
        device_id_type=MESH,
    ).wait_send()
    atom = [r[:, :128] for r in rows]
    centroid = [r[:, 128:] * oxygen for r in rows]
    result_ref[8:24, :] = jnp.concatenate(
        atom + centroid + [jnp.broadcast_to(total, (8, ATOMS))], axis=0
    )


def deal_kernel(result_ref, dipole_ref, atom_ref, centroid_ref, energy_ref):
    for c in range(3):
        dipole_ref[c, 0, 0] = result_ref[c : c + 1, :]
    for c in range(4):
        atom_ref[c, 0, 0] = result_ref[8 + c : 9 + c, :]
        centroid_ref[c, 0, 0] = result_ref[12 + c : 13 + c, :]
    energy_ref[...] = result_ref[16:17, 0:1]


def local(
    positions,
    species,
    neighbours,
    e1w,
    e1b,
    e2w,
    e2b,
    e3w,
    e3b,
    f1w,
    f1b,
    f2w,
    f2b,
    f3w,
    f3b,
    fow,
):
    ghosts = halo(positions, species)
    *late, column = [jnp.asarray(t) for t in tables()]
    vmem = pl.BlockSpec(memory_space=pltpu.VMEM)
    anywhere = pl.BlockSpec(memory_space=pl.ANY)
    row = lambda x: x.reshape(1, -1)
    result = pl.pallas_call(
        main_kernel,
        out_shape=jax.ShapeDtypeStruct((24, ATOMS), F32),
        in_specs=[pl.BlockSpec(memory_space=pltpu.SMEM)] + [anywhere] * (len(EARLY) + len(LATE)),
        out_specs=vmem,
        scratch_shapes=[pltpu.VMEM(shape, dtype) for shape, dtype in EARLY + LATE]
        + [
            pltpu.VMEM((36, 8, ATOMS), F32),
            pltpu.VMEM((3, ATOMS, ATOMS), F32),
            pltpu.VMEM((4, ATOMS, ATOMS), F32),
            pltpu.VMEM((2, TILE, 768), BF16),
            pltpu.VMEM((CY, 512), F32),
            pltpu.VMEM((2, 2, FOLD, MODES), BF16),
            pltpu.VMEM((4, ND, MODES), F32),
            pltpu.VMEM((2, ND, TILE), F32),
            pltpu.VMEM((ND, ROWS, 128), F32),
            pltpu.VMEM((ND, ROWS, 128), F32),
            pltpu.VMEM((ND, ROWS, 128), F32),
            pltpu.VMEM((ND, ROWS, 128), F32),
            pltpu.SemaphoreType.DMA((len(EARLY) + len(LATE),)),
            pltpu.SemaphoreType.DMA((2,)),
            pltpu.SemaphoreType.DMA((5,)),
        ],
        compiler_params=pltpu.CompilerParams(
            collective_id=1, has_side_effects=True, vmem_limit_bytes=58 << 20
        ),
        name="main",
    )(
        column,
        ghosts,
        neighbours.reshape(ATOMS, ATOMS),
        e1w,
        e1b,
        e2w,
        row(e2b),
        e3w,
        row(e3b),
        row(f1b),
        row(f2b),
        row(f3b),
        f1w.T,
        f2w,
        f3w,
        fow.T,
        *late,
    )
    dipole, atom, centroid, energy = pl.pallas_call(
        deal_kernel,
        out_shape=(
            jax.ShapeDtypeStruct((3, 1, 1, 1, ATOMS), F32),
            jax.ShapeDtypeStruct((4, 1, 1, 1, ATOMS), F32),
            jax.ShapeDtypeStruct((4, 1, 1, 1, ATOMS), F32),
            jax.ShapeDtypeStruct((1, 1), F32),
        ),
        in_specs=[vmem],
        out_specs=(vmem,) * 4,
        name="deal",
    )(result)
    return dipole, atom, centroid, energy.reshape(())


def solution(mesh):
    return jax.shard_map(
        local,
        mesh=mesh,
        in_specs=(
            P(None, "wide", "narrow", None, None),
            P("wide", "narrow", None, None),
            P("wide", "narrow", None, None, None),
        )
        + (P(),) * 13,
        out_specs=(
            P(None, "wide", "narrow", None, None),
            P(None, "wide", "narrow", None, None),
            P(None, "wide", "narrow", None, None),
            P(),
        ),
        check_vma=False,
    )
```
